256 devices in a mesh: seq: 16 (over z, x_hi), mp: 16 (over y, x_lo, core).
Axes of the slice: x: 4 (x_hi: 2, x_lo: 2; x = x_hi * 2 + x_lo), y: 4, z: 8, core: 2. Of those that a mesh axis runs over, the one named last changes fastest.
Arguments:
- tokens: bfloat16 [8192, 4608], P('seq', 'mp')
- pre_gain: bfloat16 [4608], P('mp'), may hold values from -2.5 to 2.5
- post_gain: bfloat16 [4608], P('mp'), may hold values from -2.5 to 2.5
- w_query: bfloat16 [4608, 4096], P('seq', 'mp')
- w_key: bfloat16 [4608, 2048], P('seq', 'mp')
- w_value: bfloat16 [4608, 2048], P('seq', 'mp'), may hold values from -0.09375 to 0.09375
- w_out: bfloat16 [4096, 4608], P('mp', 'seq')
- segment_ids: int32 [8192], P('seq'), may hold values from 0 to 3, never falling along the last dimension, each value on 1 to 6553 neighbouring positions
- page_table: int32 [64], P('seq'), may hold values from 0 to 63, as said below
Outputs:
- layer_output: bfloat16 [8192, 4608], P('seq', 'mp')
- key_cache: bfloat16 [64, 128, 2048], P('seq', None, 'mp')
- value_cache: bfloat16 [64, 128, 2048], P('seq', None, 'mp')
The draws below stay inside these ranges and needn't reach their ends.
Inputs may be any that keep to these rules, and one draw needn't show every extreme that they name: segment_ids never fall along the stream, every tenant of 0 to 3 is present, each has at least 1 and at most 6553 tokens and one has exactly 6553. page_table is a permutation; the slot of page p lies in the same block of 4 slots as p, that is page_table[p] // 4 = p // 4.
All inputs are finite; a program needn't handle non-finite values.
Results may differ from the reference program's by a relative error of at most 0.019.
Values may be sent and summed in bfloat16 or wider, within the bound.
No kernel may reach another device: no remote copies, remote signals or barrier semaphores. Data moves between devices by JAX's collectives and lax.ppermute only.
A program may use at most 64 MiB of HBM per device.

```python
import math
import jax
import jax.numpy as jnp
import numpy as np
from jax import lax

D = 4608
HQ = 32
HK = 16
HD = 128
WINDOW = 4096
PAGE = 128
SEGS = 4
TOKENS = 8192
PAGES = 64
PAGES_DEV = 4
LONGEST = 6553
N_MP = 16


def draw_tokens(key, part):
    first, second, third = jax.random.split(key, 3)
    row_scale = jnp.exp(jax.random.uniform(first, (TOKENS, 1), jnp.float32, math.log(0.3), math.log(3.0)))
    col_scale = jnp.exp(jax.random.uniform(second, (1, D), jnp.float32, math.log(0.4), math.log(2.5)))
    base = jnp.clip(jax.random.normal(third, (TOKENS, D), jnp.float32), -4.0, 4.0)
    return (base * row_scale * col_scale).astype(jnp.bfloat16)


def head_projection(key, heads, largest):
    first, second = jax.random.split(key, 2)
    factors = jnp.exp(jax.random.uniform(first, (heads,), jnp.float32, 0.0, math.log(largest)))
    columns = jnp.repeat(factors, HD)[None, :]
    base = jnp.clip(jax.random.normal(second, (D, heads * HD), jnp.float32), -4.0, 4.0)
    return base * D ** (-0.5) * columns


def draw_w_query(key, part):
    return head_projection(jax.random.fold_in(key, 11), HQ, 6.0).astype(jnp.bfloat16)


def draw_w_key(key, part):
    return head_projection(jax.random.fold_in(key, 23), HK, 3.0).astype(jnp.bfloat16)


def draw_w_out(key, part):
    first, second = jax.random.split(key, 2)
    rows = HQ * HD
    ramp = jnp.arange(D, dtype=jnp.float32)[None, :] / D
    rough = jnp.exp(jax.random.uniform(first, (1, D), jnp.float32, -0.5, 0.5))
    base = jnp.clip(jax.random.normal(second, (rows, D), jnp.float32), -4.0, 4.0)
    slope = 0.6 + 1.4 * ramp
    return (base * rows ** (-0.5) * slope * rough).astype(jnp.bfloat16)


def draw_page_table(key, part):
    groups = PAGES // PAGES_DEV
    scores = jax.random.randint(key, (groups, PAGES_DEV), 0, 1 << 20) * PAGES_DEV + jnp.arange(PAGES_DEV, dtype=jnp.int32)[None, :]
    order = jnp.argsort(scores, axis=1, stable=True).astype(jnp.int32)
    table = order + (jnp.arange(groups, dtype=jnp.int32) * PAGES_DEV)[:, None]
    return table.reshape(PAGES).astype(jnp.int32)


def block_scale(own_key, dims, pieces, low, top_value):
    def one(dim, blocks):
        steps = jax.random.uniform(jax.random.fold_in(jax.random.fold_in(own_key, 6), dim), (blocks,), jnp.float32, low / len(pieces), top_value / len(pieces))
        return jnp.repeat(jnp.exp(steps), dims[dim] // blocks).reshape((-1,) + (1,) * (len(dims) - dim - 1))

    loudness = one(*pieces[0])
    for cut in pieces[1:]:
        loudness = loudness * one(*cut)
    return loudness


def length_profile(count, total, bound, skew):
    portions = [(1 << 20) // math.isqrt(standing ** skew) + 1 for standing in range(2, count + 1)]
    surplus, given = total - bound - (count - 1), [1] * (count - 1)
    while surplus > 0:
        candidates = [i for i in range(count - 1) if given[i] < bound]
        mass, remaining = sum([portions[i] for i in candidates]), surplus
        for i in candidates:
            more = min(bound - given[i], max(1, remaining * portions[i] // mass), surplus)
            given[i] = given[i] + more
            surplus = surplus - more
    return np.array([bound] + given)


def ragged_sizes(rng, amount, total, reach, skew):
    if amount == 2:
        one = jax.random.randint(rng, (), max(1, total - reach), min(reach, total - 1) + 1)
        return jnp.stack([one, total - one])
    lengths = jnp.asarray(length_profile(amount, total, reach, skew), jnp.int32)
    twos = (amount - 1) // 2
    source_of, sink = lengths[1:1 + 2 * twos:2], lengths[2:2 + 2 * twos:2]
    slack = jnp.minimum(source_of - 1, reach - sink)
    passed = jax.random.randint(jax.random.fold_in(rng, 1), (twos,), 0, 1 << 20) % (slack + 1)
    lengths = lengths.at[1:1 + 2 * twos:2].set(source_of - passed).at[2:2 + 2 * twos:2].set(sink + passed)
    return lengths[jax.random.permutation(jax.random.fold_in(rng, 2), amount)]


def centred(key, extent, deviation, most, cuts=(), held_as=jnp.bfloat16):
    values = deviation * jax.random.normal(key, extent, jnp.float32)
    if cuts:
        values = values * block_scale(key, extent, cuts, -0.22, 0.18)
    return jnp.clip(values, -most, most).astype(held_as)


def setup_inputs(seed: int = 0) -> dict:
    splits = jax.random.split(jax.random.key(seed), 10)
    return {
        "tokens": draw_tokens(jax.random.fold_in(splits[9], 71), 0),
        "pre_gain": centred(splits[1], (D,), 0.5, 2.5, ((0, 16),)),
        "post_gain": centred(splits[2], (D,), 0.5, 2.5, ((0, 16),)),
        "w_query": draw_w_query(jax.random.fold_in(splits[9], 71), 0),
        "w_key": draw_w_key(jax.random.fold_in(splits[9], 71), 0),
        "w_value": centred(splits[5], (D, HK * HD), D ** -0.5, 0.09375, ((0, 16), (1, 16))),
        "w_out": draw_w_out(jax.random.fold_in(splits[9], 71), 0),
        "segment_ids": jnp.searchsorted(jnp.cumsum(ragged_sizes(splits[7], SEGS, TOKENS, LONGEST, 2)), jnp.arange(TOKENS), side="right").astype(jnp.int32),
        "page_table": draw_page_table(jax.random.fold_in(splits[9], 71), 0),
    }


EPSILON = 1e-06
SOFT_CAP = 50.0
LARGE_INDEX = 1 << 30

def lifted(array):
    return lax.optimization_barrier(array).astype(jnp.float32)

def rotate(values, positions):
    half = values.shape[-1] // 2
    freqs = jnp.exp(-math.log(10000.0) * jnp.arange(half, dtype=jnp.float32) * (2.0 / values.shape[-1]))
    angles = positions.astype(jnp.float32)[:, None] * freqs[None, :]
    cosine = jnp.cos(angles)[:, None, :]
    sine = jnp.sin(angles)[:, None, :]
    first = values[..., :half]
    second = values[..., half:]
    return jnp.concatenate([first * cosine - second * sine, second * cosine + first * sine], axis=-1)

def reference(tokens, pre_gain, post_gain, w_query, w_key, w_value, w_out, segment_ids, page_table):
    total = tokens.shape[0]
    x_float = tokens.astype(jnp.float32)
    pre_scale = lax.rsqrt(lax.optimization_barrier(jnp.mean(x_float * x_float, axis=1, keepdims=True)) + EPSILON)
    normed = (x_float * pre_scale * (1.0 + pre_gain.astype(jnp.float32))[None, :]).astype(jnp.bfloat16)
    query_raw = jnp.dot(normed, w_query, preferred_element_type=jnp.float32).reshape(total, HQ, HD)
    key_raw = jnp.dot(normed, w_key, preferred_element_type=jnp.float32).reshape(total, HK, HD)
    value_raw = jnp.dot(normed, w_value, preferred_element_type=jnp.float32).reshape(total, HK, HD)
    position = jnp.arange(total, dtype=jnp.int32)
    starts = jnp.stack([jnp.min(jnp.where(segment_ids == s, position, LARGE_INDEX)) for s in range(SEGS)]).astype(jnp.int32)
    within = position - starts[segment_ids]
    query_scale = float(D // HQ) ** (-0.5)
    queries = (rotate(query_raw, within) * query_scale).astype(jnp.bfloat16)
    keys = rotate(key_raw, within).astype(jnp.bfloat16)
    values = value_raw.astype(jnp.bfloat16)
    block = math.gcd(total, 512)
    key_pad = jnp.concatenate([jnp.zeros((WINDOW, HK, HD), jnp.bfloat16), keys], axis=0)
    value_pad = jnp.concatenate([jnp.zeros((WINDOW, HK, HD), jnp.bfloat16), values], axis=0)
    segment_pad = jnp.concatenate([jnp.full((WINDOW,), -1, jnp.int32), segment_ids.astype(jnp.int32)], axis=0)

    def attend(start):
        query_block = lax.dynamic_slice_in_dim(queries, start, block, 0).reshape(block, HK, HQ // HK, HD)
        key_block = lax.dynamic_slice_in_dim(key_pad, start, WINDOW + block, 0)
        value_block = lax.dynamic_slice_in_dim(value_pad, start, WINDOW + block, 0)
        key_segment = lax.dynamic_slice_in_dim(segment_pad, start, WINDOW + block, 0)
        query_segment = lax.dynamic_slice_in_dim(segment_ids.astype(jnp.int32), start, block, 0)
        query_pos = start + jnp.arange(block, dtype=jnp.int32)
        key_pos = start - WINDOW + jnp.arange(WINDOW + block, dtype=jnp.int32)
        distance = query_pos[:, None] - key_pos[None, :]
        allowed = (key_pos >= 0)[None, :] & (distance >= 0) & (distance < WINDOW) & (query_segment[:, None] == key_segment[None, :])
        scores = jnp.einsum('qgrd,kgd->grqk', lifted(query_block), lifted(key_block))
        capped = SOFT_CAP * jnp.tanh(scores / SOFT_CAP)
        weights = jnp.where(allowed[None, None], jnp.exp(capped), 0.0)
        denominator = lax.optimization_barrier(jnp.sum(weights, axis=-1))
        rounded = weights.astype(jnp.bfloat16)
        summed = jnp.einsum('grqk,kgd->qgrd', lifted(rounded), lifted(value_block))
        result = summed / jnp.transpose(denominator, (2, 0, 1))[..., None]
        return result.astype(jnp.bfloat16).reshape(block, HQ * HD)
    block_starts = jnp.arange(total // block, dtype=jnp.int32) * block
    attended = lax.map(attend, block_starts).reshape(total, HQ * HD)
    group = HQ * HD // N_MP
    attention_sum = jnp.zeros((total, D), jnp.float32)
    for index in range(N_MP):
        term = jnp.dot(attended[:, index * group:(index + 1) * group], w_out[index * group:(index + 1) * group], preferred_element_type=jnp.float32).astype(jnp.bfloat16)
        attention_sum = attention_sum + lifted(term)
    post_scale = lax.rsqrt(lax.optimization_barrier(jnp.mean(attention_sum * attention_sum, axis=1, keepdims=True)) + EPSILON)
    post = attention_sum * post_scale * (1.0 + post_gain.astype(jnp.float32))[None, :]
    layer_output = (x_float + post).astype(jnp.bfloat16)
    key_pages = keys.reshape(PAGES, PAGE, HK * HD)
    value_pages = values.reshape(PAGES, PAGE, HK * HD)
    key_cache = jnp.zeros((PAGES, PAGE, HK * HD), jnp.bfloat16).at[page_table].set(key_pages)
    value_cache = jnp.zeros((PAGES, PAGE, HK * HD), jnp.bfloat16).at[page_table].set(value_pages)
    return (layer_output, key_cache, value_cache)
```

```python
import functools
import math

import jax
import jax.numpy as jnp
from jax import lax
from jax.experimental import pallas as pl
from jax.experimental.pallas import tpu as pltpu
from jax.sharding import PartitionSpec as P

D = 4608
HQ = 32
HD = 128
WINDOW = 4096
PAGE = 128
SEGS = 4

EPSILON = 1e-06
SOFT_CAP = 50.0
LOG2E = 1.4426950408889634
EXTRA = 16
SEQ = 16
ROUNDS = 8

BF = jnp.bfloat16
F32 = jnp.float32

AHEAD = [(i, (i + 2) % SEQ) for i in range(SEQ)]
BEHIND = [((i + 2) % SEQ, i) for i in range(SEQ)]
LATER = [(i, i + 2) for i in range(SEQ - 2)]
ACROSS = [(i, i ^ 1) for i in range(SEQ)]
TURN = [(s * SEQ + m, m * SEQ + s) for s in range(SEQ) for m in range(SEQ)]


def move(block, perm):
    return lax.ppermute(block, "seq", perm)


def pair(block):
    return jnp.concatenate([block, move(block, ACROSS)], axis=0)


def after(value, *others):
    return lax.optimization_barrier((value, *others))[0]


def ring(block, forward, backward, split):
    out = [(block, 0, 0)]
    ahead = back = block
    for step in range(1, max(forward, backward) + 1):
        if step <= forward:
            ahead = move(ahead, AHEAD)
            out.append((ahead, 0, step))
        if step <= backward:
            back = move(back, BEHIND)
            out.append((back, 0, -step))
    if split:
        half = block.shape[1] // 2
        out.append((move(ahead[:, :half], AHEAD), 0, forward + 1))
        out.append((move(back[:, half:], BEHIND), half, forward + 1))
    return out


def chunk_order(steps, z, h):
    order = []
    for step in steps:
        source = lax.rem(z - step + 2 * ROUNDS, ROUNDS)
        order += [2 * source + h, 2 * source + 1 - h]
    return jnp.stack(order).astype(jnp.int32)


def plan(blocks):
    steps = []
    slots = []
    for _, _, step in blocks:
        step = step % ROUNDS
        if step not in steps:
            steps.append(step)
        slots.append(steps.index(step))
    return steps, slots


def project_kernel(slots, offsets, rotated, factor, order_ref, x_hbm, cos_ref, sin_ref, *rest):
    n = len(slots)
    w_refs = rest[:n]
    out_ref, x_ref, acc_ref, sem = rest[n:]
    depth = x_hbm.shape[1]
    copies = []
    for c in range(2 * ROUNDS):
        copies.append(
            pltpu.make_async_copy(
                x_hbm.at[order_ref[c]],
                x_ref.at[c // 2, pl.ds((c % 2) * depth, depth)],
                sem.at[c],
            )
        )
    for copy in copies:
        copy.start()
    squares = jnp.zeros((1, x_hbm.shape[2]), F32)
    seen = set()
    started = set()
    for w_ref, slot, offset in zip(w_refs, slots, offsets):
        if slot not in seen:
            seen.add(slot)
            copies[2 * slot].wait()
            copies[2 * slot + 1].wait()
            for part in range(2):
                rows = x_ref[slot, pl.ds((part + 1) * depth - EXTRA, EXTRA), :]
                squares = squares + jnp.sum(rows.astype(F32), axis=0, keepdims=True)
        width = w_ref.shape[1]
        product = lax.dot_general(
            x_ref[slot],
            w_ref[...],
            (((0,), (0,)), ((), ())),
            preferred_element_type=F32,
        )
        columns = slice(offset, offset + width)
        if (offset in started) or (0 in started):
            acc_ref[:, columns] += product
        else:
            acc_ref[:, columns] = product
            started.add(offset)
    scale = lax.rsqrt(squares * (1.0 / D) + EPSILON)
    scale = jnp.transpose(jnp.broadcast_to(scale, (HD, scale.shape[1])))
    for head in range(2):
        columns = slice(head * HD, (head + 1) * HD)
        value = acc_ref[:, columns] * scale
        if rotated[head]:
            value = value * cos_ref[...] + pltpu.roll(value, HD // 2, 1) * sin_ref[...]
            if factor != 1.0:
                value = value * factor
        out_ref[:, columns] = value.astype(BF)


def project(x_all, blocks, z, h, cos, sin, rotated, factor):
    steps, slots = plan(blocks)
    order = chunk_order(steps, z, h)
    rows = x_all.shape[2]
    depth = x_all.shape[1]
    vmem = pl.BlockSpec(memory_space=pltpu.VMEM)
    return pl.pallas_call(
        functools.partial(
            project_kernel, tuple(slots), tuple(b[1] for b in blocks), rotated, factor
        ),
        out_shape=jax.ShapeDtypeStruct((rows, 2 * HD), BF),
        in_specs=[
            pl.BlockSpec(memory_space=pltpu.SMEM),
            pl.BlockSpec(memory_space=pl.ANY),
            vmem,
            vmem,
        ]
        + [vmem] * len(blocks),
        out_specs=vmem,
        scratch_shapes=[
            pltpu.VMEM((ROUNDS, 2 * depth, rows), BF),
            pltpu.VMEM((rows, 2 * HD), F32),
            pltpu.SemaphoreType.DMA((2 * ROUNDS,)),
        ],
        compiler_params=pltpu.CompilerParams(vmem_limit_bytes=32 << 20),
        cost_estimate=pl.CostEstimate(
            flops=2 * rows * 2 * HD * D, bytes_accessed=8 << 20, transcendentals=0
        ),
    )(order, x_all, cos, sin, *[b[0] for b in blocks])


def attend_kernel(distances, first, last, low_ref, q_ref, *rest):
    n = len(distances)
    kv_refs = rest[:n]
    rest = rest[n:]
    if not first:
        sum_in, den_in = rest[:2]
        rest = rest[2:]
    rows = q_ref.shape[0]
    tile = 256
    for r in range(rows // tile):
        here = slice(r * tile, (r + 1) * tile)
        for head in range(2):
            columns = slice(head * HD, (head + 1) * HD)
            q = q_ref[here, columns]
            if first:
                total = jnp.zeros((tile, HD), F32)
                den = jnp.zeros((tile, HD), F32)
            else:
                total = sum_in[here, columns]
                den = den_in[here, columns]
            for kv_ref, distance in zip(kv_refs, distances):
                keys = (r + 1) * tile if distance == 0 else rows
                score = lax.dot_general(
                    q,
                    kv_ref[:keys, :HD],
                    (((1,), (1,)), ((), ())),
                    preferred_element_type=F32,
                )
                weight = jnp.exp2(jnp.tanh(score * (1.0 / SOFT_CAP)) * (SOFT_CAP * LOG2E))
                place = lax.broadcasted_iota(jnp.int32, (tile, keys), 1)
                allowed = place >= low_ref[here, :] + distance * rows
                if distance == 0:
                    own = lax.broadcasted_iota(jnp.int32, (tile, keys), 0) + r * tile
                    allowed = allowed & (place <= own)
                weight = jnp.where(allowed, weight, 0.0)
                for c in range(keys // HD):
                    den = den + weight[:, c * HD : (c + 1) * HD]
                total = total + jnp.dot(
                    weight.astype(BF), kv_ref[:keys, HD:], preferred_element_type=F32
                )
            if last:
                out_ref = rest[0]
                whole = jnp.sum(den, axis=1, keepdims=True)
                out_ref[here, columns] = (total / whole).astype(BF)
            else:
                sum_out, den_out = rest
                sum_out[here, columns] = total
                den_out[here, columns] = den


def attend(low, queries, kvs, distances, state):
    first = state is None
    last = 8 in distances
    rows = queries.shape[0]
    vmem = pl.BlockSpec(memory_space=pltpu.VMEM)
    n_in = 2 + len(kvs) + (0 if first else 2)
    part = jax.ShapeDtypeStruct((rows, 2 * HD), F32)
    elements = 2 * rows * rows * len(kvs)
    return pl.pallas_call(
        functools.partial(attend_kernel, tuple(distances), first, last),
        out_shape=jax.ShapeDtypeStruct((rows, 2 * HD), BF) if last else (part, part),
        in_specs=[vmem] * n_in,
        out_specs=vmem if last else (vmem, vmem),
        input_output_aliases={} if (first or last) else {n_in - 2: 0, n_in - 1: 1},
        compiler_params=pltpu.CompilerParams(vmem_limit_bytes=32 << 20),
        cost_estimate=pl.CostEstimate(
            flops=elements * 512, bytes_accessed=4 << 20, transcendentals=2 * elements
        ),
    )(low, queries, *kvs, *(() if first else state))


def output_kernel(slots, offsets, order_ref, a_hbm, *rest):
    n = len(slots)
    w_refs = rest[:n]
    out_ref, square_ref, a_ref, sem = rest[n:]
    copies = []
    for c in range(2 * ROUNDS):
        copies.append(
            pltpu.make_async_copy(a_hbm.at[order_ref[c]], a_ref.at[c], sem.at[c])
        )
    for copy in copies:
        copy.start()
    features = out_ref.shape[0]
    seen = set()
    total = None
    for w_ref, slot, offset in zip(w_refs, slots, offsets):
        if slot not in seen:
            seen.add(slot)
            copies[2 * slot].wait()
            copies[2 * slot + 1].wait()
        width = w_ref.shape[1]
        for half in range(2):
            product = lax.dot_general(
                w_ref[half * features : (half + 1) * features, :],
                a_ref[2 * slot + half, :, offset : offset + width],
                (((1,), (1,)), ((), ())),
                preferred_element_type=F32,
            )
            total = product if total is None else total + product
    out_ref[...] = total
    square_ref[...] = jnp.sum(total * total, axis=0, keepdims=True)


def output(a_all, blocks, z, h):
    steps, slots = plan(blocks)
    order = chunk_order(steps, z, h)
    rows, width = a_all.shape[1:]
    features = blocks[0][0].shape[0] // 2
    vmem = pl.BlockSpec(memory_space=pltpu.VMEM)
    return pl.pallas_call(
        functools.partial(output_kernel, tuple(slots), tuple(b[1] for b in blocks)),
        out_shape=(
            jax.ShapeDtypeStruct((features, rows), F32),
            jax.ShapeDtypeStruct((1, rows), F32),
        ),
        in_specs=[pl.BlockSpec(memory_space=pltpu.SMEM), pl.BlockSpec(memory_space=pl.ANY)]
        + [vmem] * len(blocks),
        out_specs=(vmem, vmem),
        scratch_shapes=[
            pltpu.VMEM((2 * ROUNDS, rows, width), BF),
            pltpu.SemaphoreType.DMA((2 * ROUNDS,)),
        ],
        compiler_params=pltpu.CompilerParams(vmem_limit_bytes=32 << 20),
        cost_estimate=pl.CostEstimate(
            flops=2 * rows * features * 4096, bytes_accessed=8 << 20, transcendentals=0
        ),
    )(order, a_all, *[b[0] for b in blocks])


def shards(tokens, pre_gain, post_gain, w_query, w_key, w_value, w_out, segment_ids, page_table):
    rows = tokens.shape[0]
    features = tokens.shape[1]
    seq_index = lax.axis_index("seq")
    z = seq_index // 2
    h = lax.rem(seq_index, 2)
    base = seq_index * rows

    x_own = tokens.T.astype(F32)
    gained = (x_own * (1.0 + pre_gain.astype(F32))[:, None]).astype(BF)
    squares = jnp.sum(x_own * x_own, axis=0, keepdims=True)
    upper = lax.reduce_precision(squares, 8, 7)
    lower = squares - upper
    side = jnp.concatenate(
        [upper.astype(BF), lower.astype(BF), jnp.zeros((EXTRA - 2, rows), BF)], axis=0
    )
    x_all = lax.all_gather(jnp.concatenate([gained, side], axis=0), "mp", axis=0)

    counts = jnp.stack([jnp.sum((segment_ids < s).astype(jnp.int32)) for s in range(1, SEGS)])
    digits = jnp.concatenate([counts // 16, lax.rem(counts, 16)]).astype(BF)
    digits = jnp.pad(digits[None, :], ((2, EXTRA - 3), (0, 2 * HD - 2 * (SEGS - 1))))
    kv_own = jnp.concatenate([jnp.concatenate([w_key, w_value], axis=1), digits], axis=0)
    kv_blocks = ring(pair(kv_own), 3, 3, True)

    q_own = jnp.pad(w_query, ((0, EXTRA), (0, 0)))
    q_pair = after(pair(q_own), kv_blocks[5][0], kv_blocks[6][0])
    q_blocks = ring(q_pair, 2, 5, False)

    out_own = lax.ppermute(w_out.T, ("seq", "mp"), TURN)
    out_pair = pair(out_own)

    marks = jnp.zeros((2 * (SEGS - 1),), F32)
    n_marks = 2 * (SEGS - 1)
    for block, offset, _ in kv_blocks:
        if offset == 0:
            for part in range(2):
                marks = marks + block[part * (features + EXTRA) + features + 2, :n_marks].astype(F32)
    starts = (marks[: SEGS - 1] * 16.0 + marks[SEGS - 1 :]).astype(jnp.int32)
    global_index = base + jnp.arange(rows, dtype=jnp.int32)
    offsets = jnp.zeros((rows,), jnp.int32)
    for s in range(1, SEGS):
        offsets = jnp.where(segment_ids == s, starts[s - 1], offsets)
    within = (global_index - offsets).astype(F32)
    low = (jnp.maximum(offsets, global_index - (WINDOW - 1)) - base)[:, None]
    half = HD // 2
    freqs = jnp.exp(-math.log(10000.0) * jnp.arange(half, dtype=F32) * (2.0 / HD))
    angles = within[:, None] * freqs[None, :]
    cosine = jnp.cos(angles)
    sine = jnp.sin(angles)
    cos = jnp.concatenate([cosine, cosine], axis=1)
    sin = jnp.concatenate([-sine, sine], axis=1)

    kv = project(x_all, kv_blocks, z, h, cos, sin, (True, False), 1.0)

    straight = [kv]
    crossed = [None]
    current = kv
    for step in range(4):
        following = move(current, LATER)
        crossing = move(jnp.where(h == 0, current, following), ACROSS)
        straight.append(following)
        crossed.append(crossing)
        current = following

    queries = project(
        x_all, q_blocks, z, h, cos, sin, (True, True), float(D // HQ) ** (-0.5)
    )
    state = attend(low, queries, [kv], [0], None)
    for step in range(1, 5):
        state = attend(
            low,
            queries,
            [straight[step], crossed[step]],
            [2 * step, 2 * step - 1],
            state,
        )
    attended = state

    out_pair = after(out_pair, q_blocks[-1][0])
    out_blocks = ring(out_pair, 3, 3, True)

    a_all = lax.all_gather(attended, "mp", axis=0)
    share, partial = output(a_all, out_blocks, z, h)
    spread = jnp.broadcast_to(partial, (lax.axis_size("mp"), rows))
    square_total = jnp.sum(lax.all_to_all(spread, "mp", 0, 0, tiled=True), axis=0)
    post_scale = lax.rsqrt(square_total / D + EPSILON)
    post = share * post_scale[None, :] * (1.0 + post_gain.astype(F32))[:, None]
    layer_output = (tokens.T.astype(F32) + post).astype(BF).T

    pages = page_table.shape[0]
    local_slot = page_table - seq_index * pages
    kv_pages = kv.reshape(pages, PAGE, 2 * HD)
    placed = []
    for slot in range(pages):
        chosen = kv_pages[0]
        for page in range(1, pages):
            chosen = jnp.where(local_slot[page] == slot, kv_pages[page], chosen)
        placed.append(chosen)
    placed = jnp.stack(placed)
    return (layer_output, placed[:, :, :HD], placed[:, :, HD:])


def solution(mesh):
    return jax.shard_map(
        shards,
        mesh=mesh,
        in_specs=(
            P("seq", "mp"),
            P("mp"),
            P("mp"),
            P("seq", "mp"),
            P("seq", "mp"),
            P("seq", "mp"),
            P("mp", "seq"),
            P("seq"),
            P("seq"),
        ),
        out_specs=(P("seq", "mp"), P("seq", None, "mp"), P("seq", None, "mp")),
        check_vma=False,
    )
```

```python
import functools
import math

import jax
import jax.numpy as jnp
from jax import lax
from jax.experimental import pallas as pl
from jax.experimental.pallas import tpu as pltpu
from jax.sharding import PartitionSpec as P

D = 4608
HQ = 32
HD = 128
WINDOW = 4096
PAGE = 128
SEGS = 4

EPSILON = 1e-06
SOFT_CAP = 50.0
LOG2E = 1.4426950408889634
EXTRA = 16
SEQ = 16
ROUNDS = 8

BF = jnp.bfloat16
F32 = jnp.float32

AHEAD = [(i, (i + 2) % SEQ) for i in range(SEQ)]
BEHIND = [((i + 2) % SEQ, i) for i in range(SEQ)]
LATER = [(i, i + 2) for i in range(SEQ - 2)]
ACROSS = [(i, i ^ 1) for i in range(SEQ)]
TURN = [(s * SEQ + m, m * SEQ + s) for s in range(SEQ) for m in range(SEQ)]


SIDE = [(i, i ^ 2) for i in range(SEQ)]
UP = [(i, (i + 4) % SEQ) for i in range(SEQ)]
DOWN = [((i + 4) % SEQ, i) for i in range(SEQ)]
SWAP = [(i, i ^ 1) for i in range(SEQ)]
PLACES = (((0, 0), (0, 1)), ((-1, 0), (-1, 1)), ((1, 0), (1, 1)), ((2, 0),), ((2, 1),))


def move(block, perm):
    return lax.ppermute(block, "seq", perm)


def shift(block, perm):
    return lax.ppermute(block, "mp", perm)


def tie(*values):
    return lax.optimization_barrier(values)


def start_loads(index_ref, x_refs, w_refs, pieces, x_ref, w_ref, x_sem, w_sem):
    w_copies, x_copies = [], []
    for slot in range(ROUNDS):
        place = index_ref[2 + ROUNDS + slot]
        for part in range(2):
            parity = index_ref[1] if part == 0 else 1 - index_ref[1]
            which, start, length = pieces[slot][part]
            w_copies.append(
                pltpu.make_async_copy(
                    w_refs[which].at[pl.ds(start, length)],
                    w_ref.at[place, parity],
                    w_sem.at[2 * slot + part],
                )
            )
    same, other = x_refs[: len(PLACES)], x_refs[len(PLACES) :]
    for k, places in enumerate(PLACES):
        for j in range(len(places)):
            for ref in (same[k], other[k]):
                n = len(x_copies)
                x_copies.append(
                    pltpu.make_async_copy(ref.at[j], x_ref.at[n // 2, n % 2], x_sem.at[n])
                )
    for copy in w_copies + x_copies:
        copy.start()
    for copy in w_copies:
        copy.wait()
    return x_copies


def project_kernel(pieces, rotated, factor, index_ref, cos_ref, sin_ref, *rest):
    n = 2 * len(PLACES)
    x_refs, w_refs = rest[:n], rest[n:-6]
    out_ref, x_ref, w_ref, acc_ref, x_sem, w_sem = rest[-6:]
    copies = start_loads(index_ref, x_refs, w_refs, pieces, x_ref, w_ref, x_sem, w_sem)
    depth = x_ref.shape[2]
    length = w_ref.shape[2]
    squares = jnp.zeros((1, x_ref.shape[3]), F32)
    for slot in range(ROUNDS):
        total = None
        place = index_ref[2 + slot]
        for part in range(2):
            copies[2 * slot + part].wait()
            parity = index_ref[0] if part == 0 else 1 - index_ref[0]
            side = x_ref[slot, part, depth - EXTRA :, :]
            squares = squares + jnp.sum(side.astype(F32), axis=0, keepdims=True)
            product = lax.dot_general(
                w_ref[place, parity],
                x_ref[slot, part, :length, :],
                (((0,), (0,)), ((), ())),
                preferred_element_type=F32,
            )
            total = product if total is None else total + product
        if slot == 0:
            acc_ref[...] = total
        else:
            acc_ref[...] += total
    scale = lax.rsqrt(squares * (1.0 / D) + EPSILON)
    half = HD // 2
    for head in range(2):
        start = head * HD
        if rotated[head]:
            first = acc_ref[start : start + half, :] * scale
            second = acc_ref[start + half : start + HD, :] * scale
            cos, sin = cos_ref[...], sin_ref[...]
            value = jnp.concatenate(
                [first * cos - second * sin, second * cos + first * sin], axis=0
            )
            if factor != 1.0:
                value = value * factor
        else:
            value = acc_ref[start : start + HD, :] * scale
        out_ref[:, start : start + HD] = jnp.transpose(value).astype(BF)


def project(chunks, weights, pieces, index, cos, sin, rotated, factor):
    _, depth, rows = chunks[0].shape
    vmem = pl.BlockSpec(memory_space=pltpu.VMEM)
    outside = pl.BlockSpec(memory_space=pltpu.HBM)
    return pl.pallas_call(
        functools.partial(project_kernel, pieces, rotated, factor),
        out_shape=jax.ShapeDtypeStruct((rows, 2 * HD), BF),
        in_specs=[pl.BlockSpec(memory_space=pltpu.SMEM), vmem, vmem]
        + [outside] * (len(chunks) + len(weights)),
        out_specs=vmem,
        scratch_shapes=[
            pltpu.VMEM((ROUNDS, 2, depth, rows), BF),
            pltpu.VMEM((ROUNDS, 2, pieces[0][0][2], 2 * HD), BF),
            pltpu.VMEM((2 * HD, rows), F32),
            pltpu.SemaphoreType.DMA((2 * ROUNDS,)),
            pltpu.SemaphoreType.DMA((2 * ROUNDS,)),
        ],
        compiler_params=pltpu.CompilerParams(vmem_limit_bytes=60 << 20),
        cost_estimate=pl.CostEstimate(
            flops=2 * rows * 2 * HD * D, bytes_accessed=8 << 20, transcendentals=0
        ),
    )(index, cos, sin, *chunks, *weights)


def attend_kernel(distances, first, last, low_ref, q_ref, *rest):
    n = len(distances)
    kv_refs = rest[:n]
    rest = rest[n:]
    if not first:
        sum_in, den_in = rest[:2]
        rest = rest[2:]
    rows = q_ref.shape[0]
    tile = 256

    def part(index, carry):
        here = pl.ds(pl.multiple_of((index // 2) * tile, tile), tile)
        columns = pl.ds(pl.multiple_of(lax.rem(index, 2) * HD, HD), HD)
        q = q_ref[here, columns]
        low = low_ref[here, :]
        if first:
            total = jnp.zeros((tile, HD), F32)
            den = jnp.zeros((tile, HD), F32)
        else:
            total = sum_in[here, columns]
            den = den_in[here, columns]
        for kv_ref, distance in zip(kv_refs, distances):
            score = lax.dot_general(
                q, kv_ref[:, :HD], (((1,), (1,)), ((), ())), preferred_element_type=F32
            )
            weight = jnp.exp2(jnp.tanh(score * (1.0 / SOFT_CAP)) * (SOFT_CAP * LOG2E))
            place = lax.broadcasted_iota(jnp.int32, (tile, rows), 1)
            allowed = place >= low + distance * rows
            if distance == 0:
                own = lax.broadcasted_iota(jnp.int32, (tile, rows), 0) + (index // 2) * tile
                allowed = allowed & (place <= own)
            weight = jnp.where(allowed, weight, 0.0)
            for c in range(rows // HD):
                den = den + weight[:, c * HD : (c + 1) * HD]
            total = total + jnp.dot(
                weight.astype(BF), kv_ref[:, HD:], preferred_element_type=F32
            )
        if last:
            whole = jnp.sum(den, axis=1, keepdims=True)
            rest[0][here, columns] = (total / whole).astype(BF)
        else:
            rest[0][here, columns] = total
            rest[1][here, columns] = den
        return carry

    lax.fori_loop(0, 2 * (rows // tile), part, 0)


def attend(low, queries, kvs, distances, state):
    first = state is None
    last = 8 in distances
    rows = queries.shape[0]
    vmem = pl.BlockSpec(memory_space=pltpu.VMEM)
    n_in = 2 + len(kvs) + (0 if first else 2)
    part = jax.ShapeDtypeStruct((rows, 2 * HD), F32)
    elements = 2 * rows * rows * len(kvs)
    return pl.pallas_call(
        functools.partial(attend_kernel, tuple(distances), first, last),
        out_shape=jax.ShapeDtypeStruct((rows, 2 * HD), BF) if last else (part, part),
        in_specs=[vmem] * n_in,
        out_specs=vmem if last else (vmem, vmem),
        input_output_aliases={} if (first or last) else {n_in - 2: 0, n_in - 1: 1},
        compiler_params=pltpu.CompilerParams(vmem_limit_bytes=8 << 20),
        cost_estimate=pl.CostEstimate(
            flops=elements * 512, bytes_accessed=4 << 20, transcendentals=2 * elements
        ),
    )(low, queries, *kvs, *(() if first else state))


def output_kernel(pieces, index_ref, *rest):
    n = 2 * len(PLACES)
    x_refs, w_refs = rest[:n], rest[n:-6]
    out_ref, square_ref, x_ref, w_ref, x_sem, w_sem = rest[-6:]
    copies = start_loads(index_ref, x_refs, w_refs, pieces, x_ref, w_ref, x_sem, w_sem)
    for slot in range(ROUNDS):
        total = None
        place = index_ref[2 + slot]
        for part in range(2):
            copies[2 * slot + part].wait()
            parity = index_ref[0] if part == 0 else 1 - index_ref[0]
            product = lax.dot_general(
                w_ref[place, parity],
                x_ref[slot, part],
                (((1,), (1,)), ((), ())),
                preferred_element_type=F32,
            )
            total = product if total is None else total + product
        if slot == 0:
            out_ref[...] = total
        elif slot < ROUNDS - 1:
            out_ref[...] += total
        else:
            total = out_ref[...] + total
            out_ref[...] = total
            square_ref[...] = jnp.sum(total * total, axis=0, keepdims=True)


def output(chunks, weights, index):
    _, rows, width = chunks[0].shape
    features = weights[0].shape[0] // 2
    vmem = pl.BlockSpec(memory_space=pltpu.VMEM)
    outside = pl.BlockSpec(memory_space=pltpu.HBM)
    pieces = tuple(((k, 0, features), (k, features, features)) for k in range(ROUNDS))
    return pl.pallas_call(
        functools.partial(output_kernel, pieces),
        out_shape=(
            jax.ShapeDtypeStruct((features, rows), F32),
            jax.ShapeDtypeStruct((1, rows), F32),
        ),
        in_specs=[pl.BlockSpec(memory_space=pltpu.SMEM)]
        + [outside] * (len(chunks) + len(weights)),
        out_specs=(vmem, vmem),
        scratch_shapes=[
            pltpu.VMEM((ROUNDS, 2, rows, width), BF),
            pltpu.VMEM((ROUNDS, 2, features, width), BF),
            pltpu.SemaphoreType.DMA((2 * ROUNDS,)),
            pltpu.SemaphoreType.DMA((2 * ROUNDS,)),
        ],
        compiler_params=pltpu.CompilerParams(vmem_limit_bytes=60 << 20),
        cost_estimate=pl.CostEstimate(
            flops=2 * rows * features * 4096, bytes_accessed=8 << 20, transcendentals=0
        ),
    )(index, *chunks, *weights)


def shards(tokens, pre_gain, post_gain, w_query, w_key, w_value, w_out, segment_ids, page_table):
    rows = tokens.shape[0]
    features = tokens.shape[1]
    seq_index = lax.axis_index("seq")
    z = seq_index // 2
    h = lax.rem(seq_index, 2)
    base = seq_index * rows

    x_own = tokens.T.astype(F32)
    gained = (x_own * (1.0 + pre_gain.astype(F32))[:, None]).astype(BF)
    squares = jnp.sum(x_own * x_own, axis=0, keepdims=True)
    upper = lax.reduce_precision(squares, 8, 7)
    lower = squares - upper
    side = jnp.concatenate(
        [upper.astype(BF), lower.astype(BF), jnp.zeros((EXTRA - 2, rows), BF)], axis=0
    )
    x_block = jnp.concatenate([gained, side], axis=0)[None]
    depth = features + EXTRA

    counts = jnp.stack([jnp.sum((segment_ids < s).astype(jnp.int32)) for s in range(1, SEGS)])
    digits = jnp.concatenate([counts // 16, lax.rem(counts, 16)]).astype(BF)
    digits = jnp.pad(digits[None, :], ((2, EXTRA - 3), (0, 2 * HD - 2 * (SEGS - 1))))
    own = jnp.concatenate(
        [jnp.concatenate([w_key, w_value], axis=1), digits, w_query], axis=0
    )
    facing = move(own, ACROSS)
    x_facing = shift(x_block, SIDE)
    q_from = 2 * depth
    start = jnp.concatenate([own[:depth], facing[:depth], w_query], axis=0)

    x_pair = jnp.concatenate([x_block, x_facing], axis=0)
    ring = {0: start, 1: move(start, AHEAD), -1: move(start, BEHIND)}
    x_up, x_down = shift(x_pair, UP), shift(x_pair, DOWN)
    x_swaps = [shift(x_pair, SWAP)]
    cross_near = move(jnp.concatenate([ring[1][q_from:], ring[-1][q_from:]], axis=0), ACROSS)
    ring[2] = move(ring[1], AHEAD)
    ring[-2] = move(ring[-1], BEHIND)
    ring[2], ring[-2], x_up, x_down, x_swaps[0] = tie(ring[2], ring[-2], x_up, x_down, x_swaps[0])
    x_swaps += [shift(x_up, SWAP), shift(x_down, SWAP)]
    x_far = [shift(x_up[:1], UP), shift(x_down[1:], DOWN)]
    cross_next = move(jnp.concatenate([ring[2][q_from:], ring[-2][q_from:]], axis=0), ACROSS)
    ring[3] = move(ring[2], AHEAD)
    ring[-3] = move(ring[-2], BEHIND)
    turned, _ = tie(w_out.T, ring[2])
    turned = lax.ppermute(turned, ("seq", "mp"), TURN)
    ring[3], ring[-3], cross_near, x_far[0], x_far[1], x_swaps[1], x_swaps[2] = tie(
        ring[3], ring[-3], cross_near, x_far[0], x_far[1], x_swaps[1], x_swaps[2]
    )
    x_swaps += [shift(x_far[0], SWAP), shift(x_far[1], SWAP)]
    ring[4] = move(ring[3][:q_from], AHEAD)
    ring[-4] = move(ring[-3][q_from:], BEHIND)
    x_chunks = [x_pair, x_up, x_down, *x_far, *x_swaps]

    mp_index = lax.axis_index("mp")
    y = mp_index // 4
    over = lax.rem(mp_index // 2, 2)
    placed = [
        2 * lax.rem(y + dy + 4, 4) + jnp.where(dx == 0, over, 1 - over)
        for places in PLACES
        for dy, dx in places
    ]

    def index_of(steps):
        places = [lax.rem(z - step + ROUNDS, ROUNDS) for step in steps]
        return jnp.stack([lax.rem(mp_index, 2), h, *placed, *places]).astype(jnp.int32)

    steps = [0, 1, -1, 2, -2, 3, -3, 4]
    index = index_of(steps)
    kv_weights = [ring[step] for step in steps]
    kv_pieces = tuple(((k, 0, depth), (k, depth, depth)) for k in range(ROUNDS))

    n_marks = 2 * (SEGS - 1)
    marks = jnp.zeros((n_marks,), F32)
    for block in kv_weights:
        for part in range(2):
            marks = marks + block[part * depth + features + 2, :n_marks].astype(F32)
    starts = (marks[: SEGS - 1] * 16.0 + marks[SEGS - 1 :]).astype(jnp.int32)
    global_index = base + jnp.arange(rows, dtype=jnp.int32)
    offsets = jnp.zeros((rows,), jnp.int32)
    for s in range(1, SEGS):
        offsets = jnp.where(segment_ids == s, starts[s - 1], offsets)
    within = (global_index - offsets).astype(F32)
    low = (jnp.maximum(offsets, global_index - (WINDOW - 1)) - base)[:, None]
    half = HD // 2
    freqs = jnp.exp(-math.log(10000.0) * jnp.arange(half, dtype=F32) * (2.0 / HD))
    angles = freqs[:, None] * within[None, :]
    cos = jnp.cos(angles)
    sin = jnp.sin(angles)

    kv = project(x_chunks, kv_weights, kv_pieces, index, cos, sin, (True, False), 1.0)

    q_last = jnp.concatenate([ring[3][q_from:], ring[-3][q_from:], ring[-4]], axis=0)
    cross_last = move(q_last, ACROSS)
    q_weights = kv_weights[:7] + [ring[-4], facing, cross_near, cross_next, cross_last]
    crossings = [(8, depth)] + [
        (9 + k // 2, (k % 2) * features) for k in range(6)
    ] + [(11, 2 * features)]
    q_pieces = tuple(
        (
            (k, q_from if k < 7 else 0, features),
            (*crossings[k], features),
        )
        for k in range(ROUNDS)
    )

    out_pair = jnp.concatenate([turned, move(turned, ACROSS)], axis=0)
    out_blocks = {0: out_pair}

    straight, crossed, current, crossing = [kv], [None], kv, None
    state = None
    for step in range(4):
        following = move(current, LATER)
        chosen = jnp.where(h == 0, current, following)
        extra = [] if crossing is None else [crossing]
        if step == 1:
            extra += [out_pair, cross_last]
        if step == 2:
            out_blocks[-1] = move(out_pair, BEHIND)
            extra += [out_blocks[-1], *state]
        if step == 3:
            out_blocks[-2] = move(out_blocks[-1], BEHIND)
            extra += [out_blocks[-2], *state]
        following, chosen, *extra = tie(following, chosen, *extra)
        if crossing is not None:
            crossed[-1] = extra[0]
        if step == 1:
            out_pair, cross_last = extra[1:]
            out_blocks[0] = out_pair
            q_weights[-1] = cross_last
            queries = project(
                x_chunks,
                q_weights,
                q_pieces,
                index,
                cos,
                sin,
                (True, True),
                float(D // HQ) ** (-0.5),
            )
            state = attend(low, queries, [kv], [0], None)
        if step > 1:
            out_blocks[1 - step], *state = extra[1:]
            k = step - 1
            state = attend(low, queries, [straight[k], crossed[k]], [2 * k, 2 * k - 1], state)
        crossing = move(chosen, ACROSS)
        straight.append(following)
        crossed.append(crossing)
        current = following
    for k in range(3, 5):
        state = attend(low, queries, [straight[k], crossed[k]], [2 * k, 2 * k - 1], state)

    a_block = state[None]
    a_pair = jnp.concatenate([a_block, shift(a_block, SIDE)], axis=0)
    a_up, a_down = shift(a_pair, UP), shift(a_pair, DOWN)
    a_swaps = [shift(a_pair, SWAP)]
    out_blocks[1] = move(out_blocks[0], AHEAD)
    out_blocks[-3] = move(out_blocks[-2], BEHIND)
    a_up, a_down, out_blocks[1], out_blocks[-3] = tie(a_up, a_down, out_blocks[1], out_blocks[-3])
    a_swaps += [shift(a_up, SWAP), shift(a_down, SWAP)]
    a_far = [shift(a_up[:1], UP), shift(a_down[1:], DOWN)]
    out_blocks[2] = move(out_blocks[1], AHEAD)
    out_blocks[-4] = move(out_blocks[-3], BEHIND)
    out_blocks[3] = move(out_blocks[2], AHEAD)
    a_far[0], a_far[1], out_blocks[2], out_blocks[-4] = tie(
        a_far[0], a_far[1], out_blocks[2], out_blocks[-4]
    )
    a_swaps += [shift(a_far[0], SWAP), shift(a_far[1], SWAP)]

    q_steps = steps[:7] + [-4]
    share, partial = output(
        [a_pair, a_up, a_down, *a_far, *a_swaps],
        [out_blocks[step] for step in q_steps],
        index,
    )
    everywhere = jnp.broadcast_to(partial, (lax.axis_size("mp"), rows))
    square_total = jnp.sum(lax.all_to_all(everywhere, "mp", 0, 0, tiled=True), axis=0)
    post_scale = lax.rsqrt(square_total / D + EPSILON)
    post = share * post_scale[None, :] * (1.0 + post_gain.astype(F32))[:, None]
    layer_output = (tokens.T.astype(F32) + post).astype(BF).T

    pages = page_table.shape[0]
    local_slot = page_table - seq_index * pages
    kv_pages = kv.reshape(pages, PAGE, 2 * HD)
    caches = []
    for slot in range(pages):
        chosen = kv_pages[0]
        for page in range(1, pages):
            chosen = jnp.where(local_slot[page] == slot, kv_pages[page], chosen)
        caches.append(chosen)
    caches = jnp.stack(caches)
    return (layer_output, caches[:, :, :HD], caches[:, :, HD:])


def solution(mesh):
    return jax.shard_map(
        shards,
        mesh=mesh,
        in_specs=(
            P("seq", "mp"),
            P("mp"),
            P("mp"),
            P("seq", "mp"),
            P("seq", "mp"),
            P("seq", "mp"),
            P("mp", "seq"),
            P("seq"),
            P("seq"),
        ),
        out_specs=(P("seq", "mp"), P("seq", None, "mp"), P("seq", None, "mp")),
        check_vma=False,
    )
```

```python
import functools
import math

import jax
import jax.numpy as jnp
from jax import lax
from jax.experimental import pallas as pl
from jax.experimental.pallas import tpu as pltpu
from jax.sharding import PartitionSpec as P

D = 4608
HQ = 32
HD = 128
WINDOW = 4096
PAGE = 128
SEGS = 4

EPSILON = 1e-06
SOFT_CAP = 50.0
LOG2E = 1.4426950408889634
EXTRA = 16
SEQ = 16
ROUNDS = 8

BF = jnp.bfloat16
F32 = jnp.float32

AHEAD = [(i, (i + 2) % SEQ) for i in range(SEQ)]
BEHIND = [((i + 2) % SEQ, i) for i in range(SEQ)]
LATER = [(i, i + 2) for i in range(SEQ - 2)]
ACROSS = [(i, i ^ 1) for i in range(SEQ)]
TURN = [(s * SEQ + m, m * SEQ + s) for s in range(SEQ) for m in range(SEQ)]


SIDE = [(i, i ^ 2) for i in range(SEQ)]
UP = [(i, (i + 4) % SEQ) for i in range(SEQ)]
DOWN = [((i + 4) % SEQ, i) for i in range(SEQ)]
SWAP = [(i, i ^ 1) for i in range(SEQ)]
COLUMNS = [[2 * i + c for i in range(ROUNDS)] for c in range(2)]
PLACES = (((0, 0), (0, 1)), ((-1, 0), (-1, 1)), ((1, 0), (1, 1)), ((2, 0),), ((2, 1),))


def move(block, perm):
    return lax.ppermute(block, "seq", perm)


def shift(block, perm):
    return lax.ppermute(block, "mp", perm)


def tie(*values):
    return lax.optimization_barrier(values)


def project_kernel(pieces, rotated, factor, index_ref, cos_ref, sin_ref, x_hbm, *rest):
    w_refs = rest[:-6]
    out_ref, x_ref, w_ref, acc_ref, x_sem, w_sem = rest[-6:]
    chunks, depth, rows = x_ref.shape
    copies = []
    for slot in range(ROUNDS):
        place = index_ref[2 + ROUNDS + slot]
        for part in range(2):
            parity = index_ref[1] if part == 0 else 1 - index_ref[1]
            which, lead = pieces[slot]
            source = w_refs[which] if lead is None else w_refs[which].at[lead]
            copies.append(
                pltpu.make_async_copy(
                    source.at[pl.ds(part * depth, depth)],
                    w_ref.at[2 * place + parity],
                    w_sem.at[2 * slot + part],
                )
            )
    step = chunks // 4
    for k in range(4):
        copies.append(
            pltpu.make_async_copy(
                x_hbm.at[pl.ds(k * step, step)], x_ref.at[pl.ds(k * step, step)], x_sem.at[k]
            )
        )
    for copy in copies:
        copy.start()
    for copy in copies[:-4]:
        copy.wait()
    squares = jnp.zeros((1, rows), F32)
    for k in range(4):
        copies[k - 4].wait()
        here = slice(k * step, (k + 1) * step)
        side = x_ref[here, depth - EXTRA :, :].astype(F32)
        squares = squares + jnp.sum(jnp.sum(side, axis=0), axis=0, keepdims=True)
        product = lax.dot_general(
            w_ref[here].reshape(step * depth, 2 * HD),
            x_ref[here].reshape(step * depth, rows),
            (((0,), (0,)), ((), ())),
            preferred_element_type=F32,
        )
        if k == 0:
            acc_ref[...] = product
        else:
            acc_ref[...] += product
    scale = lax.rsqrt(squares * (1.0 / D) + EPSILON)
    half = HD // 2
    for head in range(2):
        start = head * HD
        if rotated[head]:
            first = acc_ref[start : start + half, :] * scale
            second = acc_ref[start + half : start + HD, :] * scale
            cos, sin = cos_ref[...], sin_ref[...]
            value = jnp.concatenate(
                [first * cos - second * sin, second * cos + first * sin], axis=0
            )
            if factor != 1.0:
                value = value * factor
        else:
            value = acc_ref[start : start + HD, :] * scale
        out_ref[:, start : start + HD] = jnp.transpose(value).astype(BF)


def project(x_all, weights, pieces, index, cos, sin, rotated, factor):
    chunks, depth, rows = x_all.shape
    vmem = pl.BlockSpec(memory_space=pltpu.VMEM)
    outside = pl.BlockSpec(memory_space=pl.ANY)
    return pl.pallas_call(
        functools.partial(project_kernel, pieces, rotated, factor),
        out_shape=jax.ShapeDtypeStruct((rows, 2 * HD), BF),
        in_specs=[pl.BlockSpec(memory_space=pltpu.SMEM), vmem, vmem]
        + [outside] * (1 + len(weights)),
        out_specs=vmem,
        scratch_shapes=[
            pltpu.VMEM((chunks, depth, rows), BF),
            pltpu.VMEM((chunks, depth, 2 * HD), BF),
            pltpu.VMEM((2 * HD, rows), F32),
            pltpu.SemaphoreType.DMA((4,)),
            pltpu.SemaphoreType.DMA((2 * ROUNDS,)),
        ],
        compiler_params=pltpu.CompilerParams(vmem_limit_bytes=60 << 20),
        cost_estimate=pl.CostEstimate(
            flops=2 * rows * 2 * HD * D, bytes_accessed=8 << 20, transcendentals=0
        ),
    )(index, cos, sin, x_all, *weights)


def attend_kernel(distances, first, last, low_ref, q_ref, *rest):
    n = len(distances)
    kv_refs = rest[:n]
    rest = rest[n:]
    if not first:
        sum_in, den_in = rest[:2]
        rest = rest[2:]
    rows = q_ref.shape[0]
    tile = 256

    def part(index, carry):
        here = pl.ds(pl.multiple_of((index // 2) * tile, tile), tile)
        columns = pl.ds(pl.multiple_of(lax.rem(index, 2) * HD, HD), HD)
        q = q_ref[here, columns]
        low = low_ref[here, :]
        if first:
            total = jnp.zeros((tile, HD), F32)
            den = jnp.zeros((tile, HD), F32)
        else:
            total = sum_in[here, columns]
            den = den_in[here, columns]
        for kv_ref, distance in zip(kv_refs, distances):
            score = lax.dot_general(
                q, kv_ref[:, :HD], (((1,), (1,)), ((), ())), preferred_element_type=F32
            )
            weight = jnp.exp2(jnp.tanh(score * (1.0 / SOFT_CAP)) * (SOFT_CAP * LOG2E))
            place = lax.broadcasted_iota(jnp.int32, (tile, rows), 1)
            allowed = place >= low + distance * rows
            if distance == 0:
                own = lax.broadcasted_iota(jnp.int32, (tile, rows), 0) + (index // 2) * tile
                allowed = allowed & (place <= own)
            weight = jnp.where(allowed, weight, 0.0)
            for c in range(rows // HD):
                den = den + weight[:, c * HD : (c + 1) * HD]
            total = total + jnp.dot(
                weight.astype(BF), kv_ref[:, HD:], preferred_element_type=F32
            )
        if last:
            whole = jnp.sum(den, axis=1, keepdims=True)
            rest[0][here, columns] = (total / whole).astype(BF)
        else:
            rest[0][here, columns] = total
            rest[1][here, columns] = den
        return carry

    lax.fori_loop(0, 2 * (rows // tile), part, 0)


def attend(low, queries, kvs, distances, state):
    first = state is None
    last = 8 in distances
    rows = queries.shape[0]
    vmem = pl.BlockSpec(memory_space=pltpu.VMEM)
    n_in = 2 + len(kvs) + (0 if first else 2)
    part = jax.ShapeDtypeStruct((rows, 2 * HD), F32)
    elements = 2 * rows * rows * len(kvs)
    return pl.pallas_call(
        functools.partial(attend_kernel, tuple(distances), first, last),
        out_shape=jax.ShapeDtypeStruct((rows, 2 * HD), BF) if last else (part, part),
        in_specs=[vmem] * n_in,
        out_specs=vmem if last else (vmem, vmem),
        input_output_aliases={} if (first or last) else {n_in - 2: 0, n_in - 1: 1},
        compiler_params=pltpu.CompilerParams(vmem_limit_bytes=8 << 20),
        cost_estimate=pl.CostEstimate(
            flops=elements * 512, bytes_accessed=4 << 20, transcendentals=2 * elements
        ),
    )(low, queries, *kvs, *(() if first else state))


def output_kernel(index_ref, *rest):
    n = len(PLACES)
    same, other = rest[:n], rest[n : 2 * n]
    w_ref, out_ref, square_ref = rest[2 * n :]
    features = out_ref.shape[0]
    slot = 0
    for k, places in enumerate(PLACES):
        for j in range(len(places)):
            total = None
            place = index_ref[2 + slot]
            for part, ref in enumerate((same[k], other[k])):
                parity = index_ref[0] if part == 0 else 1 - index_ref[0]
                swapped = jnp.where(parity == index_ref[1], 0, 1)
                product = lax.dot_general(
                    w_ref[2 * place + swapped],
                    ref[j],
                    (((1,), (1,)), ((), ())),
                    preferred_element_type=F32,
                )
                total = product if total is None else total + product
            if slot == 0:
                out_ref[...] = total
            elif slot < ROUNDS - 1:
                out_ref[...] += total
            else:
                total = out_ref[...] + total
                out_ref[...] = total
                square_ref[...] = jnp.sum(total * total, axis=0, keepdims=True)
            slot += 1


def output(chunks, weights, index):
    rows = chunks[0].shape[1]
    features = weights.shape[1]
    vmem = pl.BlockSpec(memory_space=pltpu.VMEM)
    return pl.pallas_call(
        output_kernel,
        out_shape=(
            jax.ShapeDtypeStruct((features, rows), F32),
            jax.ShapeDtypeStruct((1, rows), F32),
        ),
        in_specs=[pl.BlockSpec(memory_space=pltpu.SMEM)] + [vmem] * (len(chunks) + 1),
        out_specs=(vmem, vmem),
        compiler_params=pltpu.CompilerParams(vmem_limit_bytes=10 << 20),
        cost_estimate=pl.CostEstimate(
            flops=2 * rows * features * 4096, bytes_accessed=8 << 20, transcendentals=0
        ),
    )(index, *chunks, weights)


def shards(tokens, pre_gain, post_gain, w_query, w_key, w_value, w_out, segment_ids, page_table):
    rows = tokens.shape[0]
    features = tokens.shape[1]
    seq_index = lax.axis_index("seq")
    z = seq_index // 2
    h = lax.rem(seq_index, 2)
    base = seq_index * rows

    x_own = tokens.T.astype(F32)
    gained = (x_own * (1.0 + pre_gain.astype(F32))[:, None]).astype(BF)
    squares = jnp.sum(x_own * x_own, axis=0, keepdims=True)
    upper = lax.reduce_precision(squares, 8, 7)
    lower = squares - upper
    side = jnp.concatenate(
        [upper.astype(BF), lower.astype(BF), jnp.zeros((EXTRA - 2, rows), BF)], axis=0
    )
    x_all = lax.all_gather(jnp.concatenate([gained, side], axis=0), "mp", axis=0)
    depth = features + EXTRA

    counts = jnp.stack([jnp.sum((segment_ids < s).astype(jnp.int32)) for s in range(1, SEGS)])
    digits = jnp.concatenate([counts // 16, lax.rem(counts, 16)]).astype(BF)
    digits = jnp.pad(digits[None, :], ((2, EXTRA - 3), (0, 2 * HD - 2 * (SEGS - 1))))
    kv_own = jnp.concatenate([jnp.concatenate([w_key, w_value], axis=1), digits], axis=0)
    start = jnp.concatenate([kv_own, move(kv_own, ACROSS)], axis=0)
    turned = lax.ppermute(w_out.T, ("seq", "mp"), TURN)
    q_own = jnp.pad(w_query, ((0, EXTRA), (0, 0)))
    q_pair = jnp.concatenate([q_own, move(q_own, ACROSS)], axis=0)
    ring = {0: start, 1: move(start, AHEAD), -1: move(start, BEHIND)}
    ring[1], ring[-1], q_pair = tie(ring[1], ring[-1], q_pair)
    q_all = lax.all_gather(q_pair, "seq", axis=0, axis_index_groups=COLUMNS)
    ring[2] = move(ring[1], AHEAD)
    ring[-2] = move(ring[-1], BEHIND)
    ring[2], ring[-2], turned = tie(ring[2], ring[-2], turned)
    out_pair = jnp.concatenate([turned, move(turned, ACROSS)], axis=0)
    ring[3] = move(ring[2], AHEAD)
    ring[-3] = move(ring[-2], BEHIND)
    ring[3], ring[-3], out_pair = tie(ring[3], ring[-3], out_pair)
    out_all = lax.all_gather(out_pair, "seq", axis=0, axis_index_groups=COLUMNS)
    last = move(ring[3][:, :HD], AHEAD)
    ring[4] = jnp.concatenate([last, move(ring[-3][:, HD:], BEHIND)], axis=1)

    mp_index = lax.axis_index("mp")
    y = mp_index // 4
    over = lax.rem(mp_index // 2, 2)
    placed = [
        2 * lax.rem(y + dy + 4, 4) + jnp.where(dx == 0, over, 1 - over)
        for places in PLACES
        for dy, dx in places
    ]

    def index_of(steps, origin):
        places = [lax.rem(jnp.int32(origin - step + ROUNDS), ROUNDS) for step in steps]
        return jnp.stack([lax.rem(mp_index, 2), h, *placed, *places]).astype(jnp.int32)

    steps = [0, 1, -1, 2, -2, 3, -3, 4]
    index = index_of(steps, z)
    kv_weights = [ring[step] for step in steps]
    kv_pieces = tuple((k, None) for k in range(ROUNDS))
    q_pieces = tuple((0, k) for k in range(ROUNDS))

    n_marks = 2 * (SEGS - 1)
    marks = jnp.zeros((n_marks,), F32)
    for block in kv_weights:
        for part in range(2):
            marks = marks + block[part * depth + features + 2, :n_marks].astype(F32)
    starts = (marks[: SEGS - 1] * 16.0 + marks[SEGS - 1 :]).astype(jnp.int32)
    global_index = base + jnp.arange(rows, dtype=jnp.int32)
    offsets = jnp.zeros((rows,), jnp.int32)
    for s in range(1, SEGS):
        offsets = jnp.where(segment_ids == s, starts[s - 1], offsets)
    within = (global_index - offsets).astype(F32)
    low = (jnp.maximum(offsets, global_index - (WINDOW - 1)) - base)[:, None]
    half = HD // 2
    freqs = jnp.exp(-math.log(10000.0) * jnp.arange(half, dtype=F32) * (2.0 / HD))
    angles = freqs[:, None] * within[None, :]
    cos = jnp.cos(angles)
    sin = jnp.sin(angles)

    kv = project(x_all, kv_weights, kv_pieces, index, cos, sin, (True, False), 1.0)

    straight, crossed, current, crossing = [kv], [None], kv, None
    for step in range(4):
        following = move(current, LATER)
        chosen = jnp.where(h == 0, current, following)
        if crossing is None:
            following, chosen = tie(following, chosen)
        else:
            following, chosen, crossed[-1] = tie(following, chosen, crossing)
        crossing = move(chosen, ACROSS)
        straight.append(following)
        crossed.append(crossing)
        current = following
    q_all, straight[-1] = tie(q_all, straight[-1])
    queries = project(
        x_all,
        [q_all],
        q_pieces,
        index_of([-k for k in range(ROUNDS)], 0),
        cos,
        sin,
        (True, True),
        float(D // HQ) ** (-0.5),
    )
    state = attend(low, queries, [kv], [0], None)
    for k in range(1, 5):
        state = attend(low, queries, [straight[k], crossed[k]], [2 * k, 2 * k - 1], state)

    a_block = state[None]
    a_pair = jnp.concatenate([a_block, shift(a_block, SIDE)], axis=0)
    a_up, a_down = shift(a_pair, UP), shift(a_pair, DOWN)
    a_far = [shift(a_up[:1], UP), shift(a_down[1:], DOWN)]
    a_swaps = [shift(block, SWAP) for block in (a_pair, a_up, a_down, *a_far)]
    share, partial = output(
        [a_pair, a_up, a_down, *a_far, *a_swaps],
        out_all.reshape(2 * ROUNDS, features, 2 * HD),
        index,
    )
    everywhere = jnp.broadcast_to(partial, (lax.axis_size("mp"), rows))
    square_total = jnp.sum(lax.all_to_all(everywhere, "mp", 0, 0, tiled=True), axis=0)
    post_scale = lax.rsqrt(square_total / D + EPSILON)
    post = share * post_scale[None, :] * (1.0 + post_gain.astype(F32))[:, None]
    layer_output = (tokens.T.astype(F32) + post).astype(BF).T

    pages = page_table.shape[0]
    local_slot = page_table - seq_index * pages
    kv_pages = kv.reshape(pages, PAGE, 2 * HD)
    caches = []
    for slot in range(pages):
        chosen = kv_pages[0]
        for page in range(1, pages):
            chosen = jnp.where(local_slot[page] == slot, kv_pages[page], chosen)
        caches.append(chosen)
    caches = jnp.stack(caches)
    return (layer_output, caches[:, :, :HD], caches[:, :, HD:])


def solution(mesh):
    return jax.shard_map(
        shards,
        mesh=mesh,
        in_specs=(
            P("seq", "mp"),
            P("mp"),
            P("mp"),
            P("seq", "mp"),
            P("seq", "mp"),
            P("seq", "mp"),
            P("mp", "seq"),
            P("seq"),
            P("seq"),
        ),
        out_specs=(P("seq", "mp"), P("seq", None, "mp"), P("seq", None, "mp")),
        check_vma=False,
    )
```

```python
import functools
import math

import jax
import jax.numpy as jnp
from jax import lax
from jax.experimental import pallas as pl
from jax.experimental.pallas import tpu as pltpu
from jax.sharding import PartitionSpec as P

D = 4608
HQ = 32
HD = 128
WINDOW = 4096
PAGE = 128
SEGS = 4

EPSILON = 1e-06
SOFT_CAP = 50.0
LOG2E = 1.4426950408889634
EXTRA = 16
SEQ = 16
ROUNDS = 8

BF = jnp.bfloat16
F32 = jnp.float32

AHEAD = [(i, (i + 2) % SEQ) for i in range(SEQ)]
BEHIND = [((i + 2) % SEQ, i) for i in range(SEQ)]
LATER = [(i, i + 2) for i in range(SEQ - 2)]
ACROSS = [(i, i ^ 1) for i in range(SEQ)]
TURNS = (
    [(s * SEQ + m, s * SEQ + (s + m) % SEQ) for s in range(SEQ) for m in range(SEQ)],
    [(s * SEQ + c, ((c - s) % SEQ) * SEQ + c) for s in range(SEQ) for c in range(SEQ)],
    [(m * SEQ + c, m * SEQ + (c - m) % SEQ) for m in range(SEQ) for c in range(SEQ)],
)


SIDE = [(i, i ^ 2) for i in range(SEQ)]
UP = [(i, (i + 4) % SEQ) for i in range(SEQ)]
DOWN = [((i + 4) % SEQ, i) for i in range(SEQ)]
SWAP = [(i, i ^ 1) for i in range(SEQ)]
COLUMNS = [[2 * i + c for i in range(ROUNDS)] for c in range(2)]
PLACES = (((0, 0), (0, 1)), ((-1, 0), (-1, 1)), ((1, 0), (1, 1)), ((2, 0),), ((2, 1),))


def move(block, perm):
    return lax.ppermute(block, "seq", perm)


def shift(block, perm):
    return lax.ppermute(block, "mp", perm)


def tie(*values):
    return lax.optimization_barrier(values)


def project_kernel(pieces, rotated, factor, index_ref, cos_ref, sin_ref, x_hbm, *rest):
    w_refs = rest[:-6]
    out_ref, x_ref, w_ref, acc_ref, x_sem, w_sem = rest[-6:]
    chunks, depth, rows = x_ref.shape
    copies = []
    for slot in range(ROUNDS):
        place = index_ref[2 + ROUNDS + slot]
        for part in range(2):
            parity = index_ref[1] if part == 0 else 1 - index_ref[1]
            which, lead = pieces[slot]
            source = w_refs[which] if lead is None else w_refs[which].at[lead]
            copies.append(
                pltpu.make_async_copy(
                    source.at[pl.ds(part * depth, depth)],
                    w_ref.at[2 * place + parity],
                    w_sem.at[2 * slot + part],
                )
            )
    step = chunks // 4
    for k in range(4):
        copies.append(
            pltpu.make_async_copy(
                x_hbm.at[pl.ds(k * step, step)], x_ref.at[pl.ds(k * step, step)], x_sem.at[k]
            )
        )
    for copy in copies:
        copy.start()
    for copy in copies[:-4]:
        copy.wait()
    squares = jnp.zeros((1, rows), F32)
    for k in range(4):
        copies[k - 4].wait()
        here = slice(k * step, (k + 1) * step)
        side = x_ref[here, depth - EXTRA :, :].astype(F32)
        squares = squares + jnp.sum(jnp.sum(side, axis=0), axis=0, keepdims=True)
        product = lax.dot_general(
            w_ref[here].reshape(step * depth, 2 * HD),
            x_ref[here].reshape(step * depth, rows),
            (((0,), (0,)), ((), ())),
            preferred_element_type=F32,
        )
        if k == 0:
            acc_ref[...] = product
        else:
            acc_ref[...] += product
    scale = lax.rsqrt(squares * (1.0 / D) + EPSILON)
    half = HD // 2
    for head in range(2):
        start = head * HD
        if rotated[head]:
            first = acc_ref[start : start + half, :] * scale
            second = acc_ref[start + half : start + HD, :] * scale
            cos, sin = cos_ref[...], sin_ref[...]
            value = jnp.concatenate(
                [first * cos - second * sin, second * cos + first * sin], axis=0
            )
            if factor != 1.0:
                value = value * factor
        else:
            value = acc_ref[start : start + HD, :] * scale
        out_ref[:, start : start + HD] = jnp.transpose(value).astype(BF)


def project(x_all, weights, pieces, index, cos, sin, rotated, factor):
    chunks, depth, rows = x_all.shape
    vmem = pl.BlockSpec(memory_space=pltpu.VMEM)
    outside = pl.BlockSpec(memory_space=pl.ANY)
    return pl.pallas_call(
        functools.partial(project_kernel, pieces, rotated, factor),
        out_shape=jax.ShapeDtypeStruct((rows, 2 * HD), BF),
        in_specs=[pl.BlockSpec(memory_space=pltpu.SMEM), vmem, vmem]
        + [outside] * (1 + len(weights)),
        out_specs=vmem,
        scratch_shapes=[
            pltpu.VMEM((chunks, depth, rows), BF),
            pltpu.VMEM((chunks, depth, 2 * HD), BF),
            pltpu.VMEM((2 * HD, rows), F32),
            pltpu.SemaphoreType.DMA((4,)),
            pltpu.SemaphoreType.DMA((2 * ROUNDS,)),
        ],
        compiler_params=pltpu.CompilerParams(vmem_limit_bytes=60 << 20),
        cost_estimate=pl.CostEstimate(
            flops=2 * rows * 2 * HD * D, bytes_accessed=8 << 20, transcendentals=0
        ),
    )(index, cos, sin, x_all, *weights)


def attend_kernel(distances, first, last, low_ref, q_ref, *rest):
    n = len(distances)
    kv_refs = rest[:n]
    rest = rest[n:]
    if not first:
        sum_in, den_in = rest[:2]
        rest = rest[2:]
    rows = q_ref.shape[0]
    tile = 256

    def part(index, carry):
        here = pl.ds(pl.multiple_of((index // 2) * tile, tile), tile)
        columns = pl.ds(pl.multiple_of(lax.rem(index, 2) * HD, HD), HD)
        q = q_ref[here, columns]
        low = low_ref[here, :]
        if first:
            total = jnp.zeros((tile, HD), F32)
            den = jnp.zeros((tile, HD), F32)
        else:
            total = sum_in[here, columns]
            den = den_in[here, columns]
        for kv_ref, distance in zip(kv_refs, distances):
            score = lax.dot_general(
                q, kv_ref[:, :HD], (((1,), (1,)), ((), ())), preferred_element_type=F32
            )
            weight = jnp.exp2(jnp.tanh(score * (1.0 / SOFT_CAP)) * (SOFT_CAP * LOG2E))
            place = lax.broadcasted_iota(jnp.int32, (tile, rows), 1)
            allowed = place >= low + distance * rows
            if distance == 0:
                own = lax.broadcasted_iota(jnp.int32, (tile, rows), 0) + (index // 2) * tile
                allowed = allowed & (place <= own)
            weight = jnp.where(allowed, weight, 0.0)
            for c in range(rows // HD):
                den = den + weight[:, c * HD : (c + 1) * HD]
            total = total + jnp.dot(
                weight.astype(BF), kv_ref[:, HD:], preferred_element_type=F32
            )
        if last:
            whole = jnp.sum(den, axis=1, keepdims=True)
            rest[0][here, columns] = (total / whole).astype(BF)
        else:
            rest[0][here, columns] = total
            rest[1][here, columns] = den
        return carry

    lax.fori_loop(0, 2 * (rows // tile), part, 0)


def attend(low, queries, kvs, distances, state):
    first = state is None
    last = 8 in distances
    rows = queries.shape[0]
    vmem = pl.BlockSpec(memory_space=pltpu.VMEM)
    n_in = 2 + len(kvs) + (0 if first else 2)
    part = jax.ShapeDtypeStruct((rows, 2 * HD), F32)
    elements = 2 * rows * rows * len(kvs)
    return pl.pallas_call(
        functools.partial(attend_kernel, tuple(distances), first, last),
        out_shape=jax.ShapeDtypeStruct((rows, 2 * HD), BF) if last else (part, part),
        in_specs=[vmem] * n_in,
        out_specs=vmem if last else (vmem, vmem),
        input_output_aliases={} if (first or last) else {n_in - 2: 0, n_in - 1: 1},
        compiler_params=pltpu.CompilerParams(vmem_limit_bytes=8 << 20),
        cost_estimate=pl.CostEstimate(
            flops=elements * 512, bytes_accessed=4 << 20, transcendentals=2 * elements
        ),
    )(low, queries, *kvs, *(() if first else state))


def output_kernel(index_ref, *rest):
    n = len(PLACES)
    same, other = rest[:n], rest[n : 2 * n]
    w_ref, out_ref, square_ref = rest[2 * n :]
    features = out_ref.shape[0]
    slot = 0
    for k, places in enumerate(PLACES):
        for j in range(len(places)):
            total = None
            place = index_ref[2 + slot]
            for part, ref in enumerate((same[k], other[k])):
                parity = index_ref[0] if part == 0 else 1 - index_ref[0]
                swapped = jnp.where(parity == index_ref[1], 0, 1)
                product = lax.dot_general(
                    w_ref[2 * place + swapped],
                    ref[j],
                    (((1,), (1,)), ((), ())),
                    preferred_element_type=F32,
                )
                total = product if total is None else total + product
            if slot == 0:
                out_ref[...] = total
            elif slot < ROUNDS - 1:
                out_ref[...] += total
            else:
                total = out_ref[...] + total
                out_ref[...] = total
                square_ref[...] = jnp.sum(total * total, axis=0, keepdims=True)
            slot += 1


def output(chunks, weights, index):
    rows = chunks[0].shape[1]
    features = weights.shape[1]
    vmem = pl.BlockSpec(memory_space=pltpu.VMEM)
    return pl.pallas_call(
        output_kernel,
        out_shape=(
            jax.ShapeDtypeStruct((features, rows), F32),
            jax.ShapeDtypeStruct((1, rows), F32),
        ),
        in_specs=[pl.BlockSpec(memory_space=pltpu.SMEM)] + [vmem] * (len(chunks) + 1),
        out_specs=(vmem, vmem),
        compiler_params=pltpu.CompilerParams(vmem_limit_bytes=10 << 20),
        cost_estimate=pl.CostEstimate(
            flops=2 * rows * features * 4096, bytes_accessed=8 << 20, transcendentals=0
        ),
    )(index, *chunks, weights)


def shards(tokens, pre_gain, post_gain, w_query, w_key, w_value, w_out, segment_ids, page_table):
    rows = tokens.shape[0]
    features = tokens.shape[1]
    seq_index = lax.axis_index("seq")
    z = seq_index // 2
    h = lax.rem(seq_index, 2)
    base = seq_index * rows

    x_own = tokens.T.astype(F32)
    gained = (x_own * (1.0 + pre_gain.astype(F32))[:, None]).astype(BF)
    squares = jnp.sum(x_own * x_own, axis=0, keepdims=True)
    upper = lax.reduce_precision(squares, 8, 7)
    lower = squares - upper
    side = jnp.concatenate(
        [upper.astype(BF), lower.astype(BF), jnp.zeros((EXTRA - 2, rows), BF)], axis=0
    )
    x_all = lax.all_gather(jnp.concatenate([gained, side], axis=0), "mp", axis=0)
    depth = features + EXTRA

    lane = jnp.arange(2 * HD, dtype=jnp.int32)
    marked = 2 * (SEGS - 1)
    limit = jnp.where(lane < marked, lax.rem(lane, SEGS - 1) + 1, 0)
    counts = jnp.sum((segment_ids[:, None] < limit[None, :]).astype(F32), axis=0)
    upper_digit = jnp.floor(counts * (1.0 / 16.0))
    digits = jnp.where(lane < SEGS - 1, upper_digit, counts - 16.0 * upper_digit).astype(BF)
    digits = jnp.pad(digits[None, :], ((2, EXTRA - 3), (0, 0)))
    kv_own = jnp.concatenate([jnp.concatenate([w_key, w_value], axis=1), digits], axis=0)
    start = jnp.concatenate([kv_own, move(kv_own, ACROSS)], axis=0)
    ring = {0: start, 1: move(start, AHEAD), -1: move(start, BEHIND)}
    turned = lax.ppermute(w_out.T, ("seq", "mp"), TURNS[0])
    ring[2] = move(ring[1], AHEAD)
    ring[-2] = move(ring[-1], BEHIND)
    ring[2], ring[-2], turned = tie(ring[2], ring[-2], turned)
    q_own = jnp.pad(w_query, ((0, EXTRA), (0, 0)))
    q_own, _ = tie(q_own, ring[1])
    q_pair = jnp.concatenate([q_own, move(q_own, ACROSS)], axis=0)
    turned = lax.ppermute(turned, ("seq", "mp"), TURNS[1])
    ring[3] = move(ring[2], AHEAD)
    ring[-3] = move(ring[-2], BEHIND)
    ring[3], ring[-3], turned, q_pair = tie(ring[3], ring[-3], turned, q_pair)
    q_all = lax.all_gather(q_pair, "seq", axis=0, axis_index_groups=COLUMNS)
    turned = lax.ppermute(turned, ("seq", "mp"), TURNS[2])
    last = move(ring[3][:, :HD], AHEAD)
    ring[4] = jnp.concatenate([last, move(ring[-3][:, HD:], BEHIND)], axis=1)
    ring[4], turned = tie(ring[4], turned)
    facing_out = move(turned, ACROSS)

    mp_index = lax.axis_index("mp")
    y = mp_index // 4
    over = lax.rem(mp_index // 2, 2)
    placed = [
        2 * lax.rem(y + dy + 4, 4) + jnp.where(dx == 0, over, 1 - over)
        for places in PLACES
        for dy, dx in places
    ]

    def index_of(steps, origin):
        places = [lax.rem(jnp.int32(origin - step + ROUNDS), ROUNDS) for step in steps]
        return jnp.stack([lax.rem(mp_index, 2), h, *placed, *places]).astype(jnp.int32)

    steps = [0, 1, -1, 2, -2, 3, -3, 4]
    index = index_of(steps, z)
    kv_weights = [ring[step] for step in steps]
    kv_pieces = tuple((k, None) for k in range(ROUNDS))
    q_pieces = tuple((0, k) for k in range(ROUNDS))

    n_marks = 2 * (SEGS - 1)
    marks = jnp.zeros((n_marks,), F32)
    for block in kv_weights:
        for part in range(2):
            marks = marks + block[part * depth + features + 2, :n_marks].astype(F32)
    starts = (marks[: SEGS - 1] * 16.0 + marks[SEGS - 1 :]).astype(jnp.int32)
    global_index = base + jnp.arange(rows, dtype=jnp.int32)
    offsets = jnp.zeros((rows,), jnp.int32)
    for s in range(1, SEGS):
        offsets = jnp.where(segment_ids == s, starts[s - 1], offsets)
    within = (global_index - offsets).astype(F32)
    low = (jnp.maximum(offsets, global_index - (WINDOW - 1)) - base)[:, None]
    half = HD // 2
    freqs = jnp.exp(-math.log(10000.0) * jnp.arange(half, dtype=F32) * (2.0 / HD))
    angles = freqs[:, None] * within[None, :]
    cos = jnp.cos(angles)
    sin = jnp.sin(angles)

    kv = project(x_all, kv_weights, kv_pieces, index, cos, sin, (True, False), 1.0)

    straight, crossed, current = [kv], [None], kv
    for step in range(4):
        following = move(current, LATER)
        chosen = jnp.where(h == 0, current, following)
        if step == 0:
            following, chosen, facing_out = tie(following, chosen, facing_out)
            out_pair = jnp.concatenate([turned, facing_out], axis=0)
            out_all = lax.all_gather(out_pair, "seq", axis=0, axis_index_groups=COLUMNS)
        else:
            following, chosen, crossed[step] = tie(following, chosen, crossed[step])
        straight.append(following)
        crossed.append(move(chosen, ACROSS))
        current = following
    q_all, straight[-1] = tie(q_all, straight[-1])
    queries = project(
        x_all,
        [q_all],
        q_pieces,
        index_of([-k for k in range(ROUNDS)], 0),
        cos,
        sin,
        (True, True),
        float(D // HQ) ** (-0.5),
    )
    state = attend(low, queries, [kv], [0], None)
    for k in range(1, 5):
        state = attend(low, queries, [straight[k], crossed[k]], [2 * k, 2 * k - 1], state)

    a_block = state[None]
    a_pair = jnp.concatenate([a_block, shift(a_block, SIDE)], axis=0)
    a_up, a_down = shift(a_pair, UP), shift(a_pair, DOWN)
    a_up, a_down, out_all = tie(a_up, a_down, out_all)
    a_far = [shift(a_up[:1], UP), shift(a_down[1:], DOWN)]
    a_swaps = [shift(block, SWAP) for block in (a_pair, a_up, a_down, *a_far)]
    share, partial = output(
        [a_pair, a_up, a_down, *a_far, *a_swaps],
        out_all.reshape(2 * ROUNDS, features, 2 * HD),
        index,
    )
    everywhere = jnp.broadcast_to(partial, (lax.axis_size("mp"), rows))
    square_total = jnp.sum(lax.all_to_all(everywhere, "mp", 0, 0, tiled=True), axis=0)
    post_scale = lax.rsqrt(square_total / D + EPSILON)
    post = share * post_scale[None, :] * (1.0 + post_gain.astype(F32))[:, None]
    layer_output = (tokens.T.astype(F32) + post).astype(BF).T

    pages = page_table.shape[0]
    local_slot = page_table - seq_index * pages
    kv_pages = kv.reshape(pages, PAGE, 2 * HD)
    caches = []
    for slot in range(pages):
        chosen = kv_pages[0]
        for page in range(1, pages):
            chosen = jnp.where(local_slot[page] == slot, kv_pages[page], chosen)
        caches.append(chosen)
    caches = jnp.stack(caches)
    return (layer_output, caches[:, :, :HD], caches[:, :, HD:])


def solution(mesh):
    return jax.shard_map(
        shards,
        mesh=mesh,
        in_specs=(
            P("seq", "mp"),
            P("mp"),
            P("mp"),
            P("seq", "mp"),
            P("seq", "mp"),
            P("seq", "mp"),
            P("mp", "seq"),
            P("seq"),
            P("seq"),
        ),
        out_specs=(P("seq", "mp"), P("seq", None, "mp"), P("seq", None, "mp")),
        check_vma=False,
    )
```

```python
import functools
import math

import jax
import jax.numpy as jnp
from jax import lax
from jax.experimental import pallas as pl
from jax.experimental.pallas import tpu as pltpu
from jax.sharding import PartitionSpec as P

D = 4608
HQ = 32
HD = 128
WINDOW = 4096
PAGE = 128
SEGS = 4

EPSILON = 1e-06
SOFT_CAP = 50.0
LOG2E = 1.4426950408889634
EXTRA = 16
SEQ = 16
ROUNDS = 8

BF = jnp.bfloat16
F32 = jnp.float32

AHEAD = [(i, (i + 2) % SEQ) for i in range(SEQ)]
BEHIND = [((i + 2) % SEQ, i) for i in range(SEQ)]
LATER = [(i, i + 2) for i in range(SEQ - 2)]
ACROSS = [(i, i ^ 1) for i in range(SEQ)]
TURNS = (
    [(s * SEQ + m, s * SEQ + (s + m) % SEQ) for s in range(SEQ) for m in range(SEQ)],
    [(s * SEQ + c, ((c - s) % SEQ) * SEQ + c) for s in range(SEQ) for c in range(SEQ)],
    [(m * SEQ + c, m * SEQ + (c - m) % SEQ) for m in range(SEQ) for c in range(SEQ)],
)


SIDE = [(i, i ^ 2) for i in range(SEQ)]
UP = [(i, (i + 4) % SEQ) for i in range(SEQ)]
DOWN = [((i + 4) % SEQ, i) for i in range(SEQ)]
SWAP = [(i, i ^ 1) for i in range(SEQ)]
COLUMNS = [[2 * i + c for i in range(ROUNDS)] for c in range(2)]
PLACES = (((0, 0), (0, 1)), ((-1, 0), (-1, 1)), ((1, 0), (1, 1)), ((2, 0),), ((2, 1),))


def move(block, perm):
    return lax.ppermute(block, "seq", perm)


def shift(block, perm):
    return lax.ppermute(block, "mp", perm)


def tie(*values):
    return lax.optimization_barrier(values)


def project_kernel(pieces, rotated, factor, index_ref, cos_ref, sin_ref, *rest):
    n = len(PLACES)
    same, other, w_refs = rest[:n], rest[n : 2 * n], rest[2 * n : -6]
    out_ref, x_ref, w_ref, acc_ref, x_sem, w_sem = rest[-6:]
    chunks, depth, rows = x_ref.shape
    step = chunks // 4
    length = pieces[0][0][2]
    copies = []
    for slot in range(ROUNDS):
        place = index_ref[2 + ROUNDS + slot]
        for part in range(2):
            parity = index_ref[1] if part == 0 else 1 - index_ref[1]
            which, start, _ = pieces[slot][part]
            copies.append(
                pltpu.make_async_copy(
                    w_refs[which].at[pl.ds(start, length)],
                    w_ref.at[2 * place + parity, pl.ds(0, length)],
                    w_sem.at[2 * slot + part],
                )
            )
    slot = 0
    for k, places in enumerate(PLACES):
        for j in range(len(places)):
            place = index_ref[2 + slot]
            for part, ref in enumerate((same[k], other[k])):
                parity = index_ref[0] if part == 0 else 1 - index_ref[0]
                copies.append(
                    pltpu.make_async_copy(
                        ref.at[j], x_ref.at[2 * place + parity], x_sem.at[2 * slot + part]
                    )
                )
            slot += 1
    for copy in copies:
        copy.start()
    if length < depth:
        w_ref[:, length:, :] = jnp.zeros((chunks, depth - length, 2 * HD), BF)
    for copy in copies:
        copy.wait()
    squares = jnp.zeros((1, rows), F32)
    for k in range(4):
        here = slice(k * step, (k + 1) * step)
        side = x_ref[here, depth - EXTRA :, :].astype(F32)
        squares = squares + jnp.sum(jnp.sum(side, axis=0), axis=0, keepdims=True)
        product = lax.dot_general(
            w_ref[here].reshape(step * depth, 2 * HD),
            x_ref[here].reshape(step * depth, rows),
            (((0,), (0,)), ((), ())),
            preferred_element_type=F32,
        )
        if k == 0:
            acc_ref[...] = product
        else:
            acc_ref[...] += product
    scale = lax.rsqrt(squares * (1.0 / D) + EPSILON)
    half = HD // 2
    for head in range(2):
        start = head * HD
        if rotated[head]:
            first = acc_ref[start : start + half, :] * scale
            second = acc_ref[start + half : start + HD, :] * scale
            cos, sin = cos_ref[...], sin_ref[...]
            value = jnp.concatenate(
                [first * cos - second * sin, second * cos + first * sin], axis=0
            )
            if factor != 1.0:
                value = value * factor
        else:
            value = acc_ref[start : start + HD, :] * scale
        out_ref[:, start : start + HD] = jnp.transpose(value).astype(BF)


def project(chunks, weights, pieces, index, cos, sin, rotated, factor):
    _, depth, rows = chunks[0].shape
    vmem = pl.BlockSpec(memory_space=pltpu.VMEM)
    outside = pl.BlockSpec(memory_space=pl.ANY)
    return pl.pallas_call(
        functools.partial(project_kernel, pieces, rotated, factor),
        out_shape=jax.ShapeDtypeStruct((rows, 2 * HD), BF),
        in_specs=[pl.BlockSpec(memory_space=pltpu.SMEM), vmem, vmem]
        + [outside] * (len(chunks) + len(weights)),
        out_specs=vmem,
        scratch_shapes=[
            pltpu.VMEM((2 * ROUNDS, depth, rows), BF),
            pltpu.VMEM((2 * ROUNDS, depth, 2 * HD), BF),
            pltpu.VMEM((2 * HD, rows), F32),
            pltpu.SemaphoreType.DMA((2 * ROUNDS,)),
            pltpu.SemaphoreType.DMA((2 * ROUNDS,)),
        ],
        compiler_params=pltpu.CompilerParams(vmem_limit_bytes=60 << 20),
        cost_estimate=pl.CostEstimate(
            flops=2 * rows * 2 * HD * D, bytes_accessed=8 << 20, transcendentals=0
        ),
    )(index, cos, sin, *chunks, *weights)


def attend_kernel(distances, first, last, low_ref, q_ref, *rest):
    n = len(distances)
    kv_refs = rest[:n]
    rest = rest[n:]
    if not first:
        sum_in, den_in = rest[:2]
        rest = rest[2:]
    rows = q_ref.shape[0]
    tile = 256

    def part(index, carry):
        here = pl.ds(pl.multiple_of((index // 2) * tile, tile), tile)
        columns = pl.ds(pl.multiple_of(lax.rem(index, 2) * HD, HD), HD)
        q = q_ref[here, columns]
        low = low_ref[here, :]
        if first:
            total = jnp.zeros((tile, HD), F32)
            den = jnp.zeros((tile, HD), F32)
        else:
            total = sum_in[here, columns]
            den = den_in[here, columns]
        for kv_ref, distance in zip(kv_refs, distances):
            score = lax.dot_general(
                q, kv_ref[:, :HD], (((1,), (1,)), ((), ())), preferred_element_type=F32
            )
            weight = jnp.exp2(jnp.tanh(score * (1.0 / SOFT_CAP)) * (SOFT_CAP * LOG2E))
            place = lax.broadcasted_iota(jnp.int32, (tile, rows), 1)
            allowed = place >= low + distance * rows
            if distance == 0:
                own = lax.broadcasted_iota(jnp.int32, (tile, rows), 0) + (index // 2) * tile
                allowed = allowed & (place <= own)
            weight = jnp.where(allowed, weight, 0.0)
            for c in range(rows // HD):
                den = den + weight[:, c * HD : (c + 1) * HD]
            total = total + jnp.dot(
                weight.astype(BF), kv_ref[:, HD:], preferred_element_type=F32
            )
        if last:
            whole = jnp.sum(den, axis=1, keepdims=True)
            rest[0][here, columns] = (total / whole).astype(BF)
        else:
            rest[0][here, columns] = total
            rest[1][here, columns] = den
        return carry

    lax.fori_loop(0, 2 * (rows // tile), part, 0)


def attend(low, queries, kvs, distances, state):
    first = state is None
    last = 8 in distances
    rows = queries.shape[0]
    vmem = pl.BlockSpec(memory_space=pltpu.VMEM)
    n_in = 2 + len(kvs) + (0 if first else 2)
    part = jax.ShapeDtypeStruct((rows, 2 * HD), F32)
    elements = 2 * rows * rows * len(kvs)
    return pl.pallas_call(
        functools.partial(attend_kernel, tuple(distances), first, last),
        out_shape=jax.ShapeDtypeStruct((rows, 2 * HD), BF) if last else (part, part),
        in_specs=[vmem] * n_in,
        out_specs=vmem if last else (vmem, vmem),
        input_output_aliases={} if (first or last) else {n_in - 2: 0, n_in - 1: 1},
        compiler_params=pltpu.CompilerParams(vmem_limit_bytes=8 << 20),
        cost_estimate=pl.CostEstimate(
            flops=elements * 512, bytes_accessed=4 << 20, transcendentals=2 * elements
        ),
    )(low, queries, *kvs, *(() if first else state))


def output_kernel(index_ref, *rest):
    n = len(PLACES)
    same, other, w_refs = rest[:n], rest[n : 2 * n], rest[2 * n : -4]
    out_ref, square_ref, w_ref, sem = rest[-4:]
    features = out_ref.shape[0]
    copies = []
    for slot in range(ROUNDS):
        place = index_ref[2 + ROUNDS + slot]
        copies.append(pltpu.make_async_copy(w_refs[slot], w_ref.at[place], sem.at[slot]))
    for copy in copies:
        copy.start()
    for copy in copies:
        copy.wait()
    slot = 0
    for k, places in enumerate(PLACES):
        for j in range(len(places)):
            total = None
            place = index_ref[2 + slot]
            for part, ref in enumerate((same[k], other[k])):
                parity = index_ref[0] if part == 0 else 1 - index_ref[0]
                swapped = jnp.where(parity == index_ref[1], 0, features)
                product = lax.dot_general(
                    w_ref[place, pl.ds(pl.multiple_of(swapped, 16), features), :],
                    ref[j],
                    (((1,), (1,)), ((), ())),
                    preferred_element_type=F32,
                )
                total = product if total is None else total + product
            if slot == 0:
                out_ref[...] = total
            elif slot < ROUNDS - 1:
                out_ref[...] += total
            else:
                total = out_ref[...] + total
                out_ref[...] = total
                square_ref[...] = jnp.sum(total * total, axis=0, keepdims=True)
            slot += 1


def output(chunks, weights, index):
    rows = chunks[0].shape[1]
    features = weights[0].shape[0] // 2
    vmem = pl.BlockSpec(memory_space=pltpu.VMEM)
    outside = pl.BlockSpec(memory_space=pl.ANY)
    return pl.pallas_call(
        output_kernel,
        out_shape=(
            jax.ShapeDtypeStruct((features, rows), F32),
            jax.ShapeDtypeStruct((1, rows), F32),
        ),
        in_specs=[pl.BlockSpec(memory_space=pltpu.SMEM)]
        + [vmem] * len(chunks)
        + [outside] * len(weights),
        out_specs=(vmem, vmem),
        scratch_shapes=[
            pltpu.VMEM((ROUNDS, 2 * features, 2 * HD), BF),
            pltpu.SemaphoreType.DMA((ROUNDS,)),
        ],
        compiler_params=pltpu.CompilerParams(vmem_limit_bytes=12 << 20),
        cost_estimate=pl.CostEstimate(
            flops=2 * rows * features * 4096, bytes_accessed=8 << 20, transcendentals=0
        ),
    )(index, *chunks, *weights)


def shards(tokens, pre_gain, post_gain, w_query, w_key, w_value, w_out, segment_ids, page_table):
    rows = tokens.shape[0]
    features = tokens.shape[1]
    seq_index = lax.axis_index("seq")
    z = seq_index // 2
    h = lax.rem(seq_index, 2)
    base = seq_index * rows

    x_own = tokens.T.astype(F32)
    gained = (x_own * (1.0 + pre_gain.astype(F32))[:, None]).astype(BF)
    squares = jnp.sum(x_own * x_own, axis=0, keepdims=True)
    upper = lax.reduce_precision(squares, 8, 7)
    lower = squares - upper
    side = jnp.concatenate(
        [upper.astype(BF), lower.astype(BF), jnp.zeros((EXTRA - 2, rows), BF)], axis=0
    )
    x_block = jnp.concatenate([gained, side], axis=0)[None]
    depth = features + EXTRA
    q_from = 2 * depth

    lane = jnp.arange(2 * HD, dtype=jnp.int32)
    marked = 2 * (SEGS - 1)
    limit = jnp.where(lane < marked, lax.rem(lane, SEGS - 1) + 1, 0)
    counts = jnp.sum((segment_ids[:, None] < limit[None, :]).astype(F32), axis=0)
    upper_digit = jnp.floor(counts * (1.0 / 16.0))
    digits = jnp.where(lane < SEGS - 1, upper_digit, counts - 16.0 * upper_digit).astype(BF)
    digits = jnp.pad(digits[None, :], ((2, EXTRA - 3), (0, 0)))
    kv_own = jnp.concatenate([jnp.concatenate([w_key, w_value], axis=1), digits], axis=0)
    start = jnp.concatenate([kv_own, move(kv_own, ACROSS), w_query], axis=0)
    x_pair = jnp.concatenate([x_block, shift(x_block, SIDE)], axis=0)

    ring = {0: start, 1: move(start, AHEAD), -1: move(start, BEHIND)}
    x_up, x_down = shift(x_pair, UP), shift(x_pair, DOWN)
    x_swaps = [shift(x_pair, SWAP)]
    cross_near = move(
        jnp.concatenate([w_query, ring[1][q_from:], ring[-1][q_from:]], axis=0), ACROSS
    )
    ring[2] = move(ring[1], AHEAD)
    ring[-2] = move(ring[-1], BEHIND)
    ring[2], ring[-2], x_up, x_down, x_swaps[0] = tie(ring[2], ring[-2], x_up, x_down, x_swaps[0])
    x_swaps += [shift(x_up, SWAP), shift(x_down, SWAP)]
    x_far = [shift(x_up[:1], UP), shift(x_down[1:], DOWN)]
    cross_next = move(jnp.concatenate([ring[2][q_from:], ring[-2][q_from:]], axis=0), ACROSS)
    ring[3] = move(ring[2], AHEAD)
    ring[-3] = move(ring[-2], BEHIND)
    turned = lax.ppermute(w_out.T, ("seq", "mp"), TURNS[0])
    (ring[3], ring[-3], cross_near, x_far[0], x_far[1], x_swaps[1], x_swaps[2], turned) = tie(
        ring[3], ring[-3], cross_near, x_far[0], x_far[1], x_swaps[1], x_swaps[2], turned
    )
    x_swaps += [shift(x_far[0], SWAP), shift(x_far[1], SWAP)]
    ring[4] = move(ring[3][:q_from], AHEAD)
    ring[-4] = move(ring[-3][q_from:], BEHIND)
    turned = lax.ppermute(turned, ("seq", "mp"), TURNS[1])
    ring[4], ring[-4], cross_next, turned = tie(ring[4], ring[-4], cross_next, turned)
    x_chunks = [x_pair, x_up, x_down, *x_far, *x_swaps]

    mp_index = lax.axis_index("mp")
    y = mp_index // 4
    over = lax.rem(mp_index // 2, 2)
    placed = [
        2 * lax.rem(y + dy + 4, 4) + jnp.where(dx == 0, over, 1 - over)
        for places in PLACES
        for dy, dx in places
    ]

    def index_of(steps, origin):
        places = [lax.rem(jnp.int32(origin - step + ROUNDS), ROUNDS) for step in steps]
        return jnp.stack([lax.rem(mp_index, 2), h, *placed, *places]).astype(jnp.int32)

    steps = [0, 1, -1, 2, -2, 3, -3, 4]
    index = index_of(steps, z)
    kv_weights = [ring[step] for step in steps]
    kv_pieces = tuple(((k, 0, depth), (k, depth, depth)) for k in range(ROUNDS))
    q_weights = kv_weights[:7] + [ring[-4], w_query, cross_near, cross_next]
    crossings = [(9, k * features) for k in range(3)]
    crossings += [(10, k * features) for k in range(2)]
    crossings += [(11, k * features) for k in range(3)]
    own_places = [(8, 0)] + [(k, q_from) for k in range(1, 7)] + [(7, 0)]
    q_pieces = tuple(
        ((*own_places[k], features), (*crossings[k], features)) for k in range(ROUNDS)
    )

    n_marks = 2 * (SEGS - 1)
    marks = jnp.zeros((n_marks,), F32)
    for block in kv_weights:
        for part in range(2):
            marks = marks + block[part * depth + features + 2, :n_marks].astype(F32)
    starts = (marks[: SEGS - 1] * 16.0 + marks[SEGS - 1 :]).astype(jnp.int32)
    global_index = base + jnp.arange(rows, dtype=jnp.int32)
    offsets = jnp.zeros((rows,), jnp.int32)
    for s in range(1, SEGS):
        offsets = jnp.where(segment_ids == s, starts[s - 1], offsets)
    within = (global_index - offsets).astype(F32)
    low = (jnp.maximum(offsets, global_index - (WINDOW - 1)) - base)[:, None]
    half = HD // 2
    freqs = jnp.exp(-math.log(10000.0) * jnp.arange(half, dtype=F32) * (2.0 / HD))
    angles = freqs[:, None] * within[None, :]
    cos = jnp.cos(angles)
    sin = jnp.sin(angles)

    kv = project(x_chunks, kv_weights, kv_pieces, index, cos, sin, (True, False), 1.0)

    cross_last = move(
        jnp.concatenate([ring[3][q_from:], ring[-3][q_from:], ring[-4]], axis=0), ACROSS
    )
    turned = lax.ppermute(turned, ("seq", "mp"), TURNS[2])
    straight, crossed, current, state = [kv], [None], kv, None
    out_blocks = {}
    for step in range(4):
        following = move(current, LATER)
        chosen = jnp.where(h == 0, current, following)
        if step == 0:
            following, chosen, turned = tie(following, chosen, turned)
            out_blocks[0] = jnp.concatenate([turned, move(turned, ACROSS)], axis=0)
        elif step == 1:
            following, chosen, crossed[1], cross_last, out_blocks[0] = tie(
                following, chosen, crossed[1], cross_last, out_blocks[0]
            )
            out_blocks[-1] = move(out_blocks[0], BEHIND)
            queries = project(
                x_chunks,
                q_weights + [cross_last],
                q_pieces,
                index_of(steps[:7] + [-4], z),
                cos,
                sin,
                (True, True),
                float(D // HQ) ** (-0.5),
            )
            state = attend(low, queries, [kv], [0], None)
        else:
            following, chosen, crossed[step], out_blocks[1 - step], *state = tie(
                following, chosen, crossed[step], out_blocks[1 - step], *state
            )
            k = step - 1
            state = attend(low, queries, [straight[k], crossed[k]], [2 * k, 2 * k - 1], state)
            if step == 2:
                out_blocks[-2] = move(out_blocks[-1], BEHIND)
        straight.append(following)
        crossed.append(move(chosen, ACROSS))
        current = following
    out_blocks[1] = move(out_blocks[0], AHEAD)
    out_blocks[-3] = move(out_blocks[-2], BEHIND)
    state = attend(low, queries, [straight[3], crossed[3]], [6, 5], state)
    crossed[4], out_blocks[1], out_blocks[-3] = tie(crossed[4], out_blocks[1], out_blocks[-3])
    state = attend(low, queries, [straight[4], crossed[4]], [8, 7], state)

    a_block = state[None]
    a_pair = jnp.concatenate([a_block, shift(a_block, SIDE)], axis=0)
    out_blocks[2] = move(out_blocks[1], AHEAD)
    out_blocks[-4] = move(out_blocks[-3], BEHIND)
    a_up, a_down = shift(a_pair, UP), shift(a_pair, DOWN)
    a_up, a_down, out_blocks[2], out_blocks[-4] = tie(a_up, a_down, out_blocks[2], out_blocks[-4])
    out_blocks[3] = move(out_blocks[2], AHEAD)
    a_far = [shift(a_up[:1], UP), shift(a_down[1:], DOWN)]
    a_swaps = [shift(block, SWAP) for block in (a_pair, a_up, a_down, *a_far)]
    out_steps = steps[:7] + [-4]
    share, partial = output(
        [a_pair, a_up, a_down, *a_far, *a_swaps],
        [out_blocks[step] for step in out_steps],
        index_of(out_steps, z),
    )
    everywhere = jnp.broadcast_to(partial, (lax.axis_size("mp"), rows))
    square_total = jnp.sum(lax.all_to_all(everywhere, "mp", 0, 0, tiled=True), axis=0)
    post_scale = lax.rsqrt(square_total / D + EPSILON)
    post = share * post_scale[None, :] * (1.0 + post_gain.astype(F32))[:, None]
    layer_output = (tokens.T.astype(F32) + post).astype(BF).T

    pages = page_table.shape[0]
    local_slot = page_table - seq_index * pages
    kv_pages = kv.reshape(pages, PAGE, 2 * HD)
    caches = []
    for slot in range(pages):
        chosen = kv_pages[0]
        for page in range(1, pages):
            chosen = jnp.where(local_slot[page] == slot, kv_pages[page], chosen)
        caches.append(chosen)
    caches = jnp.stack(caches)
    return (layer_output, caches[:, :, :HD], caches[:, :, HD:])


def solution(mesh):
    return jax.shard_map(
        shards,
        mesh=mesh,
        in_specs=(
            P("seq", "mp"),
            P("mp"),
            P("mp"),
            P("seq", "mp"),
            P("seq", "mp"),
            P("seq", "mp"),
            P("mp", "seq"),
            P("seq"),
            P("seq"),
        ),
        out_specs=(P("seq", "mp"), P("seq", None, "mp"), P("seq", None, "mp")),
        check_vma=False,
    )
```

```python
import functools
import math

import jax
import jax.numpy as jnp
from jax import lax
from jax.experimental import pallas as pl
from jax.experimental.pallas import tpu as pltpu
from jax.sharding import PartitionSpec as P

D = 4608
HQ = 32
HD = 128
WINDOW = 4096
PAGE = 128
SEGS = 4

EPSILON = 1e-06
SOFT_CAP = 50.0
LOG2E = 1.4426950408889634
QUERY = float(D // HQ) ** (-0.5)
EXTRA = 16
SEQ = 16
ROUNDS = 8

BF = jnp.bfloat16
F32 = jnp.float32

AHEAD = [(i, (i + 2) % SEQ) for i in range(SEQ)]
BEHIND = [((i + 2) % SEQ, i) for i in range(SEQ)]
LATER = [(i, i + 2) for i in range(SEQ - 2)]
ACROSS = [(i, i ^ 1) for i in range(SEQ)]
SWAP = [(i, i ^ 1) for i in range(SEQ)]
COLUMNS = [[2 * i + c for i in range(ROUNDS)] for c in range(2)]

def move(block, perm):
    return lax.ppermute(block, "seq", perm)


def tie(*values):
    return lax.optimization_barrier(values)


def project_kernel(offsets, order_ref, cos_ref, sin_ref, x_hbm, *rest):
    w_refs = rest[:-7]
    kv_ref, q_ref, x_ref, w_ref, acc_ref, x_sem, w_sem = rest[-7:]
    chunks, depth, rows = x_ref.shape
    copies = []
    for k, (offset, source) in enumerate(zip(offsets, w_refs)):
        width = source.shape[1]
        for part in range(2):
            parity = order_ref[0] if part == 0 else 1 - order_ref[0]
            copies.append(
                pltpu.make_async_copy(
                    source.at[pl.ds(part * depth, depth)],
                    w_ref.at[2 * order_ref[1 + k] + parity, :, pl.ds(offset, width)],
                    w_sem.at[2 * k + part],
                )
            )
    step = chunks // 4
    for k in range(4):
        copies.append(
            pltpu.make_async_copy(
                x_hbm.at[pl.ds(k * step, step)], x_ref.at[pl.ds(k * step, step)], x_sem.at[k]
            )
        )
    for copy in copies:
        copy.start()
    for copy in copies[:-4]:
        copy.wait()
    squares = jnp.zeros((1, rows), F32)
    for k in range(4):
        copies[k - 4].wait()
        here = slice(k * step, (k + 1) * step)
        side = x_ref[here, depth - EXTRA :, :].astype(F32)
        squares = squares + jnp.sum(jnp.sum(side, axis=0), axis=0, keepdims=True)
        product = lax.dot_general(
            w_ref[here].reshape(step * depth, 4 * HD),
            x_ref[here].reshape(step * depth, rows),
            (((0,), (0,)), ((), ())),
            preferred_element_type=F32,
        )
        if k == 0:
            acc_ref[...] = product
        else:
            acc_ref[...] += product
    scale = lax.rsqrt(squares * (1.0 / D) + EPSILON)
    half = HD // 2
    cos, sin = cos_ref[...], sin_ref[...]
    for head, (ref, place, factor) in enumerate(
        ((kv_ref, 0, 1.0), (kv_ref, 1, None), (q_ref, 0, QUERY), (q_ref, 1, QUERY))
    ):
        start = head * HD
        if factor is None:
            value = acc_ref[start : start + HD, :] * scale
        else:
            first = acc_ref[start : start + half, :] * scale
            second = acc_ref[start + half : start + HD, :] * scale
            value = jnp.concatenate(
                [first * cos - second * sin, second * cos + first * sin], axis=0
            )
            if factor != 1.0:
                value = value * factor
        ref[:, place * HD : (place + 1) * HD] = jnp.transpose(value).astype(BF)


def project(x_all, blocks, order, cos, sin):
    chunks, depth, rows = x_all.shape
    vmem = pl.BlockSpec(memory_space=pltpu.VMEM)
    outside = pl.BlockSpec(memory_space=pl.ANY)
    out = jax.ShapeDtypeStruct((rows, 2 * HD), BF)
    return pl.pallas_call(
        functools.partial(project_kernel, tuple(offset for _, offset in blocks)),
        out_shape=(out, out),
        in_specs=[pl.BlockSpec(memory_space=pltpu.SMEM), vmem, vmem]
        + [outside] * (1 + len(blocks)),
        out_specs=(vmem, vmem),
        scratch_shapes=[
            pltpu.VMEM((chunks, depth, rows), BF),
            pltpu.VMEM((chunks, depth, 4 * HD), BF),
            pltpu.VMEM((4 * HD, rows), F32),
            pltpu.SemaphoreType.DMA((4,)),
            pltpu.SemaphoreType.DMA((2 * len(blocks),)),
        ],
        compiler_params=pltpu.CompilerParams(vmem_limit_bytes=60 << 20),
        cost_estimate=pl.CostEstimate(
            flops=2 * rows * 4 * HD * D, bytes_accessed=10 << 20, transcendentals=0
        ),
    )(order, cos, sin, x_all, *[block for block, _ in blocks])


def attend_kernel(distances, first, last, low_ref, q_ref, *rest):
    n = len(distances)
    kv_refs = rest[:n]
    rest = rest[n:]
    if not first:
        sum_in, den_in = rest[:2]
        rest = rest[2:]
    rows = q_ref.shape[0]
    tile = 256

    def part(index, carry):
        here = pl.ds(pl.multiple_of((index // 2) * tile, tile), tile)
        columns = pl.ds(pl.multiple_of(lax.rem(index, 2) * HD, HD), HD)
        q = q_ref[here, columns]
        low = low_ref[here, :]
        if first:
            total = jnp.zeros((tile, HD), F32)
            den = jnp.zeros((tile, HD), F32)
        else:
            total = sum_in[here, columns]
            den = den_in[here, columns]
        for kv_ref, distance in zip(kv_refs, distances):
            score = lax.dot_general(
                q, kv_ref[:, :HD], (((1,), (1,)), ((), ())), preferred_element_type=F32
            )
            weight = jnp.exp2(jnp.tanh(score * (1.0 / SOFT_CAP)) * (SOFT_CAP * LOG2E))
            place = lax.broadcasted_iota(jnp.int32, (tile, rows), 1)
            allowed = place >= low + distance * rows
            if distance == 0:
                own = lax.broadcasted_iota(jnp.int32, (tile, rows), 0) + (index // 2) * tile
                allowed = allowed & (place <= own)
            weight = jnp.where(allowed, weight, 0.0)
            for c in range(rows // HD):
                den = den + weight[:, c * HD : (c + 1) * HD]
            total = total + jnp.dot(
                weight.astype(BF), kv_ref[:, HD:], preferred_element_type=F32
            )
        if last:
            whole = jnp.sum(den, axis=1, keepdims=True)
            rest[0][here, columns] = (total / whole).astype(BF)
        else:
            rest[0][here, columns] = total
            rest[1][here, columns] = den
        return carry

    lax.fori_loop(0, 2 * (rows // tile), part, 0)


def attend(low, queries, kvs, distances, state):
    first = state is None
    last = 8 in distances
    rows = queries.shape[0]
    vmem = pl.BlockSpec(memory_space=pltpu.VMEM)
    n_in = 2 + len(kvs) + (0 if first else 2)
    part = jax.ShapeDtypeStruct((rows, 2 * HD), F32)
    elements = 2 * rows * rows * len(kvs)
    return pl.pallas_call(
        functools.partial(attend_kernel, tuple(distances), first, last),
        out_shape=jax.ShapeDtypeStruct((rows, 2 * HD), BF) if last else (part, part),
        in_specs=[vmem] * n_in,
        out_specs=vmem if last else (vmem, vmem),
        input_output_aliases={} if (first or last) else {n_in - 2: 0, n_in - 1: 1},
        compiler_params=pltpu.CompilerParams(vmem_limit_bytes=8 << 20),
        cost_estimate=pl.CostEstimate(
            flops=elements * 512, bytes_accessed=4 << 20, transcendentals=2 * elements
        ),
    )(low, queries, *kvs, *(() if first else state))


def terms_kernel(added, side_ref, a_ref, w_hbm, *rest):
    if added:
        in_ref, out_ref, w_ref, sem = rest
    else:
        out_ref, w_ref, sem = rest
    part = side_ref[0]
    copies = []
    for k in range(ROUNDS):
        copies.append(pltpu.make_async_copy(w_hbm.at[2 * k + part], w_ref.at[k], sem.at[k]))
    for copy in copies:
        copy.start()
    for k in range(ROUNDS):
        copies[k].wait()
        product = lax.dot_general(
            w_ref[k], a_ref[...], (((1,), (1,)), ((), ())), preferred_element_type=F32
        )
        if added:
            product = product + in_ref[k].astype(F32)
        out_ref[k] = product.astype(BF)


def terms(attended, weights, side, received):
    rows = attended.shape[0]
    _, features, width = weights.shape
    vmem = pl.BlockSpec(memory_space=pltpu.VMEM)
    added = received is not None
    return pl.pallas_call(
        functools.partial(terms_kernel, added),
        out_shape=jax.ShapeDtypeStruct((ROUNDS, features, rows), BF),
        in_specs=[
            pl.BlockSpec(memory_space=pltpu.SMEM),
            vmem,
            pl.BlockSpec(memory_space=pl.ANY),
        ]
        + [vmem] * added,
        out_specs=vmem,
        scratch_shapes=[
            pltpu.VMEM((ROUNDS, features, width), BF),
            pltpu.SemaphoreType.DMA((ROUNDS,)),
        ],
        compiler_params=pltpu.CompilerParams(vmem_limit_bytes=16 << 20),
        cost_estimate=pl.CostEstimate(
            flops=2 * rows * features * width * ROUNDS,
            bytes_accessed=6 << 20,
            transcendentals=0,
        ),
    )(side, attended, weights, *((received,) if added else ()))


def total_kernel(in_ref, out_ref, square_ref):
    total = in_ref[0].astype(F32)
    for k in range(1, ROUNDS):
        total = total + in_ref[k].astype(F32)
    out_ref[...] = total
    square_ref[...] = jnp.sum(total * total, axis=0, keepdims=True)


def total_of(parts):
    _, features, rows = parts.shape
    vmem = pl.BlockSpec(memory_space=pltpu.VMEM)
    return pl.pallas_call(
        total_kernel,
        out_shape=(
            jax.ShapeDtypeStruct((features, rows), F32),
            jax.ShapeDtypeStruct((1, rows), F32),
        ),
        in_specs=[vmem],
        out_specs=(vmem, vmem),
        compiler_params=pltpu.CompilerParams(vmem_limit_bytes=10 << 20),
        cost_estimate=pl.CostEstimate(flops=1 << 20, bytes_accessed=3 << 20, transcendentals=0),
    )(parts)


def shards(tokens, pre_gain, post_gain, w_query, w_key, w_value, w_out, segment_ids, page_table):
    rows = tokens.shape[0]
    features = tokens.shape[1]
    seq_index = lax.axis_index("seq")
    z = seq_index // 2
    h = lax.rem(seq_index, 2)
    base = seq_index * rows

    x_own = tokens.T.astype(F32)
    gained = (x_own * (1.0 + pre_gain.astype(F32))[:, None]).astype(BF)
    squares = jnp.sum(x_own * x_own, axis=0, keepdims=True)
    upper = lax.reduce_precision(squares, 8, 7)
    lower = squares - upper
    side = jnp.concatenate(
        [upper.astype(BF), lower.astype(BF), jnp.zeros((EXTRA - 2, rows), BF)], axis=0
    )
    x_all = lax.all_gather(jnp.concatenate([gained, side], axis=0), "mp", axis=0)
    depth = features + EXTRA

    lane = jnp.arange(4 * HD, dtype=jnp.int32)
    marked = 2 * (SEGS - 1)
    limit = jnp.where(lane < marked, lax.rem(lane, SEGS - 1) + 1, 0)
    counts = jnp.sum((segment_ids[:, None] < limit[None, :]).astype(F32), axis=0)
    upper_digit = jnp.floor(counts * (1.0 / 16.0))
    digits = jnp.where(lane < SEGS - 1, upper_digit, counts - 16.0 * upper_digit).astype(BF)
    digits = jnp.pad(digits[None, :], ((2, EXTRA - 3), (0, 0)))
    own = jnp.concatenate(
        [jnp.concatenate([w_key, w_value, w_query], axis=1), digits], axis=0
    )
    start = jnp.concatenate([own, move(own, ACROSS)], axis=0)
    ring = {0: start, 1: move(start, AHEAD), -1: move(start, BEHIND)}
    out_own = w_out.T
    out_facing = move(out_own, ACROSS)
    ring[2] = move(ring[1], AHEAD)
    ring[-2] = move(ring[-1], BEHIND)
    ring[2], ring[-2], out_facing = tie(ring[2], ring[-2], out_facing)
    out_all = lax.all_gather(
        jnp.concatenate([out_own, out_facing], axis=0)[None],
        "seq",
        axis=0,
        axis_index_groups=COLUMNS,
        tiled=True,
    )
    out_all = out_all.reshape(2 * ROUNDS, features, 2 * HD)
    ring[3] = move(ring[2], AHEAD)
    ring[-3] = move(ring[-2], BEHIND)
    last = move(ring[3][:, : 2 * HD], AHEAD)
    opposite = move(ring[-3][:, 2 * HD :], BEHIND)
    steps = [0, 1, -1, 2, -2, 3, -3, 4, 4]
    blocks = [(ring[step], 0) for step in steps[:7]] + [(last, 0), (opposite, 2 * HD)]
    places = [lax.rem(z - step + ROUNDS, ROUNDS) for step in steps]
    order = jnp.stack([h, *places]).astype(jnp.int32)
    parity = lax.rem(lax.axis_index("mp"), 2)

    n_marks = 2 * (SEGS - 1)
    marks = jnp.zeros((n_marks,), F32)
    for block, _ in blocks[:8]:
        for part in range(2):
            marks = marks + block[part * depth + features + 2, :n_marks].astype(F32)
    starts = (marks[: SEGS - 1] * 16.0 + marks[SEGS - 1 :]).astype(jnp.int32)
    global_index = base + jnp.arange(rows, dtype=jnp.int32)
    offsets = jnp.zeros((rows,), jnp.int32)
    for s in range(1, SEGS):
        offsets = jnp.where(segment_ids == s, starts[s - 1], offsets)
    within = (global_index - offsets).astype(F32)
    low = (jnp.maximum(offsets, global_index - (WINDOW - 1)) - base)[:, None]
    half = HD // 2
    freqs = jnp.exp(-math.log(10000.0) * jnp.arange(half, dtype=F32) * (2.0 / HD))
    angles = freqs[:, None] * within[None, :]
    cos = jnp.cos(angles)
    sin = jnp.sin(angles)

    kv, queries = project(x_all, blocks, order, cos, sin)

    straight, crossed, current = [kv], [None], kv
    state = attend(low, queries, [kv], [0], None)
    for step in range(4):
        following = move(current, LATER)
        chosen = jnp.where(h == 0, current, following)
        if step == 0:
            following, chosen = tie(following, chosen)
        else:
            following, chosen, crossed[step], *state = tie(
                following, chosen, crossed[step], *state
            )
            if step > 1:
                k = step - 1
                state = attend(low, queries, [straight[k], crossed[k]], [2 * k, 2 * k - 1], state)
        straight.append(following)
        crossed.append(move(chosen, ACROSS))
        current = following
    for k in range(3, 5):
        state = attend(low, queries, [straight[k], crossed[k]], [2 * k, 2 * k - 1], state)

    near = jnp.where(parity == h, 0, 1).astype(jnp.int32)[None]
    sent = lax.ppermute(terms(state, out_all, 1 - near, None), "mp", SWAP)
    mine = terms(state, out_all, near, sent)
    arrived = lax.all_to_all(mine, "mp", 0, 0, axis_index_groups=COLUMNS, tiled=True)
    share, partial = total_of(arrived)
    everywhere = jnp.broadcast_to(partial, (lax.axis_size("mp"), rows))
    square_total = jnp.sum(lax.all_to_all(everywhere, "mp", 0, 0, tiled=True), axis=0)
    post_scale = lax.rsqrt(square_total / D + EPSILON)
    post = share * post_scale[None, :] * (1.0 + post_gain.astype(F32))[:, None]
    layer_output = (tokens.T.astype(F32) + post).astype(BF).T

    pages = page_table.shape[0]
    local_slot = page_table - seq_index * pages
    kv_pages = kv.reshape(pages, PAGE, 2 * HD)
    caches = []
    for slot in range(pages):
        chosen = kv_pages[0]
        for page in range(1, pages):
            chosen = jnp.where(local_slot[page] == slot, kv_pages[page], chosen)
        caches.append(chosen)
    caches = jnp.stack(caches)
    return (layer_output, caches[:, :, :HD], caches[:, :, HD:])


def solution(mesh):
    return jax.shard_map(
        shards,
        mesh=mesh,
        in_specs=(
            P("seq", "mp"),
            P("mp"),
            P("mp"),
            P("seq", "mp"),
            P("seq", "mp"),
            P("seq", "mp"),
            P("mp", "seq"),
            P("seq"),
            P("seq"),
        ),
        out_specs=(P("seq", "mp"), P("seq", None, "mp"), P("seq", None, "mp")),
        check_vma=False,
    )
```

```python
import functools
import math

import jax
import jax.numpy as jnp
from jax import lax
from jax.experimental import pallas as pl
from jax.experimental.pallas import tpu as pltpu
from jax.sharding import PartitionSpec as P

D = 4608
HQ = 32
HD = 128
WINDOW = 4096
PAGE = 128
SEGS = 4

EPSILON = 1e-06
SOFT_CAP = 50.0
LOG2E = 1.4426950408889634
QUERY = float(D // HQ) ** (-0.5)
EXTRA = 16
SEQ = 16
ROUNDS = 8

BF = jnp.bfloat16
F32 = jnp.float32

AHEAD = [(i, (i + 2) % SEQ) for i in range(SEQ)]
BEHIND = [((i + 2) % SEQ, i) for i in range(SEQ)]
LATER = [(i, i + 2) for i in range(SEQ - 2)]
ACROSS = [(i, i ^ 1) for i in range(SEQ)]
TURNS = (
    [(s * SEQ + m, s * SEQ + (s + m) % SEQ) for s in range(SEQ) for m in range(SEQ)],
    [(s * SEQ + c, ((c - s) % SEQ) * SEQ + c) for s in range(SEQ) for c in range(SEQ)],
    [(m * SEQ + c, m * SEQ + (c - m) % SEQ) for m in range(SEQ) for c in range(SEQ)],
)


SIDE = [(i, i ^ 2) for i in range(SEQ)]
UP = [(i, (i + 4) % SEQ) for i in range(SEQ)]
DOWN = [((i + 4) % SEQ, i) for i in range(SEQ)]
SWAP = [(i, i ^ 1) for i in range(SEQ)]
COLUMNS = [[2 * i + c for i in range(ROUNDS)] for c in range(2)]

PLACES = (((0, 0), (0, 1)), ((-1, 0), (-1, 1)), ((1, 0), (1, 1)), ((2, 0),), ((2, 1),))


def move(block, perm):
    return lax.ppermute(block, "seq", perm)


def shift(block, perm):
    return lax.ppermute(block, "mp", perm)


def tie(*values):
    return lax.optimization_barrier(values)


def block_kernel(segment_ref, key_ref, value_ref, query_ref, out_ref):
    features = key_ref.shape[0]
    out_ref[:features, :HD] = key_ref[...]
    out_ref[:features, HD : 2 * HD] = value_ref[...]
    out_ref[:features, 2 * HD :] = query_ref[...]
    shape = (EXTRA, 4 * HD)
    lane = lax.broadcasted_iota(jnp.int32, shape, 1)
    digits = jnp.zeros(shape, F32)
    for s in range(1, SEGS):
        count = jnp.sum((segment_ref[...] < s).astype(F32), axis=1, keepdims=True)
        upper = jnp.floor(count * (1.0 / 16.0))
        digits = jnp.where(lane == s - 1, upper, digits)
        digits = jnp.where(lane == s + SEGS - 2, count - 16.0 * upper, digits)
    third = lax.broadcasted_iota(jnp.int32, shape, 0) == 2
    out_ref[features:, :] = jnp.where(third, digits, 0.0).astype(BF)


def weight_block(segments, w_key, w_value, w_query):
    vmem = pl.BlockSpec(memory_space=pltpu.VMEM)
    return pl.pallas_call(
        block_kernel,
        out_shape=jax.ShapeDtypeStruct((w_key.shape[0] + EXTRA, 4 * HD), BF),
        in_specs=[vmem] * 4,
        out_specs=vmem,
        compiler_params=pltpu.CompilerParams(vmem_limit_bytes=8 << 20),
        cost_estimate=pl.CostEstimate(flops=1 << 18, bytes_accessed=1 << 19, transcendentals=0),
    )(segments[None, :], w_key, w_value, w_query)


def load_weights(order_ref, offsets, w_refs, w_ref, sem, compact):
    copies = []
    for k, (offset, source) in enumerate(zip(offsets, w_refs)):
        depth = w_ref.shape[1]
        for part in range(2):
            parity = order_ref[0] if part == 0 else 1 - order_ref[0]
            place = 0 if compact else order_ref[1 + k]
            copies.append(
                pltpu.make_async_copy(
                    source.at[pl.ds(part * depth, depth)],
                    w_ref.at[2 * place + parity, :, pl.ds(offset, source.shape[1])],
                    sem.at[2 * k + part],
                )
            )
    return copies


def early_kernel(order_ref, x_hbm, *rest):
    w_refs = rest[:-6]
    acc_ref, square_ref, x_ref, w_ref, x_sem, w_sem = rest[-6:]
    chunks, depth, rows = x_ref.shape
    copies = load_weights(order_ref, (0,) * len(w_refs), w_refs, w_ref, w_sem, False)
    step = chunks // 4
    for k in range(4):
        copies.append(
            pltpu.make_async_copy(
                x_hbm.at[pl.ds(k * step, step)], x_ref.at[pl.ds(k * step, step)], x_sem.at[k]
            )
        )
    for copy in copies:
        copy.start()
    w_ref[pl.ds(2 * order_ref[1 + len(w_refs)], 2)] = jnp.zeros((2, depth, 4 * HD), BF)
    for copy in copies[:-4]:
        copy.wait()
    squares = jnp.zeros((1, rows), F32)
    for k in range(4):
        copies[k - 4].wait()
        here = slice(k * step, (k + 1) * step)
        side = x_ref[here, depth - EXTRA :, :].astype(F32)
        squares = squares + jnp.sum(jnp.sum(side, axis=0), axis=0, keepdims=True)
        product = lax.dot_general(
            w_ref[here].reshape(step * depth, 4 * HD),
            x_ref[here].reshape(step * depth, rows),
            (((0,), (0,)), ((), ())),
            preferred_element_type=F32,
        )
        if k == 0:
            acc_ref[...] = product
        else:
            acc_ref[...] += product
    square_ref[...] = squares


def late_kernel(offsets, order_ref, acc_ref, square_ref, cos_ref, sin_ref, x_hbm, *rest):
    w_refs = rest[:-6]
    kv_ref, q_ref, x_ref, w_ref, x_sem, w_sem = rest[-6:]
    _, depth, rows = x_ref.shape
    copies = load_weights(order_ref, offsets, w_refs, w_ref, w_sem, True)
    copies.append(
        pltpu.make_async_copy(x_hbm.at[pl.ds(2 * order_ref[ROUNDS], 2)], x_ref, x_sem)
    )
    for copy in copies:
        copy.start()
    for copy in copies:
        copy.wait()
    scale = lax.rsqrt(square_ref[...] * (1.0 / D) + EPSILON)
    half = HD // 2
    cos, sin = cos_ref[...], sin_ref[...]
    for head, (ref, place, factor) in enumerate(
        ((kv_ref, 0, 1.0), (kv_ref, 1, None), (q_ref, 0, QUERY), (q_ref, 1, QUERY))
    ):
        if head % 2 == 0:
            columns = slice(head * HD, (head + 2) * HD)
            product = acc_ref[columns, :] + lax.dot_general(
                w_ref[:, :, columns].reshape(2 * depth, 2 * HD),
                x_ref[...].reshape(2 * depth, rows),
                (((0,), (0,)), ((), ())),
                preferred_element_type=F32,
            )
        value = product[place * HD : (place + 1) * HD] * scale
        if factor is not None:
            first, second = value[:half], value[half:]
            value = jnp.concatenate(
                [first * cos - second * sin, second * cos + first * sin], axis=0
            )
            if factor != 1.0:
                value = value * factor
        ref[:, place * HD : (place + 1) * HD] = jnp.transpose(value).astype(BF)


def project_early(x_all, blocks, order):
    chunks, depth, rows = x_all.shape
    vmem = pl.BlockSpec(memory_space=pltpu.VMEM)
    outside = pl.BlockSpec(memory_space=pl.ANY)
    return pl.pallas_call(
        early_kernel,
        out_shape=(
            jax.ShapeDtypeStruct((4 * HD, rows), F32),
            jax.ShapeDtypeStruct((1, rows), F32),
        ),
        in_specs=[pl.BlockSpec(memory_space=pltpu.SMEM)] + [outside] * (1 + len(blocks)),
        out_specs=(vmem, vmem),
        scratch_shapes=[
            pltpu.VMEM((chunks, depth, rows), BF),
            pltpu.VMEM((chunks, depth, 4 * HD), BF),
            pltpu.SemaphoreType.DMA((4,)),
            pltpu.SemaphoreType.DMA((2 * len(blocks),)),
        ],
        compiler_params=pltpu.CompilerParams(vmem_limit_bytes=60 << 20),
        cost_estimate=pl.CostEstimate(
            flops=2 * rows * 4 * HD * D, bytes_accessed=10 << 20, transcendentals=0
        ),
    )(order, x_all, *blocks)


def project_late(partial, x_all, blocks, order, cos, sin):
    _, depth, rows = x_all.shape
    vmem = pl.BlockSpec(memory_space=pltpu.VMEM)
    outside = pl.BlockSpec(memory_space=pl.ANY)
    out = jax.ShapeDtypeStruct((rows, 2 * HD), BF)
    return pl.pallas_call(
        functools.partial(late_kernel, tuple(offset for _, offset in blocks)),
        out_shape=(out, out),
        in_specs=[pl.BlockSpec(memory_space=pltpu.SMEM)]
        + [vmem] * 4
        + [outside] * (1 + len(blocks)),
        out_specs=(vmem, vmem),
        scratch_shapes=[
            pltpu.VMEM((2, depth, rows), BF),
            pltpu.VMEM((2, depth, 4 * HD), BF),
            pltpu.SemaphoreType.DMA,
            pltpu.SemaphoreType.DMA((2 * len(blocks),)),
        ],
        compiler_params=pltpu.CompilerParams(vmem_limit_bytes=60 << 20),
        cost_estimate=pl.CostEstimate(
            flops=2 * rows * 4 * HD * D // 8, bytes_accessed=4 << 20, transcendentals=0
        ),
    )(order, *partial, cos, sin, x_all, *[block for block, _ in blocks])


def attend_kernel(distances, first, last, low_ref, q_ref, *rest):
    n = len(distances)
    kv_refs = rest[:n]
    rest = rest[n:]
    if not first:
        sum_in, den_in = rest[:2]
        rest = rest[2:]
    rows = q_ref.shape[0]
    tile = 256

    def part(index, carry):
        here = pl.ds(pl.multiple_of((index // 2) * tile, tile), tile)
        columns = pl.ds(pl.multiple_of(lax.rem(index, 2) * HD, HD), HD)
        q = q_ref[here, columns]
        low = low_ref[here, :]
        if first:
            total = jnp.zeros((tile, HD), F32)
            den = jnp.zeros((tile, HD), F32)
        else:
            total = sum_in[here, columns]
            den = den_in[here, columns]
        for kv_ref, distance in zip(kv_refs, distances):
            score = lax.dot_general(
                q, kv_ref[:, :HD], (((1,), (1,)), ((), ())), preferred_element_type=F32
            )
            weight = jnp.exp2(jnp.tanh(score * (1.0 / SOFT_CAP)) * (SOFT_CAP * LOG2E))
            place = lax.broadcasted_iota(jnp.int32, (tile, rows), 1)
            allowed = place >= low + distance * rows
            if distance == 0:
                own = lax.broadcasted_iota(jnp.int32, (tile, rows), 0) + (index // 2) * tile
                allowed = allowed & (place <= own)
            weight = jnp.where(allowed, weight, 0.0)
            for c in range(rows // HD):
                den = den + weight[:, c * HD : (c + 1) * HD]
            total = total + jnp.dot(
                weight.astype(BF), kv_ref[:, HD:], preferred_element_type=F32
            )
        if last:
            whole = jnp.sum(den, axis=1, keepdims=True)
            rest[0][here, columns] = (total / whole).astype(BF)
        else:
            rest[0][here, columns] = total
            rest[1][here, columns] = den
        return carry

    lax.fori_loop(0, 2 * (rows // tile), part, 0)


def attend(low, queries, kvs, distances, state):
    first = state is None
    last = 8 in distances
    rows = queries.shape[0]
    vmem = pl.BlockSpec(memory_space=pltpu.VMEM)
    n_in = 2 + len(kvs) + (0 if first else 2)
    part = jax.ShapeDtypeStruct((rows, 2 * HD), F32)
    elements = 2 * rows * rows * len(kvs)
    return pl.pallas_call(
        functools.partial(attend_kernel, tuple(distances), first, last),
        out_shape=jax.ShapeDtypeStruct((rows, 2 * HD), BF) if last else (part, part),
        in_specs=[vmem] * n_in,
        out_specs=vmem if last else (vmem, vmem),
        input_output_aliases={} if (first or last) else {n_in - 2: 0, n_in - 1: 1},
        compiler_params=pltpu.CompilerParams(vmem_limit_bytes=8 << 20),
        cost_estimate=pl.CostEstimate(
            flops=elements * 512, bytes_accessed=4 << 20, transcendentals=2 * elements
        ),
    )(low, queries, *kvs, *(() if first else state))


def output_kernel(index_ref, *rest):
    n = len(PLACES)
    same, other = rest[:n], rest[n : 2 * n]
    w_ref, out_ref, square_ref = rest[2 * n :]
    features = out_ref.shape[0]
    slot = 0
    for k, places in enumerate(PLACES):
        for j in range(len(places)):
            total = None
            place = index_ref[2 + slot]
            for part, ref in enumerate((same[k], other[k])):
                parity = index_ref[0] if part == 0 else 1 - index_ref[0]
                swapped = jnp.where(parity == index_ref[1], 0, 1)
                product = lax.dot_general(
                    w_ref[2 * place + swapped],
                    ref[j],
                    (((1,), (1,)), ((), ())),
                    preferred_element_type=F32,
                )
                total = product if total is None else total + product
            if slot == 0:
                out_ref[...] = total
            elif slot < ROUNDS - 1:
                out_ref[...] += total
            else:
                total = out_ref[...] + total
                out_ref[...] = total
                square_ref[...] = jnp.sum(total * total, axis=0, keepdims=True)
            slot += 1


def output(chunks, weights, index):
    rows = chunks[0].shape[1]
    features = weights.shape[1]
    vmem = pl.BlockSpec(memory_space=pltpu.VMEM)
    return pl.pallas_call(
        output_kernel,
        out_shape=(
            jax.ShapeDtypeStruct((features, rows), F32),
            jax.ShapeDtypeStruct((1, rows), F32),
        ),
        in_specs=[pl.BlockSpec(memory_space=pltpu.SMEM)] + [vmem] * (len(chunks) + 1),
        out_specs=(vmem, vmem),
        compiler_params=pltpu.CompilerParams(vmem_limit_bytes=10 << 20),
        cost_estimate=pl.CostEstimate(
            flops=2 * rows * features * 4096, bytes_accessed=8 << 20, transcendentals=0
        ),
    )(index, *chunks, weights)


def shards(tokens, pre_gain, post_gain, w_query, w_key, w_value, w_out, segment_ids, page_table):
    rows = tokens.shape[0]
    features = tokens.shape[1]
    seq_index = lax.axis_index("seq")
    z = seq_index // 2
    h = lax.rem(seq_index, 2)
    base = seq_index * rows

    own = weight_block(segment_ids, w_key, w_value, w_query)
    facing = move(own, ACROSS)
    x_own, own = tie(tokens.T, own)
    x_own = x_own.astype(F32)
    gained = (x_own * (1.0 + pre_gain.astype(F32))[:, None]).astype(BF)
    squares = jnp.sum(x_own * x_own, axis=0, keepdims=True)
    upper = lax.reduce_precision(squares, 8, 7)
    lower = squares - upper
    side = jnp.concatenate(
        [upper.astype(BF), lower.astype(BF), jnp.zeros((EXTRA - 2, rows), BF)], axis=0
    )
    x_all = lax.all_gather(jnp.concatenate([gained, side], axis=0), "mp", axis=0)
    depth = features + EXTRA

    start = jnp.concatenate([own, facing], axis=0)
    ring = {0: start, 1: move(start, AHEAD), -1: move(start, BEHIND)}
    turned = lax.ppermute(w_out.T, ("seq", "mp"), TURNS[0])
    ring[1], ring[-1], turned = tie(ring[1], ring[-1], turned)
    turned = lax.ppermute(turned, ("seq", "mp"), TURNS[1])
    ring[2] = move(ring[1], AHEAD)
    ring[-2] = move(ring[-1], BEHIND)
    ring[2], ring[-2], turned = tie(ring[2], ring[-2], turned)
    turned = lax.ppermute(turned, ("seq", "mp"), TURNS[2])
    ring[3] = move(ring[2], AHEAD)
    ring[-3] = move(ring[-2], BEHIND)
    ring[3], ring[-3], turned = tie(ring[3], ring[-3], turned)
    out_facing = move(turned, ACROSS)
    last = move(ring[3][:, : 2 * HD], AHEAD)
    opposite = move(ring[-3][:, 2 * HD :], BEHIND)
    steps = [0, 1, -1, 2, -2, 3, -3, 4, 4]
    blocks = [(ring[step], 0) for step in steps[:7]] + [(last, 0), (opposite, 2 * HD)]
    places = [lax.rem(z - step + ROUNDS, ROUNDS) for step in steps]
    order = jnp.stack([h, *places]).astype(jnp.int32)
    partial = project_early(x_all, [block for block, _ in blocks[:7]], order)
    last, opposite, out_facing, *partial = tie(last, opposite, out_facing, *partial)
    blocks[7:] = [(last, 0), (opposite, 2 * HD)]
    out_all = lax.all_gather(
        jnp.concatenate([turned, out_facing], axis=0),
        "seq",
        axis=0,
        axis_index_groups=COLUMNS,
    )

    mp_index = lax.axis_index("mp")
    y = mp_index // 4
    over = lax.rem(mp_index // 2, 2)
    placed = [
        2 * lax.rem(y + dy + 4, 4) + jnp.where(dx == 0, over, 1 - over)
        for pairs in PLACES
        for dy, dx in pairs
    ]
    index = jnp.stack([lax.rem(mp_index, 2), h, *placed]).astype(jnp.int32)

    n_marks = 2 * (SEGS - 1)
    marks = jnp.zeros((n_marks,), F32)
    for block, _ in blocks[:8]:
        for part in range(2):
            marks = marks + block[part * depth + features + 2, :n_marks].astype(F32)
    starts = (marks[: SEGS - 1] * 16.0 + marks[SEGS - 1 :]).astype(jnp.int32)
    global_index = base + jnp.arange(rows, dtype=jnp.int32)
    offsets = jnp.zeros((rows,), jnp.int32)
    for s in range(1, SEGS):
        offsets = jnp.where(segment_ids == s, starts[s - 1], offsets)
    within = (global_index - offsets).astype(F32)
    low = (jnp.maximum(offsets, global_index - (WINDOW - 1)) - base)[:, None]
    half = HD // 2
    freqs = jnp.exp(-math.log(10000.0) * jnp.arange(half, dtype=F32) * (2.0 / HD))
    angles = freqs[:, None] * within[None, :]
    cos = jnp.cos(angles)
    sin = jnp.sin(angles)

    kv, queries = project_late(partial, x_all, blocks[7:], order, cos, sin)

    straight, crossed, current = [kv], [None], kv
    state = attend(low, queries, [kv], [0], None)
    for step in range(4):
        following = move(current, LATER)
        chosen = jnp.where(h == 0, current, following)
        if step == 0:
            following, chosen = tie(following, chosen)
        else:
            following, chosen, crossed[step], *state = tie(
                following, chosen, crossed[step], *state
            )
            if step > 1:
                k = step - 1
                state = attend(low, queries, [straight[k], crossed[k]], [2 * k, 2 * k - 1], state)
        straight.append(following)
        crossed.append(move(chosen, ACROSS))
        current = following
    for k in range(3, 5):
        state = attend(low, queries, [straight[k], crossed[k]], [2 * k, 2 * k - 1], state)

    a_block = state[None]
    a_pair = jnp.concatenate([a_block, shift(a_block, SIDE)], axis=0)
    a_up, a_down = shift(a_pair, UP), shift(a_pair, DOWN)
    a_swaps = [shift(a_pair, SWAP)]
    a_up, a_down, out_all, a_swaps[0] = tie(a_up, a_down, out_all, a_swaps[0])
    a_far = [shift(a_up[:1], UP), shift(a_down[1:], DOWN)]
    a_swaps += [shift(a_up, SWAP), shift(a_down, SWAP)]
    a_far[0], a_far[1], a_swaps[1], a_swaps[2] = tie(*a_far, *a_swaps[1:])
    a_swaps += [shift(block, SWAP) for block in a_far]
    share, partial = output(
        [a_pair, a_up, a_down, *a_far, *a_swaps],
        out_all.reshape(2 * ROUNDS, features, 2 * HD),
        index,
    )
    everywhere = jnp.broadcast_to(partial, (lax.axis_size("mp"), rows))
    square_total = jnp.sum(lax.all_to_all(everywhere, "mp", 0, 0, tiled=True), axis=0)
    post_scale = lax.rsqrt(square_total / D + EPSILON)
    post = share * post_scale[None, :] * (1.0 + post_gain.astype(F32))[:, None]
    layer_output = (tokens.T.astype(F32) + post).astype(BF).T

    pages = page_table.shape[0]
    local_slot = page_table - seq_index * pages
    kv_pages = kv.reshape(pages, PAGE, 2 * HD)
    caches = []
    for slot in range(pages):
        chosen = kv_pages[0]
        for page in range(1, pages):
            chosen = jnp.where(local_slot[page] == slot, kv_pages[page], chosen)
        caches.append(chosen)
    caches = jnp.stack(caches)
    return (layer_output, caches[:, :, :HD], caches[:, :, HD:])


def solution(mesh):
    return jax.shard_map(
        shards,
        mesh=mesh,
        in_specs=(
            P("seq", "mp"),
            P("mp"),
            P("mp"),
            P("seq", "mp"),
            P("seq", "mp"),
            P("seq", "mp"),
            P("mp", "seq"),
            P("seq"),
            P("seq"),
        ),
        out_specs=(P("seq", "mp"), P("seq", None, "mp"), P("seq", None, "mp")),
        check_vma=False,
    )
```

```python
import functools
import math

import jax
import jax.numpy as jnp
from jax import lax
from jax.experimental import pallas as pl
from jax.experimental.pallas import tpu as pltpu
from jax.sharding import PartitionSpec as P

D = 4608
HQ = 32
HD = 128
WINDOW = 4096
PAGE = 128
SEGS = 4

EPSILON = 1e-06
SOFT_CAP = 50.0
LOG2E = 1.4426950408889634
EXTRA = 16
SEQ = 16
ROUNDS = 8

BF = jnp.bfloat16
F32 = jnp.float32

AHEAD = [(i, (i + 2) % SEQ) for i in range(SEQ)]
BEHIND = [((i + 2) % SEQ, i) for i in range(SEQ)]
LATER = [(i, i + 2) for i in range(SEQ - 2)]
ACROSS = [(i, i ^ 1) for i in range(SEQ)]
TURNS = (
    [(s * SEQ + m, s * SEQ + (s + m) % SEQ) for s in range(SEQ) for m in range(SEQ)],
    [(s * SEQ + c, ((c - s) % SEQ) * SEQ + c) for s in range(SEQ) for c in range(SEQ)],
    [(m * SEQ + c, m * SEQ + (c - m) % SEQ) for m in range(SEQ) for c in range(SEQ)],
)


SIDE = [(i, i ^ 2) for i in range(SEQ)]
UP = [(i, (i + 4) % SEQ) for i in range(SEQ)]
DOWN = [((i + 4) % SEQ, i) for i in range(SEQ)]
SWAP = [(i, i ^ 1) for i in range(SEQ)]
COLUMNS = [[2 * i + c for i in range(ROUNDS)] for c in range(2)]
PLACES = (((0, 0), (0, 1)), ((-1, 0), (-1, 1)), ((1, 0), (1, 1)), ((2, 0),), ((2, 1),))


def move(block, perm):
    return lax.ppermute(block, "seq", perm)


def shift(block, perm):
    return lax.ppermute(block, "mp", perm)


def tie(*values):
    return lax.optimization_barrier(values)


def project_kernel(pieces, rotated, factor, index_ref, cos_ref, sin_ref, x_hbm, *rest):
    w_refs = rest[:-6]
    out_ref, x_ref, w_ref, acc_ref, x_sem, w_sem = rest[-6:]
    chunks, depth, rows = x_ref.shape
    copies = []
    for slot in range(ROUNDS):
        place = index_ref[2 + ROUNDS + slot]
        for part in range(2):
            parity = index_ref[1] if part == 0 else 1 - index_ref[1]
            which, lead = pieces[slot]
            source = w_refs[which] if lead is None else w_refs[which].at[lead]
            copies.append(
                pltpu.make_async_copy(
                    source.at[pl.ds(part * depth, depth)],
                    w_ref.at[2 * place + parity],
                    w_sem.at[2 * slot + part],
                )
            )
    step = chunks // 4
    for k in range(4):
        copies.append(
            pltpu.make_async_copy(
                x_hbm.at[pl.ds(k * step, step)], x_ref.at[pl.ds(k * step, step)], x_sem.at[k]
            )
        )
    for copy in copies:
        copy.start()
    for copy in copies[:-4]:
        copy.wait()
    squares = jnp.zeros((1, rows), F32)
    for k in range(4):
        copies[k - 4].wait()
        here = slice(k * step, (k + 1) * step)
        side = x_ref[here, depth - EXTRA :, :].astype(F32)
        squares = squares + jnp.sum(jnp.sum(side, axis=0), axis=0, keepdims=True)
        product = lax.dot_general(
            w_ref[here].reshape(step * depth, 2 * HD),
            x_ref[here].reshape(step * depth, rows),
            (((0,), (0,)), ((), ())),
            preferred_element_type=F32,
        )
        if k == 0:
            acc_ref[...] = product
        else:
            acc_ref[...] += product
    scale = lax.rsqrt(squares * (1.0 / D) + EPSILON)
    half = HD // 2
    for head in range(2):
        start = head * HD
        if rotated[head]:
            first = acc_ref[start : start + half, :] * scale
            second = acc_ref[start + half : start + HD, :] * scale
            cos, sin = cos_ref[...], sin_ref[...]
            value = jnp.concatenate(
                [first * cos - second * sin, second * cos + first * sin], axis=0
            )
            if factor != 1.0:
                value = value * factor
        else:
            value = acc_ref[start : start + HD, :] * scale
        out_ref[:, start : start + HD] = jnp.transpose(value).astype(BF)


def project(x_all, weights, pieces, index, cos, sin, rotated, factor):
    chunks, depth, rows = x_all.shape
    vmem = pl.BlockSpec(memory_space=pltpu.VMEM)
    outside = pl.BlockSpec(memory_space=pl.ANY)
    return pl.pallas_call(
        functools.partial(project_kernel, pieces, rotated, factor),
        out_shape=jax.ShapeDtypeStruct((rows, 2 * HD), BF),
        in_specs=[pl.BlockSpec(memory_space=pltpu.SMEM), vmem, vmem]
        + [outside] * (1 + len(weights)),
        out_specs=vmem,
        scratch_shapes=[
            pltpu.VMEM((chunks, depth, rows), BF),
            pltpu.VMEM((chunks, depth, 2 * HD), BF),
            pltpu.VMEM((2 * HD, rows), F32),
            pltpu.SemaphoreType.DMA((4,)),
            pltpu.SemaphoreType.DMA((2 * ROUNDS,)),
        ],
        compiler_params=pltpu.CompilerParams(vmem_limit_bytes=60 << 20),
        cost_estimate=pl.CostEstimate(
            flops=2 * rows * 2 * HD * D, bytes_accessed=8 << 20, transcendentals=0
        ),
    )(index, cos, sin, x_all, *weights)


def attend_kernel(distances, first, last, low_ref, q_ref, *rest):
    n = len(distances)
    kv_refs = rest[:n]
    rest = rest[n:]
    if not first:
        sum_in, den_in = rest[:2]
        rest = rest[2:]
    rows = q_ref.shape[0]
    tile = 256

    def part(index, carry):
        here = pl.ds(pl.multiple_of((index // 2) * tile, tile), tile)
        columns = pl.ds(pl.multiple_of(lax.rem(index, 2) * HD, HD), HD)
        q = q_ref[here, columns]
        low = low_ref[here, :]
        if first:
            total = jnp.zeros((tile, HD), F32)
            den = jnp.zeros((tile, HD), F32)
        else:
            total = sum_in[here, columns]
            den = den_in[here, columns]
        for kv_ref, distance in zip(kv_refs, distances):
            score = lax.dot_general(
                q, kv_ref[:, :HD], (((1,), (1,)), ((), ())), preferred_element_type=F32
            )
            weight = jnp.exp2(jnp.tanh(score * (1.0 / SOFT_CAP)) * (SOFT_CAP * LOG2E))
            place = lax.broadcasted_iota(jnp.int32, (tile, rows), 1)
            allowed = place >= low + distance * rows
            if distance == 0:
                own = lax.broadcasted_iota(jnp.int32, (tile, rows), 0) + (index // 2) * tile
                allowed = allowed & (place <= own)
            weight = jnp.where(allowed, weight, 0.0)
            for c in range(rows // HD):
                den = den + weight[:, c * HD : (c + 1) * HD]
            total = total + jnp.dot(
                weight.astype(BF), kv_ref[:, HD:], preferred_element_type=F32
            )
        if last:
            whole = jnp.sum(den, axis=1, keepdims=True)
            rest[0][here, columns] = (total / whole).astype(BF)
        else:
            rest[0][here, columns] = total
            rest[1][here, columns] = den
        return carry

    lax.fori_loop(0, 2 * (rows // tile), part, 0)


def attend(low, queries, kvs, distances, state):
    first = state is None
    last = 8 in distances
    rows = queries.shape[0]
    vmem = pl.BlockSpec(memory_space=pltpu.VMEM)
    n_in = 2 + len(kvs) + (0 if first else 2)
    part = jax.ShapeDtypeStruct((rows, 2 * HD), F32)
    elements = 2 * rows * rows * len(kvs)
    return pl.pallas_call(
        functools.partial(attend_kernel, tuple(distances), first, last),
        out_shape=jax.ShapeDtypeStruct((rows, 2 * HD), BF) if last else (part, part),
        in_specs=[vmem] * n_in,
        out_specs=vmem if last else (vmem, vmem),
        input_output_aliases={} if (first or last) else {n_in - 2: 0, n_in - 1: 1},
        compiler_params=pltpu.CompilerParams(vmem_limit_bytes=8 << 20),
        cost_estimate=pl.CostEstimate(
            flops=elements * 512, bytes_accessed=4 << 20, transcendentals=2 * elements
        ),
    )(low, queries, *kvs, *(() if first else state))


def output_kernel(index_ref, *rest):
    n = len(PLACES)
    same, other = rest[:n], rest[n : 2 * n]
    w_ref, out_ref, square_ref = rest[2 * n :]
    features = out_ref.shape[0]
    slot = 0
    for k, places in enumerate(PLACES):
        for j in range(len(places)):
            total = None
            place = index_ref[2 + slot]
            for part, ref in enumerate((same[k], other[k])):
                parity = index_ref[0] if part == 0 else 1 - index_ref[0]
                swapped = jnp.where(parity == index_ref[1], 0, 1)
                product = lax.dot_general(
                    w_ref[2 * place + swapped],
                    ref[j],
                    (((1,), (1,)), ((), ())),
                    preferred_element_type=F32,
                )
                total = product if total is None else total + product
            if slot == 0:
                out_ref[...] = total
            elif slot < ROUNDS - 1:
                out_ref[...] += total
            else:
                total = out_ref[...] + total
                out_ref[...] = total
                square_ref[...] = jnp.sum(total * total, axis=0, keepdims=True)
            slot += 1


def output(chunks, weights, index):
    rows = chunks[0].shape[1]
    features = weights.shape[1]
    vmem = pl.BlockSpec(memory_space=pltpu.VMEM)
    return pl.pallas_call(
        output_kernel,
        out_shape=(
            jax.ShapeDtypeStruct((features, rows), F32),
            jax.ShapeDtypeStruct((1, rows), F32),
        ),
        in_specs=[pl.BlockSpec(memory_space=pltpu.SMEM)] + [vmem] * (len(chunks) + 1),
        out_specs=(vmem, vmem),
        compiler_params=pltpu.CompilerParams(vmem_limit_bytes=10 << 20),
        cost_estimate=pl.CostEstimate(
            flops=2 * rows * features * 4096, bytes_accessed=8 << 20, transcendentals=0
        ),
    )(index, *chunks, weights)


def shards(tokens, pre_gain, post_gain, w_query, w_key, w_value, w_out, segment_ids, page_table):
    rows = tokens.shape[0]
    features = tokens.shape[1]
    seq_index = lax.axis_index("seq")
    z = seq_index // 2
    h = lax.rem(seq_index, 2)
    base = seq_index * rows

    x_own = tokens.T.astype(F32)
    gained = (x_own * (1.0 + pre_gain.astype(F32))[:, None]).astype(BF)
    squares = jnp.sum(x_own * x_own, axis=0, keepdims=True)
    upper = lax.reduce_precision(squares, 8, 7)
    lower = squares - upper
    side = jnp.concatenate(
        [upper.astype(BF), lower.astype(BF), jnp.zeros((EXTRA - 2, rows), BF)], axis=0
    )
    x_all = lax.all_gather(jnp.concatenate([gained, side], axis=0), "mp", axis=0)
    depth = features + EXTRA

    lane = jnp.arange(2 * HD, dtype=jnp.int32)
    marked = 2 * (SEGS - 1)
    limit = jnp.where(lane < marked, lax.rem(lane, SEGS - 1) + 1, 0)
    counts = jnp.sum((segment_ids[:, None] < limit[None, :]).astype(F32), axis=0)
    upper_digit = jnp.floor(counts * (1.0 / 16.0))
    digits = jnp.where(lane < SEGS - 1, upper_digit, counts - 16.0 * upper_digit).astype(BF)
    digits = jnp.pad(digits[None, :], ((2, EXTRA - 3), (0, 0)))
    kv_own = jnp.concatenate([jnp.concatenate([w_key, w_value], axis=1), digits], axis=0)
    start = jnp.concatenate([kv_own, move(kv_own, ACROSS)], axis=0)
    ring = {0: start, 1: move(start, AHEAD), -1: move(start, BEHIND)}
    turned = lax.ppermute(w_out.T, ("seq", "mp"), TURNS[0])
    ring[2] = move(ring[1], AHEAD)
    ring[-2] = move(ring[-1], BEHIND)
    ring[2], ring[-2], turned = tie(ring[2], ring[-2], turned)
    q_own = jnp.pad(w_query, ((0, EXTRA), (0, 0)))
    q_own, _ = tie(q_own, ring[1])
    q_pair = jnp.concatenate([q_own, move(q_own, ACROSS)], axis=0)
    turned = lax.ppermute(turned, ("seq", "mp"), TURNS[1])
    ring[3] = move(ring[2], AHEAD)
    ring[-3] = move(ring[-2], BEHIND)
    ring[3], ring[-3], turned, q_pair = tie(ring[3], ring[-3], turned, q_pair)
    q_all = lax.all_gather(q_pair, "seq", axis=0, axis_index_groups=COLUMNS)
    turned = lax.ppermute(turned, ("seq", "mp"), TURNS[2])
    last = move(ring[3][:, :HD], AHEAD)
    ring[4] = jnp.concatenate([last, move(ring[-3][:, HD:], BEHIND)], axis=1)
    ring[4], turned = tie(ring[4], turned)

    mp_index = lax.axis_index("mp")
    y = mp_index // 4
    over = lax.rem(mp_index // 2, 2)
    placed = [
        2 * lax.rem(y + dy + 4, 4) + jnp.where(dx == 0, over, 1 - over)
        for places in PLACES
        for dy, dx in places
    ]

    def index_of(steps, origin):
        places = [lax.rem(jnp.int32(origin - step + ROUNDS), ROUNDS) for step in steps]
        return jnp.stack([lax.rem(mp_index, 2), h, *placed, *places]).astype(jnp.int32)

    steps = [0, 1, -1, 2, -2, 3, -3, 4]
    index = index_of(steps, z)
    kv_weights = [ring[step] for step in steps]
    kv_pieces = tuple((k, None) for k in range(ROUNDS))
    q_pieces = tuple((0, k) for k in range(ROUNDS))

    n_marks = 2 * (SEGS - 1)
    marks = jnp.zeros((n_marks,), F32)
    for block in kv_weights:
        for part in range(2):
            marks = marks + block[part * depth + features + 2, :n_marks].astype(F32)
    starts = (marks[: SEGS - 1] * 16.0 + marks[SEGS - 1 :]).astype(jnp.int32)
    global_index = base + jnp.arange(rows, dtype=jnp.int32)
    offsets = jnp.zeros((rows,), jnp.int32)
    for s in range(1, SEGS):
        offsets = jnp.where(segment_ids == s, starts[s - 1], offsets)
    within = (global_index - offsets).astype(F32)
    low = (jnp.maximum(offsets, global_index - (WINDOW - 1)) - base)[:, None]
    half = HD // 2
    freqs = jnp.exp(-math.log(10000.0) * jnp.arange(half, dtype=F32) * (2.0 / HD))
    angles = freqs[:, None] * within[None, :]
    cos = jnp.cos(angles)
    sin = jnp.sin(angles)

    kv = project(x_all, kv_weights, kv_pieces, index, cos, sin, (True, False), 1.0)

    straight, crossed, current, state = [kv], [None], kv, None
    for step in range(4):
        following = move(current, LATER)
        chosen = jnp.where(h == 0, current, following)
        if step == 0:
            following, chosen = tie(following, chosen)
        elif step == 1:
            following, chosen, crossed[1], q_all = tie(following, chosen, crossed[1], q_all)
            queries = project(
                x_all,
                [q_all],
                q_pieces,
                index_of([-k for k in range(ROUNDS)], 0),
                cos,
                sin,
                (True, True),
                float(D // HQ) ** (-0.5),
            )
            state = attend(low, queries, [kv], [0], None)
        else:
            if step == 2:
                facing_out = move(turned, ACROSS)
                following, chosen, crossed[2], facing_out, *state = tie(
                    following, chosen, crossed[2], facing_out, *state
                )
            else:
                following, chosen, crossed[3], *state = tie(
                    following, chosen, crossed[3], *state
                )
            k = step - 1
            state = attend(low, queries, [straight[k], crossed[k]], [2 * k, 2 * k - 1], state)
        straight.append(following)
        crossed.append(move(chosen, ACROSS))
        current = following
    out_pair, straight[4] = tie(jnp.concatenate([turned, facing_out], axis=0), straight[4])
    out_all = lax.all_gather(out_pair, "seq", axis=0, axis_index_groups=COLUMNS)
    for k in range(3, 5):
        state = attend(low, queries, [straight[k], crossed[k]], [2 * k, 2 * k - 1], state)

    a_block = state[None]
    a_pair = jnp.concatenate([a_block, shift(a_block, SIDE)], axis=0)
    a_up, a_down = shift(a_pair, UP), shift(a_pair, DOWN)
    a_swaps = [shift(a_pair, SWAP)]
    a_up, a_down, a_swaps[0] = tie(a_up, a_down, a_swaps[0])
    a_far = [shift(a_up[:1], UP), shift(a_down[1:], DOWN)]
    a_swaps += [shift(a_up, SWAP), shift(a_down, SWAP)]
    a_far[0], a_far[1], a_swaps[1], a_swaps[2] = tie(*a_far, *a_swaps[1:])
    a_swaps += [shift(block, SWAP) for block in a_far]
    share, partial = output(
        [a_pair, a_up, a_down, *a_far, *a_swaps],
        out_all.reshape(2 * ROUNDS, features, 2 * HD),
        index,
    )
    everywhere = jnp.broadcast_to(partial, (lax.axis_size("mp"), rows))
    square_total = jnp.sum(lax.all_to_all(everywhere, "mp", 0, 0, tiled=True), axis=0)
    post_scale = lax.rsqrt(square_total / D + EPSILON)
    post = share * post_scale[None, :] * (1.0 + post_gain.astype(F32))[:, None]
    layer_output = (tokens.T.astype(F32) + post).astype(BF).T

    pages = page_table.shape[0]
    local_slot = page_table - seq_index * pages
    kv_pages = kv.reshape(pages, PAGE, 2 * HD)
    caches = []
    for slot in range(pages):
        chosen = kv_pages[0]
        for page in range(1, pages):
            chosen = jnp.where(local_slot[page] == slot, kv_pages[page], chosen)
        caches.append(chosen)
    caches = jnp.stack(caches)
    return (layer_output, caches[:, :, :HD], caches[:, :, HD:])


def solution(mesh):
    return jax.shard_map(
        shards,
        mesh=mesh,
        in_specs=(
            P("seq", "mp"),
            P("mp"),
            P("mp"),
            P("seq", "mp"),
            P("seq", "mp"),
            P("seq", "mp"),
            P("mp", "seq"),
            P("seq"),
            P("seq"),
        ),
        out_specs=(P("seq", "mp"), P("seq", None, "mp"), P("seq", None, "mp")),
        check_vma=False,
    )
```

```python
import functools
import math

import jax
import jax.numpy as jnp
from jax import lax
from jax.experimental import pallas as pl
from jax.experimental.pallas import tpu as pltpu
from jax.sharding import PartitionSpec as P

D = 4608
HQ = 32
HD = 128
WINDOW = 4096
PAGE = 128
SEGS = 4

EPSILON = 1e-06
SOFT_CAP = 50.0
LOG2E = 1.4426950408889634
EXTRA = 16
SEQ = 16
ROUNDS = 8

BF = jnp.bfloat16
F32 = jnp.float32

AHEAD = [(i, (i + 2) % SEQ) for i in range(SEQ)]
BEHIND = [((i + 2) % SEQ, i) for i in range(SEQ)]
LATER = [(i, i + 2) for i in range(SEQ - 2)]
ACROSS = [(i, i ^ 1) for i in range(SEQ)]
TURNS = (
    [(s * SEQ + m, s * SEQ + (s + m) % SEQ) for s in range(SEQ) for m in range(SEQ)],
    [(s * SEQ + c, ((c - s) % SEQ) * SEQ + c) for s in range(SEQ) for c in range(SEQ)],
    [(m * SEQ + c, m * SEQ + (c - m) % SEQ) for m in range(SEQ) for c in range(SEQ)],
)


SIDE = [(i, i ^ 2) for i in range(SEQ)]
UP = [(i, (i + 4) % SEQ) for i in range(SEQ)]
DOWN = [((i + 4) % SEQ, i) for i in range(SEQ)]
SWAP = [(i, i ^ 1) for i in range(SEQ)]
COLUMNS = [[2 * i + c for i in range(ROUNDS)] for c in range(2)]
PLACES = (((0, 0), (0, 1)), ((-1, 0), (-1, 1)), ((1, 0), (1, 1)), ((2, 0),), ((2, 1),))


def move(block, perm):
    return lax.ppermute(block, "seq", perm)


def shift(block, perm):
    return lax.ppermute(block, "mp", perm)


def tie(*values):
    return lax.optimization_barrier(values)


def project_kernel(pieces, rotated, factor, index_ref, cos_ref, sin_ref, x_hbm, *rest):
    w_refs = rest[:-6]
    out_ref, x_ref, w_ref, acc_ref, x_sem, w_sem = rest[-6:]
    chunks, depth, rows = x_ref.shape
    copies = []
    for k, (which, lead, slot, offset) in enumerate(pieces):
        place = index_ref[2 + ROUNDS + slot]
        source = w_refs[which] if lead is None else w_refs[which].at[lead]
        width = source.shape[1]
        for part in range(2):
            parity = index_ref[1] if part == 0 else 1 - index_ref[1]
            copies.append(
                pltpu.make_async_copy(
                    source.at[pl.ds(part * depth, depth)],
                    w_ref.at[2 * place + parity, :, pl.ds(offset, width)],
                    w_sem.at[2 * k + part],
                )
            )
    step = chunks // 4
    for k in range(4):
        copies.append(
            pltpu.make_async_copy(
                x_hbm.at[pl.ds(k * step, step)], x_ref.at[pl.ds(k * step, step)], x_sem.at[k]
            )
        )
    for copy in copies:
        copy.start()
    for copy in copies[:-4]:
        copy.wait()
    squares = jnp.zeros((1, rows), F32)
    for k in range(4):
        copies[k - 4].wait()
        here = slice(k * step, (k + 1) * step)
        side = x_ref[here, depth - EXTRA :, :].astype(F32)
        squares = squares + jnp.sum(jnp.sum(side, axis=0), axis=0, keepdims=True)
        product = lax.dot_general(
            w_ref[here].reshape(step * depth, 2 * HD),
            x_ref[here].reshape(step * depth, rows),
            (((0,), (0,)), ((), ())),
            preferred_element_type=F32,
        )
        if k == 0:
            acc_ref[...] = product
        else:
            acc_ref[...] += product
    scale = lax.rsqrt(squares * (1.0 / D) + EPSILON)
    half = HD // 2
    for head in range(2):
        start = head * HD
        if rotated[head]:
            first = acc_ref[start : start + half, :] * scale
            second = acc_ref[start + half : start + HD, :] * scale
            cos, sin = cos_ref[...], sin_ref[...]
            value = jnp.concatenate(
                [first * cos - second * sin, second * cos + first * sin], axis=0
            )
            if factor != 1.0:
                value = value * factor
        else:
            value = acc_ref[start : start + HD, :] * scale
        out_ref[:, start : start + HD] = jnp.transpose(value).astype(BF)


def project(x_all, weights, pieces, index, cos, sin, rotated, factor):
    chunks, depth, rows = x_all.shape
    vmem = pl.BlockSpec(memory_space=pltpu.VMEM)
    outside = pl.BlockSpec(memory_space=pl.ANY)
    return pl.pallas_call(
        functools.partial(project_kernel, pieces, rotated, factor),
        out_shape=jax.ShapeDtypeStruct((rows, 2 * HD), BF),
        in_specs=[pl.BlockSpec(memory_space=pltpu.SMEM), vmem, vmem]
        + [outside] * (1 + len(weights)),
        out_specs=vmem,
        scratch_shapes=[
            pltpu.VMEM((chunks, depth, rows), BF),
            pltpu.VMEM((chunks, depth, 2 * HD), BF),
            pltpu.VMEM((2 * HD, rows), F32),
            pltpu.SemaphoreType.DMA((4,)),
            pltpu.SemaphoreType.DMA((2 * len(pieces),)),
        ],
        compiler_params=pltpu.CompilerParams(vmem_limit_bytes=60 << 20),
        cost_estimate=pl.CostEstimate(
            flops=2 * rows * 2 * HD * D, bytes_accessed=8 << 20, transcendentals=0
        ),
    )(index, cos, sin, x_all, *weights)


def attend_kernel(distances, first, last, low_ref, q_ref, *rest):
    n = len(distances)
    kv_refs = rest[:n]
    rest = rest[n:]
    if not first:
        sum_in, den_in = rest[:2]
        rest = rest[2:]
    rows = q_ref.shape[0]
    tile = 256

    def part(index, carry):
        here = pl.ds(pl.multiple_of((index // 2) * tile, tile), tile)
        columns = pl.ds(pl.multiple_of(lax.rem(index, 2) * HD, HD), HD)
        q = q_ref[here, columns]
        low = low_ref[here, :]
        if first:
            total = jnp.zeros((tile, HD), F32)
            den = jnp.zeros((tile, HD), F32)
        else:
            total = sum_in[here, columns]
            den = den_in[here, columns]
        for kv_ref, distance in zip(kv_refs, distances):
            score = lax.dot_general(
                q, kv_ref[:, :HD], (((1,), (1,)), ((), ())), preferred_element_type=F32
            )
            weight = jnp.exp2(jnp.tanh(score * (1.0 / SOFT_CAP)) * (SOFT_CAP * LOG2E))
            place = lax.broadcasted_iota(jnp.int32, (tile, rows), 1)
            allowed = place >= low + distance * rows
            if distance == 0:
                own = lax.broadcasted_iota(jnp.int32, (tile, rows), 0) + (index // 2) * tile
                allowed = allowed & (place <= own)
            weight = jnp.where(allowed, weight, 0.0)
            for c in range(rows // HD):
                den = den + weight[:, c * HD : (c + 1) * HD]
            total = total + jnp.dot(
                weight.astype(BF), kv_ref[:, HD:], preferred_element_type=F32
            )
        if last:
            whole = jnp.sum(den, axis=1, keepdims=True)
            rest[0][here, columns] = (total / whole).astype(BF)
        else:
            rest[0][here, columns] = total
            rest[1][here, columns] = den
        return carry

    lax.fori_loop(0, 2 * (rows // tile), part, 0)


def attend(low, queries, kvs, distances, state):
    first = state is None
    last = 8 in distances
    rows = queries.shape[0]
    vmem = pl.BlockSpec(memory_space=pltpu.VMEM)
    n_in = 2 + len(kvs) + (0 if first else 2)
    part = jax.ShapeDtypeStruct((rows, 2 * HD), F32)
    elements = 2 * rows * rows * len(kvs)
    return pl.pallas_call(
        functools.partial(attend_kernel, tuple(distances), first, last),
        out_shape=jax.ShapeDtypeStruct((rows, 2 * HD), BF) if last else (part, part),
        in_specs=[vmem] * n_in,
        out_specs=vmem if last else (vmem, vmem),
        input_output_aliases={} if (first or last) else {n_in - 2: 0, n_in - 1: 1},
        compiler_params=pltpu.CompilerParams(vmem_limit_bytes=8 << 20),
        cost_estimate=pl.CostEstimate(
            flops=elements * 512, bytes_accessed=4 << 20, transcendentals=2 * elements
        ),
    )(low, queries, *kvs, *(() if first else state))


def output_kernel(index_ref, *rest):
    n = len(PLACES)
    sources, w_hbm = rest[: 2 * n], rest[2 * n]
    out_ref, square_ref, x_ref, w_ref, x_sem, w_sem = rest[2 * n + 1 :]
    load = pltpu.make_async_copy(w_hbm, w_ref, w_sem)
    load.start()
    copies = []
    for k, places in enumerate(PLACES):
        slot = sum(len(before) for before in PLACES[:k])
        copies.append(
            [
                pltpu.make_async_copy(
                    sources[part * n + k],
                    x_ref.at[part, pl.ds(slot, len(places))],
                    x_sem.at[part * n + k],
                )
                for part in range(2)
            ]
        )
    for both in copies:
        for copy in both:
            copy.start()
    load.wait()
    slot = 0
    for k, places in enumerate(PLACES):
        for copy in copies[k]:
            copy.wait()
        for _ in places:
            total = None
            place = index_ref[2 + slot]
            for part in range(2):
                parity = index_ref[0] if part == 0 else 1 - index_ref[0]
                swapped = jnp.where(parity == index_ref[1], 0, 1)
                product = lax.dot_general(
                    w_ref[2 * place + swapped],
                    x_ref[part, slot],
                    (((1,), (1,)), ((), ())),
                    preferred_element_type=F32,
                )
                total = product if total is None else total + product
            if slot == 0:
                out_ref[...] = total
            elif slot < ROUNDS - 1:
                out_ref[...] += total
            else:
                total = out_ref[...] + total
                out_ref[...] = total
                square_ref[...] = jnp.sum(total * total, axis=0, keepdims=True)
            slot += 1


def output(chunks, weights, index):
    _, rows, width = chunks[0].shape
    features = weights.shape[1]
    vmem = pl.BlockSpec(memory_space=pltpu.VMEM)
    outside = pl.BlockSpec(memory_space=pl.ANY)
    return pl.pallas_call(
        output_kernel,
        out_shape=(
            jax.ShapeDtypeStruct((features, rows), F32),
            jax.ShapeDtypeStruct((1, rows), F32),
        ),
        in_specs=[pl.BlockSpec(memory_space=pltpu.SMEM)] + [outside] * (len(chunks) + 1),
        out_specs=(vmem, vmem),
        scratch_shapes=[
            pltpu.VMEM((2, ROUNDS, rows, width), BF),
            pltpu.VMEM(weights.shape, BF),
            pltpu.SemaphoreType.DMA((2 * len(PLACES),)),
            pltpu.SemaphoreType.DMA,
        ],
        compiler_params=pltpu.CompilerParams(vmem_limit_bytes=60 << 20),
        cost_estimate=pl.CostEstimate(
            flops=2 * rows * features * 4096, bytes_accessed=8 << 20, transcendentals=0
        ),
    )(index, *chunks, weights)


def shards(tokens, pre_gain, post_gain, w_query, w_key, w_value, w_out, segment_ids, page_table):
    rows = tokens.shape[0]
    features = tokens.shape[1]
    seq_index = lax.axis_index("seq")
    z = seq_index // 2
    h = lax.rem(seq_index, 2)
    base = seq_index * rows

    depth = features + EXTRA
    lane = jnp.arange(2 * HD, dtype=jnp.int32)
    marked = 2 * (SEGS - 1)
    limit = jnp.where(lane < marked, lax.rem(lane, SEGS - 1) + 1, 0)
    counts = jnp.sum((segment_ids[:, None] < limit[None, :]).astype(F32), axis=0)
    upper_digit = jnp.floor(counts * (1.0 / 16.0))
    digits = jnp.where(lane < SEGS - 1, upper_digit, counts - 16.0 * upper_digit).astype(BF)
    digits = jnp.pad(digits[None, :], ((2, EXTRA - 3), (0, 0)))
    kv_own = jnp.concatenate([jnp.concatenate([w_key, w_value], axis=1), digits], axis=0)
    q_own = jnp.pad(w_query, ((0, EXTRA), (0, 0)))
    facing, q_facing = tie(move(kv_own, ACROSS), move(q_own, ACROSS))
    x_own, kv_own = tie(tokens.T, kv_own)
    x_own = x_own.astype(F32)
    gained = (x_own * (1.0 + pre_gain.astype(F32))[:, None]).astype(BF)
    squares = jnp.sum(x_own * x_own, axis=0, keepdims=True)
    upper = lax.reduce_precision(squares, 8, 7)
    lower = squares - upper
    side = jnp.concatenate(
        [upper.astype(BF), lower.astype(BF), jnp.zeros((EXTRA - 2, rows), BF)], axis=0
    )
    x_all = lax.all_gather(jnp.concatenate([gained, side], axis=0), "mp", axis=0)
    start = jnp.concatenate([kv_own, facing], axis=0)
    ring = {0: start, 1: move(start, AHEAD), -1: move(start, BEHIND)}
    turned = lax.ppermute(w_out.T, ("seq", "mp"), TURNS[0])
    ring[2] = move(ring[1], AHEAD)
    ring[-2] = move(ring[-1], BEHIND)
    ring[2], ring[-2], turned = tie(ring[2], ring[-2], turned)
    q_pair = jnp.concatenate([q_own, q_facing], axis=0)
    turned = lax.ppermute(turned, ("seq", "mp"), TURNS[1])
    ring[3] = move(ring[2], AHEAD)
    ring[-3] = move(ring[-2], BEHIND)
    ring[3], ring[-3], turned = tie(ring[3], ring[-3], turned)
    q_all = lax.all_gather(q_pair, "seq", axis=0, axis_index_groups=COLUMNS)
    turned = lax.ppermute(turned, ("seq", "mp"), TURNS[2])
    last = move(ring[3][:, :HD], AHEAD)
    opposite = move(ring[-3][:, HD:], BEHIND)
    last, opposite, turned = tie(last, opposite, turned)

    mp_index = lax.axis_index("mp")
    y = mp_index // 4
    over = lax.rem(mp_index // 2, 2)
    placed = [
        2 * lax.rem(y + dy + 4, 4) + jnp.where(dx == 0, over, 1 - over)
        for places in PLACES
        for dy, dx in places
    ]

    def index_of(steps, origin):
        places = [lax.rem(jnp.int32(origin - step + ROUNDS), ROUNDS) for step in steps]
        return jnp.stack([lax.rem(mp_index, 2), h, *placed, *places]).astype(jnp.int32)

    steps = [0, 1, -1, 2, -2, 3, -3, 4]
    index = index_of(steps, z)
    kv_weights = [ring[step] for step in steps[:7]] + [last, opposite]
    kv_pieces = tuple((k, None, k, 0) for k in range(ROUNDS)) + ((8, None, 7, HD),)
    q_pieces = tuple((0, k, k, 0) for k in range(ROUNDS))

    n_marks = 2 * (SEGS - 1)
    marks = jnp.zeros((n_marks,), F32)
    for block in kv_weights[:8]:
        for part in range(2):
            marks = marks + block[part * depth + features + 2, :n_marks].astype(F32)
    starts = (marks[: SEGS - 1] * 16.0 + marks[SEGS - 1 :]).astype(jnp.int32)
    global_index = base + jnp.arange(rows, dtype=jnp.int32)
    offsets = jnp.zeros((rows,), jnp.int32)
    for s in range(1, SEGS):
        offsets = jnp.where(segment_ids == s, starts[s - 1], offsets)
    within = (global_index - offsets).astype(F32)
    low = (jnp.maximum(offsets, global_index - (WINDOW - 1)) - base)[:, None]
    half = HD // 2
    freqs = jnp.exp(-math.log(10000.0) * jnp.arange(half, dtype=F32) * (2.0 / HD))
    angles = freqs[:, None] * within[None, :]
    cos = jnp.cos(angles)
    sin = jnp.sin(angles)

    kv = project(x_all, kv_weights, kv_pieces, index, cos, sin, (True, False), 1.0)

    straight, crossed, current, state = [kv], [None], kv, None
    for step in range(4):
        following = move(current, LATER)
        chosen = jnp.where(h == 0, current, following)
        if step == 0:
            following, chosen = tie(following, chosen)
        elif step == 1:
            following, chosen, crossed[1], q_all = tie(following, chosen, crossed[1], q_all)
            queries = project(
                x_all,
                [q_all],
                q_pieces,
                index_of([-k for k in range(ROUNDS)], 0),
                cos,
                sin,
                (True, True),
                float(D // HQ) ** (-0.5),
            )
            state = attend(low, queries, [kv], [0], None)
        else:
            if step == 2:
                facing_out = move(turned, ACROSS)
                following, chosen, crossed[2], facing_out = tie(
                    following, chosen, crossed[2], facing_out
                )
            else:
                following, chosen, crossed[3], *state = tie(
                    following, chosen, crossed[3], *state
                )
            k = step - 1
            state = attend(low, queries, [straight[k], crossed[k]], [2 * k, 2 * k - 1], state)
        straight.append(following)
        crossed.append(move(chosen, ACROSS))
        current = following
    out_pair, straight[4] = tie(jnp.concatenate([turned, facing_out], axis=0), straight[4])
    out_all = lax.all_gather(out_pair, "seq", axis=0, axis_index_groups=COLUMNS)
    for k in range(3, 5):
        state = attend(low, queries, [straight[k], crossed[k]], [2 * k, 2 * k - 1], state)

    a_block = state[None]
    a_pair = jnp.concatenate([a_block, shift(a_block, SIDE)], axis=0)
    a_up, a_down = shift(a_pair, UP), shift(a_pair, DOWN)
    a_swaps = [shift(a_pair, SWAP)]
    a_up, a_down, a_swaps[0] = tie(a_up, a_down, a_swaps[0])
    a_far = [shift(a_up[:1], UP), shift(a_down[1:], DOWN)]
    a_swaps += [shift(a_up, SWAP), shift(a_down, SWAP)]
    a_far[0], a_far[1], a_swaps[1], a_swaps[2] = tie(*a_far, *a_swaps[1:])
    a_swaps += [shift(block, SWAP) for block in a_far]
    share, partial = output(
        [a_pair, a_up, a_down, *a_far, *a_swaps],
        out_all.reshape(2 * ROUNDS, features, 2 * HD),
        index,
    )
    everywhere = jnp.broadcast_to(partial, (lax.axis_size("mp"), rows))
    square_total = jnp.sum(lax.all_to_all(everywhere, "mp", 0, 0, tiled=True), axis=0)
    post_scale = lax.rsqrt(square_total / D + EPSILON)
    post = share * post_scale[None, :] * (1.0 + post_gain.astype(F32))[:, None]
    layer_output = (tokens.T.astype(F32) + post).astype(BF).T

    pages = page_table.shape[0]
    local_slot = page_table - seq_index * pages
    kv_pages = kv.reshape(pages, PAGE, 2 * HD)
    caches = []
    for slot in range(pages):
        chosen = kv_pages[0]
        for page in range(1, pages):
            chosen = jnp.where(local_slot[page] == slot, kv_pages[page], chosen)
        caches.append(chosen)
    caches = jnp.stack(caches)
    return (layer_output, caches[:, :, :HD], caches[:, :, HD:])


def solution(mesh):
    return jax.shard_map(
        shards,
        mesh=mesh,
        in_specs=(
            P("seq", "mp"),
            P("mp"),
            P("mp"),
            P("seq", "mp"),
            P("seq", "mp"),
            P("seq", "mp"),
            P("mp", "seq"),
            P("seq"),
            P("seq"),
        ),
        out_specs=(P("seq", "mp"), P("seq", None, "mp"), P("seq", None, "mp")),
        check_vma=False,
    )
```

```python
import functools
import math

import jax
import jax.numpy as jnp
from jax import lax
from jax.experimental import pallas as pl
from jax.experimental.pallas import tpu as pltpu
from jax.sharding import PartitionSpec as P

D = 4608
HQ = 32
HD = 128
WINDOW = 4096
PAGE = 128
SEGS = 4

EPSILON = 1e-06
SOFT_CAP = 50.0
LOG2E = 1.4426950408889634
EXTRA = 16
SEQ = 16
ROUNDS = 8

BF = jnp.bfloat16
F32 = jnp.float32

AHEAD = [(i, (i + 2) % SEQ) for i in range(SEQ)]
BEHIND = [((i + 2) % SEQ, i) for i in range(SEQ)]
LATER = [(i, i + 2) for i in range(SEQ - 2)]
ACROSS = [(i, i ^ 1) for i in range(SEQ)]
TURNS = (
    [(s * SEQ + m, (s + m) % SEQ * SEQ + m) for s in range(SEQ) for m in range(SEQ)],
    [(a * SEQ + m, a * SEQ + (a - m) % SEQ) for a in range(SEQ) for m in range(SEQ)],
)
SIDE = [(i, i ^ 2) for i in range(SEQ)]
UP = [(i, (i + 4) % SEQ) for i in range(SEQ)]
DOWN = [((i + 4) % SEQ, i) for i in range(SEQ)]
SWAP = [(i, i ^ 1) for i in range(SEQ)]
COLUMNS = [[2 * i + c for i in range(ROUNDS)] for c in range(2)]
PLACES = (((0, 0), (0, 1)), ((-1, 0), (-1, 1)), ((1, 0), (1, 1)), ((2, 0),), ((2, 1),))


def move(block, perm):
    return lax.ppermute(block, "seq", perm)


def shift(block, perm):
    return lax.ppermute(block, "mp", perm)


def tie(*values):
    return lax.optimization_barrier(values)


def project_kernel(pieces, rotated, factor, index_ref, cos_ref, sin_ref, x_hbm, *rest):
    w_refs = rest[:-6]
    out_ref, x_ref, w_ref, acc_ref, x_sem, w_sem = rest[-6:]
    chunks, depth, rows = x_ref.shape
    copies = []
    for k, (which, lead, slot, offset) in enumerate(pieces):
        place = index_ref[2 + ROUNDS + slot]
        source = w_refs[which] if lead is None else w_refs[which].at[lead]
        width = source.shape[1]
        for part in range(2):
            parity = index_ref[1] if part == 0 else 1 - index_ref[1]
            copies.append(
                pltpu.make_async_copy(
                    source.at[pl.ds(part * depth, depth)],
                    w_ref.at[2 * place + parity, :, pl.ds(offset, width)],
                    w_sem.at[2 * k + part],
                )
            )
    step = chunks // 4
    for k in range(4):
        copies.append(
            pltpu.make_async_copy(
                x_hbm.at[pl.ds(k * step, step)], x_ref.at[pl.ds(k * step, step)], x_sem.at[k]
            )
        )
    for copy in copies:
        copy.start()
    for copy in copies[:-4]:
        copy.wait()
    squares = jnp.zeros((1, rows), F32)
    for k in range(4):
        copies[k - 4].wait()
        here = slice(k * step, (k + 1) * step)
        side = x_ref[here, depth - EXTRA :, :].astype(F32)
        squares = squares + jnp.sum(jnp.sum(side, axis=0), axis=0, keepdims=True)
        product = lax.dot_general(
            w_ref[here].reshape(step * depth, 2 * HD),
            x_ref[here].reshape(step * depth, rows),
            (((0,), (0,)), ((), ())),
            preferred_element_type=F32,
        )
        if k == 0:
            acc_ref[...] = product
        else:
            acc_ref[...] += product
    scale = lax.rsqrt(squares * (1.0 / D) + EPSILON)
    half = HD // 2
    for head in range(2):
        start = head * HD
        if rotated[head]:
            first = acc_ref[start : start + half, :] * scale
            second = acc_ref[start + half : start + HD, :] * scale
            cos, sin = cos_ref[...], sin_ref[...]
            value = jnp.concatenate(
                [first * cos - second * sin, second * cos + first * sin], axis=0
            )
            if factor != 1.0:
                value = value * factor
        else:
            value = acc_ref[start : start + HD, :] * scale
        out_ref[:, start : start + HD] = jnp.transpose(value).astype(BF)


def project(x_all, weights, pieces, index, cos, sin, rotated, factor):
    chunks, depth, rows = x_all.shape
    vmem = pl.BlockSpec(memory_space=pltpu.VMEM)
    outside = pl.BlockSpec(memory_space=pl.ANY)
    return pl.pallas_call(
        functools.partial(project_kernel, pieces, rotated, factor),
        out_shape=jax.ShapeDtypeStruct((rows, 2 * HD), BF),
        in_specs=[pl.BlockSpec(memory_space=pltpu.SMEM), vmem, vmem]
        + [outside] * (1 + len(weights)),
        out_specs=vmem,
        scratch_shapes=[
            pltpu.VMEM((chunks, depth, rows), BF),
            pltpu.VMEM((chunks, depth, 2 * HD), BF),
            pltpu.VMEM((2 * HD, rows), F32),
            pltpu.SemaphoreType.DMA((4,)),
            pltpu.SemaphoreType.DMA((2 * len(pieces),)),
        ],
        compiler_params=pltpu.CompilerParams(vmem_limit_bytes=60 << 20),
        cost_estimate=pl.CostEstimate(
            flops=2 * rows * 2 * HD * D, bytes_accessed=8 << 20, transcendentals=0
        ),
    )(index, cos, sin, x_all, *weights)


def attend_kernel(distances, first, last, low_ref, q_ref, *rest):
    n = len(distances)
    kv_refs = rest[:n]
    rest = rest[n:]
    if not first:
        sum_in, den_in = rest[:2]
        rest = rest[2:]
    rows = q_ref.shape[0]
    tile = 256

    def part(index, carry):
        here = pl.ds(pl.multiple_of((index // 2) * tile, tile), tile)
        columns = pl.ds(pl.multiple_of(lax.rem(index, 2) * HD, HD), HD)
        q = q_ref[here, columns]
        low = low_ref[here, :]
        if first:
            total = jnp.zeros((tile, HD), F32)
            den = jnp.zeros((tile, HD), F32)
        else:
            total = sum_in[here, columns]
            den = den_in[here, columns]
        for kv_ref, distance in zip(kv_refs, distances):
            score = lax.dot_general(
                q, kv_ref[:, :HD], (((1,), (1,)), ((), ())), preferred_element_type=F32
            )
            weight = jnp.exp2(jnp.tanh(score * (1.0 / SOFT_CAP)) * (SOFT_CAP * LOG2E))
            place = lax.broadcasted_iota(jnp.int32, (tile, rows), 1)
            allowed = place >= low + distance * rows
            if distance == 0:
                own = lax.broadcasted_iota(jnp.int32, (tile, rows), 0) + (index // 2) * tile
                allowed = allowed & (place <= own)
            weight = jnp.where(allowed, weight, 0.0)
            for c in range(rows // HD):
                den = den + weight[:, c * HD : (c + 1) * HD]
            total = total + jnp.dot(
                weight.astype(BF), kv_ref[:, HD:], preferred_element_type=F32
            )
        if last:
            whole = jnp.sum(den, axis=1, keepdims=True)
            rest[0][here, columns] = (total / whole).astype(BF)
        else:
            rest[0][here, columns] = total
            rest[1][here, columns] = den
        return carry

    lax.fori_loop(0, 2 * (rows // tile), part, 0)


def attend(low, queries, kvs, distances, state):
    first = state is None
    last = 8 in distances
    rows = queries.shape[0]
    vmem = pl.BlockSpec(memory_space=pltpu.VMEM)
    n_in = 2 + len(kvs) + (0 if first else 2)
    part = jax.ShapeDtypeStruct((rows, 2 * HD), F32)
    elements = 2 * rows * rows * len(kvs)
    return pl.pallas_call(
        functools.partial(attend_kernel, tuple(distances), first, last),
        out_shape=jax.ShapeDtypeStruct((rows, 2 * HD), BF) if last else (part, part),
        in_specs=[vmem] * n_in,
        out_specs=vmem if last else (vmem, vmem),
        input_output_aliases={} if (first or last) else {n_in - 2: 0, n_in - 1: 1},
        compiler_params=pltpu.CompilerParams(vmem_limit_bytes=8 << 20),
        cost_estimate=pl.CostEstimate(
            flops=elements * 512, bytes_accessed=4 << 20, transcendentals=2 * elements
        ),
    )(low, queries, *kvs, *(() if first else state))


def output_kernel(index_ref, *rest):
    n = len(PLACES)
    sources, w_hbm = rest[: 2 * n], rest[2 * n]
    out_ref, square_ref, x_ref, w_ref, x_sem, w_sem = rest[2 * n + 1 :]
    load = pltpu.make_async_copy(w_hbm, w_ref, w_sem)
    load.start()
    copies = []
    for k, places in enumerate(PLACES):
        slot = sum(len(before) for before in PLACES[:k])
        copies.append(
            [
                pltpu.make_async_copy(
                    sources[part * n + k],
                    x_ref.at[part, pl.ds(slot, len(places))],
                    x_sem.at[part * n + k],
                )
                for part in range(2)
            ]
        )
    for both in copies:
        for copy in both:
            copy.start()
    load.wait()
    slot = 0
    for k, places in enumerate(PLACES):
        for copy in copies[k]:
            copy.wait()
        for _ in places:
            total = None
            place = index_ref[2 + slot]
            for part in range(2):
                parity = index_ref[0] if part == 0 else 1 - index_ref[0]
                holder = lax.rem(2 * place + parity + index_ref[2 + ROUNDS], 2 * ROUNDS)
                side = lax.rem(holder, 2)
                swapped = jnp.where(side == index_ref[1], 0, 1)
                product = lax.dot_general(
                    w_ref[holder - side + swapped],
                    x_ref[part, slot],
                    (((1,), (1,)), ((), ())),
                    preferred_element_type=F32,
                )
                total = product if total is None else total + product
            if slot == 0:
                out_ref[...] = total
            elif slot < ROUNDS - 1:
                out_ref[...] += total
            else:
                total = out_ref[...] + total
                out_ref[...] = total
                square_ref[...] = jnp.sum(total * total, axis=0, keepdims=True)
            slot += 1


def output(chunks, weights, index):
    _, rows, width = chunks[0].shape
    features = weights.shape[1]
    vmem = pl.BlockSpec(memory_space=pltpu.VMEM)
    outside = pl.BlockSpec(memory_space=pl.ANY)
    return pl.pallas_call(
        output_kernel,
        out_shape=(
            jax.ShapeDtypeStruct((features, rows), F32),
            jax.ShapeDtypeStruct((1, rows), F32),
        ),
        in_specs=[pl.BlockSpec(memory_space=pltpu.SMEM)] + [outside] * (len(chunks) + 1),
        out_specs=(vmem, vmem),
        scratch_shapes=[
            pltpu.VMEM((2, ROUNDS, rows, width), BF),
            pltpu.VMEM(weights.shape, BF),
            pltpu.SemaphoreType.DMA((2 * len(PLACES),)),
            pltpu.SemaphoreType.DMA,
        ],
        compiler_params=pltpu.CompilerParams(vmem_limit_bytes=60 << 20),
        cost_estimate=pl.CostEstimate(
            flops=2 * rows * features * 4096, bytes_accessed=8 << 20, transcendentals=0
        ),
    )(index, *chunks, weights)


def shards(tokens, pre_gain, post_gain, w_query, w_key, w_value, w_out, segment_ids, page_table):
    rows = tokens.shape[0]
    features = tokens.shape[1]
    seq_index = lax.axis_index("seq")
    z = seq_index // 2
    h = lax.rem(seq_index, 2)
    base = seq_index * rows

    x_own = tokens.T.astype(F32)
    gained = (x_own * (1.0 + pre_gain.astype(F32))[:, None]).astype(BF)
    squares = jnp.sum(x_own * x_own, axis=0, keepdims=True)
    upper = lax.reduce_precision(squares, 8, 7)
    lower = squares - upper
    side = jnp.concatenate(
        [upper.astype(BF), lower.astype(BF), jnp.zeros((EXTRA - 2, rows), BF)], axis=0
    )
    x_all = lax.all_gather(jnp.concatenate([gained, side], axis=0), "mp", axis=0)
    depth = features + EXTRA

    lane = jnp.arange(2 * HD, dtype=jnp.int32)
    marked = 2 * (SEGS - 1)
    limit = jnp.where(lane < marked, lax.rem(lane, SEGS - 1) + 1, 0)
    counts = jnp.sum((segment_ids[:, None] < limit[None, :]).astype(F32), axis=0)
    upper_digit = jnp.floor(counts * (1.0 / 16.0))
    digits = jnp.where(lane < SEGS - 1, upper_digit, counts - 16.0 * upper_digit).astype(BF)
    digits = jnp.pad(digits[None, :], ((2, EXTRA - 3), (0, 0)))
    kv_own = jnp.concatenate([jnp.concatenate([w_key, w_value], axis=1), digits], axis=0)
    start = jnp.concatenate([kv_own, move(kv_own, ACROSS)], axis=0)
    ring = {0: start, 1: move(start, AHEAD), -1: move(start, BEHIND)}
    turned = lax.ppermute(w_out.T, ("seq", "mp"), TURNS[0])
    ring[2] = move(ring[1], AHEAD)
    ring[-2] = move(ring[-1], BEHIND)
    ring[2], ring[-2], turned = tie(ring[2], ring[-2], turned)
    q_own = jnp.pad(w_query, ((0, EXTRA), (0, 0)))
    q_own, _ = tie(q_own, ring[1])
    q_pair = jnp.concatenate([q_own, move(q_own, ACROSS)], axis=0)
    ring[3] = move(ring[2], AHEAD)
    ring[-3] = move(ring[-2], BEHIND)
    ring[3], ring[-3], q_pair = tie(ring[3], ring[-3], q_pair)
    q_all = lax.all_gather(q_pair, "seq", axis=0, axis_index_groups=COLUMNS)
    turned = lax.ppermute(turned, ("seq", "mp"), TURNS[1])
    last = move(ring[3][:, :HD], AHEAD)
    opposite = move(ring[-3][:, HD:], BEHIND)
    last, opposite, turned = tie(last, opposite, turned)

    mp_index = lax.axis_index("mp")
    y = mp_index // 4
    over = lax.rem(mp_index // 2, 2)
    placed = [
        2 * lax.rem(y + dy + 4, 4) + jnp.where(dx == 0, over, 1 - over)
        for places in PLACES
        for dy, dx in places
    ]

    def index_of(steps, origin):
        places = [lax.rem(jnp.int32(origin - step + ROUNDS), ROUNDS) for step in steps]
        return jnp.stack([lax.rem(mp_index, 2), h, *placed, *places]).astype(jnp.int32)

    steps = [0, 1, -1, 2, -2, 3, -3, 4]
    index = index_of(steps, z)
    kv_weights = [ring[step] for step in steps[:7]] + [last, opposite]
    kv_pieces = tuple((k, None, k, 0) for k in range(ROUNDS)) + ((8, None, 7, HD),)
    q_pieces = tuple((0, k, k, 0) for k in range(ROUNDS))

    n_marks = 2 * (SEGS - 1)
    marks = jnp.zeros((n_marks,), F32)
    for block in kv_weights[:8]:
        for part in range(2):
            marks = marks + block[part * depth + features + 2, :n_marks].astype(F32)
    starts = (marks[: SEGS - 1] * 16.0 + marks[SEGS - 1 :]).astype(jnp.int32)
    global_index = base + jnp.arange(rows, dtype=jnp.int32)
    offsets = jnp.zeros((rows,), jnp.int32)
    for s in range(1, SEGS):
        offsets = jnp.where(segment_ids == s, starts[s - 1], offsets)
    within = (global_index - offsets).astype(F32)
    low = (jnp.maximum(offsets, global_index - (WINDOW - 1)) - base)[:, None]
    half = HD // 2
    freqs = jnp.exp(-math.log(10000.0) * jnp.arange(half, dtype=F32) * (2.0 / HD))
    angles = freqs[:, None] * within[None, :]
    cos = jnp.cos(angles)
    sin = jnp.sin(angles)

    kv = project(x_all, kv_weights, kv_pieces, index, cos, sin, (True, False), 1.0)

    straight, crossed, current, state = [kv], [None], kv, None
    for step in range(4):
        following = move(current, LATER)
        chosen = jnp.where(h == 0, current, following)
        if step == 0:
            following, chosen = tie(following, chosen)
        elif step == 1:
            following, chosen, crossed[1], q_all = tie(following, chosen, crossed[1], q_all)
            queries = project(
                x_all,
                [q_all],
                q_pieces,
                index_of([-k for k in range(ROUNDS)], 0),
                cos,
                sin,
                (True, True),
                float(D // HQ) ** (-0.5),
            )
            state = attend(low, queries, [kv], [0], None)
        else:
            if step == 2:
                facing_out = move(turned, ACROSS)
                following, chosen, crossed[2], facing_out, *state = tie(
                    following, chosen, crossed[2], facing_out, *state
                )
            else:
                following, chosen, crossed[3], *state = tie(
                    following, chosen, crossed[3], *state
                )
            k = step - 1
            state = attend(low, queries, [straight[k], crossed[k]], [2 * k, 2 * k - 1], state)
        straight.append(following)
        crossed.append(move(chosen, ACROSS))
        current = following
    out_pair, straight[4] = tie(jnp.concatenate([turned, facing_out], axis=0), straight[4])
    out_all = lax.all_gather(out_pair, "seq", axis=0, axis_index_groups=COLUMNS)
    for k in range(3, 5):
        state = attend(low, queries, [straight[k], crossed[k]], [2 * k, 2 * k - 1], state)

    a_block = state[None]
    a_pair = jnp.concatenate([a_block, shift(a_block, SIDE)], axis=0)
    a_up, a_down = shift(a_pair, UP), shift(a_pair, DOWN)
    a_swaps = [shift(a_pair, SWAP)]
    a_up, a_down, a_swaps[0] = tie(a_up, a_down, a_swaps[0])
    a_far = [shift(a_up[:1], UP), shift(a_down[1:], DOWN)]
    a_swaps += [shift(a_up, SWAP), shift(a_down, SWAP)]
    a_far[0], a_far[1], a_swaps[1], a_swaps[2] = tie(*a_far, *a_swaps[1:])
    a_swaps += [shift(block, SWAP) for block in a_far]
    share, partial = output(
        [a_pair, a_up, a_down, *a_far, *a_swaps],
        out_all.reshape(2 * ROUNDS, features, 2 * HD),
        jnp.concatenate([index[: 2 + ROUNDS], mp_index[None].astype(jnp.int32)]),
    )
    everywhere = jnp.broadcast_to(partial, (lax.axis_size("mp"), rows))
    square_total = jnp.sum(lax.all_to_all(everywhere, "mp", 0, 0, tiled=True), axis=0)
    post_scale = lax.rsqrt(square_total / D + EPSILON)
    post = share * post_scale[None, :] * (1.0 + post_gain.astype(F32))[:, None]
    layer_output = (tokens.T.astype(F32) + post).astype(BF).T

    pages = page_table.shape[0]
    local_slot = page_table - seq_index * pages
    kv_pages = kv.reshape(pages, PAGE, 2 * HD)
    caches = []
    for slot in range(pages):
        chosen = kv_pages[0]
        for page in range(1, pages):
            chosen = jnp.where(local_slot[page] == slot, kv_pages[page], chosen)
        caches.append(chosen)
    caches = jnp.stack(caches)
    return (layer_output, caches[:, :, :HD], caches[:, :, HD:])


def solution(mesh):
    return jax.shard_map(
        shards,
        mesh=mesh,
        in_specs=(
            P("seq", "mp"),
            P("mp"),
            P("mp"),
            P("seq", "mp"),
            P("seq", "mp"),
            P("seq", "mp"),
            P("mp", "seq"),
            P("seq"),
            P("seq"),
        ),
        out_specs=(P("seq", "mp"), P("seq", None, "mp"), P("seq", None, "mp")),
        check_vma=False,
    )
```

```python
import functools
import math

import jax
import jax.numpy as jnp
from jax import lax
from jax.experimental import pallas as pl
from jax.experimental.pallas import tpu as pltpu
from jax.sharding import PartitionSpec as P

D = 4608
HQ = 32
HD = 128
WINDOW = 4096
PAGE = 128
SEGS = 4

EPSILON = 1e-06
SOFT_CAP = 50.0
LOG2E = 1.4426950408889634
EXTRA = 16
SEQ = 16
ROUNDS = 8

BF = jnp.bfloat16
F32 = jnp.float32

AHEAD = [(i, (i + 2) % SEQ) for i in range(SEQ)]
BEHIND = [((i + 2) % SEQ, i) for i in range(SEQ)]
LATER = [(i, i + 2) for i in range(SEQ - 2)]
ACROSS = [(i, i ^ 1) for i in range(SEQ)]
TURNS = (
    [(s * SEQ + m, (s + m) % SEQ * SEQ + m) for s in range(SEQ) for m in range(SEQ)],
    [(a * SEQ + m, a * SEQ + (a - m) % SEQ) for a in range(SEQ) for m in range(SEQ)],
)
SIDE = [(i, i ^ 2) for i in range(SEQ)]
UP = [(i, (i + 4) % SEQ) for i in range(SEQ)]
DOWN = [((i + 4) % SEQ, i) for i in range(SEQ)]
SWAP = [(i, i ^ 1) for i in range(SEQ)]
COLUMNS = [[2 * i + c for i in range(ROUNDS)] for c in range(2)]
PLACES = (((0, 0), (0, 1)), ((-1, 0), (-1, 1)), ((1, 0), (1, 1)), ((2, 0),), ((2, 1),))


def move(block, perm):
    return lax.ppermute(block, "seq", perm)


def shift(block, perm):
    return lax.ppermute(block, "mp", perm)


def tie(*values):
    return lax.optimization_barrier(values)


def project_kernel(pieces, rotated, factor, index_ref, cos_ref, sin_ref, x_hbm, *rest):
    w_refs = rest[:-6]
    out_ref, x_ref, w_ref, acc_ref, x_sem, w_sem = rest[-6:]
    chunks, depth, rows = x_ref.shape
    copies = []
    for k, (which, lead, slot, offset) in enumerate(pieces):
        place = index_ref[2 + ROUNDS + slot]
        source = w_refs[which] if lead is None else w_refs[which].at[lead]
        width = source.shape[1]
        for part in range(2):
            parity = index_ref[1] if part == 0 else 1 - index_ref[1]
            copies.append(
                pltpu.make_async_copy(
                    source.at[pl.ds(part * depth, depth)],
                    w_ref.at[2 * place + parity, :, pl.ds(offset, width)],
                    w_sem.at[2 * k + part],
                )
            )
    step = chunks // 4
    for k in range(4):
        copies.append(
            pltpu.make_async_copy(
                x_hbm.at[pl.ds(k * step, step)], x_ref.at[pl.ds(k * step, step)], x_sem.at[k]
            )
        )
    for copy in copies:
        copy.start()
    for copy in copies[:-4]:
        copy.wait()
    squares = jnp.zeros((1, rows), F32)
    for k in range(4):
        copies[k - 4].wait()
        here = slice(k * step, (k + 1) * step)
        side = x_ref[here, depth - EXTRA :, :].astype(F32)
        squares = squares + jnp.sum(jnp.sum(side, axis=0), axis=0, keepdims=True)
        product = lax.dot_general(
            w_ref[here].reshape(step * depth, 2 * HD),
            x_ref[here].reshape(step * depth, rows),
            (((0,), (0,)), ((), ())),
            preferred_element_type=F32,
        )
        if k == 0:
            acc_ref[...] = product
        else:
            acc_ref[...] += product
    scale = lax.rsqrt(squares * (1.0 / D) + EPSILON)
    half = HD // 2
    for head in range(2):
        start = head * HD
        if rotated[head]:
            first = acc_ref[start : start + half, :] * scale
            second = acc_ref[start + half : start + HD, :] * scale
            cos, sin = cos_ref[...], sin_ref[...]
            value = jnp.concatenate(
                [first * cos - second * sin, second * cos + first * sin], axis=0
            )
            if factor != 1.0:
                value = value * factor
        else:
            value = acc_ref[start : start + HD, :] * scale
        out_ref[:, start : start + HD] = jnp.transpose(value).astype(BF)


def project(x_all, weights, pieces, index, cos, sin, rotated, factor):
    chunks, depth, rows = x_all.shape
    vmem = pl.BlockSpec(memory_space=pltpu.VMEM)
    outside = pl.BlockSpec(memory_space=pl.ANY)
    return pl.pallas_call(
        functools.partial(project_kernel, pieces, rotated, factor),
        out_shape=jax.ShapeDtypeStruct((rows, 2 * HD), BF),
        in_specs=[pl.BlockSpec(memory_space=pltpu.SMEM), vmem, vmem]
        + [outside] * (1 + len(weights)),
        out_specs=vmem,
        scratch_shapes=[
            pltpu.VMEM((chunks, depth, rows), BF),
            pltpu.VMEM((chunks, depth, 2 * HD), BF),
            pltpu.VMEM((2 * HD, rows), F32),
            pltpu.SemaphoreType.DMA((4,)),
            pltpu.SemaphoreType.DMA((2 * len(pieces),)),
        ],
        compiler_params=pltpu.CompilerParams(vmem_limit_bytes=60 << 20),
        cost_estimate=pl.CostEstimate(
            flops=2 * rows * 2 * HD * D, bytes_accessed=8 << 20, transcendentals=0
        ),
    )(index, cos, sin, x_all, *weights)


def attend_kernel(distances, first, last, low_ref, q_ref, *rest):
    n = len(distances)
    kv_refs = rest[:n]
    rest = rest[n:]
    if not first:
        sum_in, den_in = rest[:2]
        rest = rest[2:]
    rows = q_ref.shape[0]
    tile = 256

    def part(index, carry):
        here = pl.ds(pl.multiple_of((index // 2) * tile, tile), tile)
        columns = pl.ds(pl.multiple_of(lax.rem(index, 2) * HD, HD), HD)
        q = q_ref[here, columns]
        low = low_ref[here, :]
        if first:
            total = jnp.zeros((tile, HD), F32)
            den = jnp.zeros((tile, HD), F32)
        else:
            total = sum_in[here, columns]
            den = den_in[here, columns]
        for kv_ref, distance in zip(kv_refs, distances):
            score = lax.dot_general(
                q, kv_ref[:, :HD], (((1,), (1,)), ((), ())), preferred_element_type=F32
            )
            weight = jnp.exp2(jnp.tanh(score * (1.0 / SOFT_CAP)) * (SOFT_CAP * LOG2E))
            place = lax.broadcasted_iota(jnp.int32, (tile, rows), 1)
            allowed = place >= low + distance * rows
            if distance == 0:
                own = lax.broadcasted_iota(jnp.int32, (tile, rows), 0) + (index // 2) * tile
                allowed = allowed & (place <= own)
            weight = jnp.where(allowed, weight, 0.0)
            for c in range(rows // HD):
                den = den + weight[:, c * HD : (c + 1) * HD]
            total = total + jnp.dot(
                weight.astype(BF), kv_ref[:, HD:], preferred_element_type=F32
            )
        if last:
            whole = jnp.sum(den, axis=1, keepdims=True)
            rest[0][here, columns] = (total / whole).astype(BF)
        else:
            rest[0][here, columns] = total
            rest[1][here, columns] = den
        return carry

    lax.fori_loop(0, 2 * (rows // tile), part, 0)


def attend(low, queries, kvs, distances, state):
    first = state is None
    last = 8 in distances
    rows = queries.shape[0]
    vmem = pl.BlockSpec(memory_space=pltpu.VMEM)
    n_in = 2 + len(kvs) + (0 if first else 2)
    part = jax.ShapeDtypeStruct((rows, 2 * HD), F32)
    elements = 2 * rows * rows * len(kvs)
    return pl.pallas_call(
        functools.partial(attend_kernel, tuple(distances), first, last),
        out_shape=jax.ShapeDtypeStruct((rows, 2 * HD), BF) if last else (part, part),
        in_specs=[vmem] * n_in,
        out_specs=vmem if last else (vmem, vmem),
        input_output_aliases={} if (first or last) else {n_in - 2: 0, n_in - 1: 1},
        compiler_params=pltpu.CompilerParams(vmem_limit_bytes=8 << 20),
        cost_estimate=pl.CostEstimate(
            flops=elements * 512, bytes_accessed=4 << 20, transcendentals=2 * elements
        ),
    )(low, queries, *kvs, *(() if first else state))


def output_kernel(index_ref, *rest):
    n = len(PLACES)
    sources, w_hbm = rest[: 2 * n], rest[2 * n]
    out_ref, square_ref, x_ref, w_ref, x_sem, w_sem = rest[2 * n + 1 :]
    load = pltpu.make_async_copy(w_hbm, w_ref, w_sem)
    load.start()
    copies = []
    for k, places in enumerate(PLACES):
        slot = sum(len(before) for before in PLACES[:k])
        copies.append(
            [
                pltpu.make_async_copy(
                    sources[part * n + k],
                    x_ref.at[part, pl.ds(slot, len(places))],
                    x_sem.at[part * n + k],
                )
                for part in range(2)
            ]
        )
    for both in copies:
        for copy in both:
            copy.start()
    load.wait()
    slot = 0
    for k, places in enumerate(PLACES):
        for copy in copies[k]:
            copy.wait()
        for _ in places:
            total = None
            place = index_ref[2 + slot]
            for part in range(2):
                parity = index_ref[0] if part == 0 else 1 - index_ref[0]
                holder = lax.rem(2 * place + parity + index_ref[2 + ROUNDS], 2 * ROUNDS)
                side = lax.rem(holder, 2)
                swapped = jnp.where(side == index_ref[1], 0, 1)
                product = lax.dot_general(
                    w_ref[holder - side + swapped],
                    x_ref[part, slot],
                    (((1,), (1,)), ((), ())),
                    preferred_element_type=F32,
                )
                total = product if total is None else total + product
            if slot == 0:
                out_ref[...] = total
            elif slot < ROUNDS - 1:
                out_ref[...] += total
            else:
                total = out_ref[...] + total
                out_ref[...] = total
                squares = jnp.sum(total * total, axis=0, keepdims=True)
                square_ref[...] = jnp.broadcast_to(squares[None], square_ref.shape)
            slot += 1


def output(chunks, weights, index):
    _, rows, width = chunks[0].shape
    features = weights.shape[1]
    vmem = pl.BlockSpec(memory_space=pltpu.VMEM)
    outside = pl.BlockSpec(memory_space=pl.ANY)
    return pl.pallas_call(
        output_kernel,
        out_shape=(
            jax.ShapeDtypeStruct((features, rows), F32),
            jax.ShapeDtypeStruct((SEQ, 1, rows), F32),
        ),
        in_specs=[pl.BlockSpec(memory_space=pltpu.SMEM)] + [outside] * (len(chunks) + 1),
        out_specs=(vmem, vmem),
        scratch_shapes=[
            pltpu.VMEM((2, ROUNDS, rows, width), BF),
            pltpu.VMEM(weights.shape, BF),
            pltpu.SemaphoreType.DMA((2 * len(PLACES),)),
            pltpu.SemaphoreType.DMA,
        ],
        compiler_params=pltpu.CompilerParams(vmem_limit_bytes=60 << 20),
        cost_estimate=pl.CostEstimate(
            flops=2 * rows * features * 4096, bytes_accessed=8 << 20, transcendentals=0
        ),
    )(index, *chunks, weights)


def shards(tokens, pre_gain, post_gain, w_query, w_key, w_value, w_out, segment_ids, page_table):
    rows = tokens.shape[0]
    features = tokens.shape[1]
    seq_index = lax.axis_index("seq")
    z = seq_index // 2
    h = lax.rem(seq_index, 2)
    base = seq_index * rows

    x_own = tokens.T.astype(F32)
    gained = (x_own * (1.0 + pre_gain.astype(F32))[:, None]).astype(BF)
    squares = jnp.sum(x_own * x_own, axis=0, keepdims=True)
    upper = lax.reduce_precision(squares, 8, 7)
    lower = squares - upper
    side = jnp.concatenate(
        [upper.astype(BF), lower.astype(BF), jnp.zeros((EXTRA - 2, rows), BF)], axis=0
    )
    x_all = lax.all_gather(jnp.concatenate([gained, side], axis=0), "mp", axis=0)
    depth = features + EXTRA

    lane = jnp.arange(2 * HD, dtype=jnp.int32)
    marked = 2 * (SEGS - 1)
    limit = jnp.where(lane < marked, lax.rem(lane, SEGS - 1) + 1, 0)
    counts = jnp.sum((segment_ids[:, None] < limit[None, :]).astype(F32), axis=0)
    upper_digit = jnp.floor(counts * (1.0 / 16.0))
    digits = jnp.where(lane < SEGS - 1, upper_digit, counts - 16.0 * upper_digit).astype(BF)
    digits = jnp.pad(digits[None, :], ((2, EXTRA - 3), (0, 0)))
    kv_own = jnp.concatenate([jnp.concatenate([w_key, w_value], axis=1), digits], axis=0)
    start = jnp.concatenate([kv_own, move(kv_own, ACROSS)], axis=0)
    ring = {0: start, 1: move(start, AHEAD), -1: move(start, BEHIND)}
    turned = lax.ppermute(w_out.T, ("seq", "mp"), TURNS[0])
    ring[1], ring[-1], turned = tie(ring[1], ring[-1], turned)
    q_own = jnp.pad(w_query, ((0, EXTRA), (0, 0)))
    q_own, _ = tie(q_own, ring[1])
    q_near = move(q_own[:, :HD], ACROSS)
    ring[2] = move(ring[1], AHEAD)
    ring[-2] = move(ring[-1], BEHIND)
    ring[2], ring[-2], q_near = tie(ring[2], ring[-2], q_near)
    q_far, _ = tie(q_own[:, HD:], q_near)
    q_far = move(q_far, ACROSS)
    ring[3] = move(ring[2], AHEAD)
    ring[-3] = move(ring[-2], BEHIND)
    ring[3], ring[-3], q_far = tie(ring[3], ring[-3], q_far)
    q_pair = jnp.concatenate([q_own, jnp.concatenate([q_near, q_far], axis=1)], axis=0)
    q_all = lax.all_gather(q_pair, "seq", axis=0, axis_index_groups=COLUMNS)
    turned = lax.ppermute(turned, ("seq", "mp"), TURNS[1])
    last = move(ring[3][:, :HD], AHEAD)
    opposite = move(ring[-3][:, HD:], BEHIND)
    last, opposite, turned = tie(last, opposite, turned)

    mp_index = lax.axis_index("mp")
    y = mp_index // 4
    over = lax.rem(mp_index // 2, 2)
    placed = [
        2 * lax.rem(y + dy + 4, 4) + jnp.where(dx == 0, over, 1 - over)
        for places in PLACES
        for dy, dx in places
    ]

    def index_of(steps, origin):
        places = [lax.rem(jnp.int32(origin - step + ROUNDS), ROUNDS) for step in steps]
        return jnp.stack([lax.rem(mp_index, 2), h, *placed, *places]).astype(jnp.int32)

    steps = [0, 1, -1, 2, -2, 3, -3, 4]
    index = index_of(steps, z)
    kv_weights = [ring[step] for step in steps[:7]] + [last, opposite]
    kv_pieces = tuple((k, None, k, 0) for k in range(ROUNDS)) + ((8, None, 7, HD),)
    q_pieces = tuple((0, k, k, 0) for k in range(ROUNDS))

    n_marks = 2 * (SEGS - 1)
    marks = jnp.zeros((n_marks,), F32)
    for block in kv_weights[:8]:
        for part in range(2):
            marks = marks + block[part * depth + features + 2, :n_marks].astype(F32)
    starts = (marks[: SEGS - 1] * 16.0 + marks[SEGS - 1 :]).astype(jnp.int32)
    global_index = base + jnp.arange(rows, dtype=jnp.int32)
    offsets = jnp.zeros((rows,), jnp.int32)
    for s in range(1, SEGS):
        offsets = jnp.where(segment_ids == s, starts[s - 1], offsets)
    within = (global_index - offsets).astype(F32)
    low = (jnp.maximum(offsets, global_index - (WINDOW - 1)) - base)[:, None]
    half = HD // 2
    freqs = jnp.exp(-math.log(10000.0) * jnp.arange(half, dtype=F32) * (2.0 / HD))
    angles = freqs[:, None] * within[None, :]
    cos = jnp.cos(angles)
    sin = jnp.sin(angles)

    kv = project(x_all, kv_weights, kv_pieces, index, cos, sin, (True, False), 1.0)

    straight, crossed, current, state = [kv], [None], kv, None
    for step in range(4):
        following = move(current, LATER)
        chosen = jnp.where(h == 0, current, following)
        if step == 0:
            following, chosen = tie(following, chosen)
        elif step == 1:
            following, chosen, crossed[1], q_all = tie(following, chosen, crossed[1], q_all)
            queries = project(
                x_all,
                [q_all],
                q_pieces,
                index_of([-k for k in range(ROUNDS)], 0),
                cos,
                sin,
                (True, True),
                float(D // HQ) ** (-0.5),
            )
            state = attend(low, queries, [kv], [0], None)
        else:
            if step == 2:
                facing_out = move(turned, ACROSS)
                following, chosen, crossed[2], facing_out, *state = tie(
                    following, chosen, crossed[2], facing_out, *state
                )
            else:
                following, chosen, crossed[3], *state = tie(
                    following, chosen, crossed[3], *state
                )
            k = step - 1
            state = attend(low, queries, [straight[k], crossed[k]], [2 * k, 2 * k - 1], state)
        straight.append(following)
        crossed.append(move(chosen, ACROSS))
        current = following
    out_pair, straight[4] = tie(jnp.concatenate([turned, facing_out], axis=0), straight[4])
    out_all = lax.all_gather(out_pair, "seq", axis=0, axis_index_groups=COLUMNS)
    for k in range(3, 5):
        state = attend(low, queries, [straight[k], crossed[k]], [2 * k, 2 * k - 1], state)

    a_block = state[None]
    a_pair = jnp.concatenate([a_block, shift(a_block, SIDE)], axis=0)
    a_up, a_down = shift(a_pair, UP), shift(a_pair, DOWN)
    a_swaps = [shift(a_pair, SWAP)]
    a_up, a_down, a_swaps[0] = tie(a_up, a_down, a_swaps[0])
    a_far = [shift(a_up[:1], UP), shift(a_down[1:], DOWN)]
    a_swaps += [shift(a_up, SWAP), shift(a_down, SWAP)]
    a_far[0], a_far[1], a_swaps[1], a_swaps[2] = tie(*a_far, *a_swaps[1:])
    a_swaps += [shift(block, SWAP) for block in a_far]
    share, partial = output(
        [a_pair, a_up, a_down, *a_far, *a_swaps],
        out_all.reshape(2 * ROUNDS, features, 2 * HD),
        jnp.concatenate([index[: 2 + ROUNDS], mp_index[None].astype(jnp.int32)]),
    )
    square_total = jnp.sum(lax.all_to_all(partial, "mp", 0, 0, tiled=True), axis=(0, 1))
    post_scale = lax.rsqrt(square_total / D + EPSILON)
    post = share * post_scale[None, :] * (1.0 + post_gain.astype(F32))[:, None]
    layer_output = (tokens.T.astype(F32) + post).astype(BF).T

    pages = page_table.shape[0]
    local_slot = page_table - seq_index * pages
    kv_pages = kv.reshape(pages, PAGE, 2 * HD)
    caches = []
    for slot in range(pages):
        chosen = kv_pages[0]
        for page in range(1, pages):
            chosen = jnp.where(local_slot[page] == slot, kv_pages[page], chosen)
        caches.append(chosen)
    caches = jnp.stack(caches)
    return (layer_output, caches[:, :, :HD], caches[:, :, HD:])


def solution(mesh):
    return jax.shard_map(
        shards,
        mesh=mesh,
        in_specs=(
            P("seq", "mp"),
            P("mp"),
            P("mp"),
            P("seq", "mp"),
            P("seq", "mp"),
            P("seq", "mp"),
            P("mp", "seq"),
            P("seq"),
            P("seq"),
        ),
        out_specs=(P("seq", "mp"), P("seq", None, "mp"), P("seq", None, "mp")),
        check_vma=False,
    )
```

```python
import functools
import math

import jax
import jax.numpy as jnp
from jax import lax
from jax.experimental import pallas as pl
from jax.experimental.pallas import tpu as pltpu
from jax.sharding import PartitionSpec as P

D = 4608
HQ = 32
HD = 128
WINDOW = 4096
PAGE = 128
SEGS = 4

EPSILON = 1e-06
SOFT_CAP = 50.0
LOG2E = 1.4426950408889634
EXTRA = 16
SEQ = 16
ROUNDS = 8

BF = jnp.bfloat16
F32 = jnp.float32

AHEAD = [(i, (i + 2) % SEQ) for i in range(SEQ)]
BEHIND = [((i + 2) % SEQ, i) for i in range(SEQ)]
LATER = [(i, i + 2) for i in range(SEQ - 2)]
ACROSS = [(i, i ^ 1) for i in range(SEQ)]
TURNS = (
    [(s * SEQ + m, (s + m) % SEQ * SEQ + m) for s in range(SEQ) for m in range(SEQ)],
    [(a * SEQ + m, a * SEQ + (a - m) % SEQ) for a in range(SEQ) for m in range(SEQ)],
)
SIDE = [(i, i ^ 2) for i in range(SEQ)]
UP = [(i, (i + 4) % SEQ) for i in range(SEQ)]
DOWN = [((i + 4) % SEQ, i) for i in range(SEQ)]
SWAP = [(i, i ^ 1) for i in range(SEQ)]
COLUMNS = [[2 * i + c for i in range(ROUNDS)] for c in range(2)]
PLACES = (((0, 0), (0, 1)), ((-1, 0), (-1, 1)), ((1, 0), (1, 1)), ((2, 0),), ((2, 1),))


def move(block, perm):
    return lax.ppermute(block, "seq", perm)


def shift(block, perm):
    return lax.ppermute(block, "mp", perm)


def tie(*values):
    return lax.optimization_barrier(values)


def project_kernel(pieces, rotated, factor, index_ref, cos_ref, sin_ref, x_hbm, *rest):
    w_refs = rest[:-6]
    out_ref, x_ref, w_ref, acc_ref, x_sem, w_sem = rest[-6:]
    chunks, depth, rows = x_ref.shape
    copies = []
    for k, (which, lead, slot, offset) in enumerate(pieces):
        place = index_ref[2 + ROUNDS + slot]
        source = w_refs[which] if lead is None else w_refs[which].at[lead]
        length, width = source.shape[0] // 2, source.shape[1]
        for part in range(2):
            parity = index_ref[1] if part == 0 else 1 - index_ref[1]
            copies.append(
                pltpu.make_async_copy(
                    source.at[pl.ds(part * length, length)],
                    w_ref.at[2 * place + parity, pl.ds(0, length), pl.ds(offset, width)],
                    w_sem.at[2 * k + part],
                )
            )
    step = chunks // 4
    for k in range(4):
        copies.append(
            pltpu.make_async_copy(
                x_hbm.at[pl.ds(k * step, step)], x_ref.at[pl.ds(k * step, step)], x_sem.at[k]
            )
        )
    for copy in copies:
        copy.start()
    if length < depth:
        w_ref[:, length:, :] = jnp.zeros((chunks, depth - length, 2 * HD), BF)
    for copy in copies[:-4]:
        copy.wait()
    squares = jnp.zeros((1, rows), F32)
    for k in range(4):
        copies[k - 4].wait()
        here = slice(k * step, (k + 1) * step)
        side = x_ref[here, depth - EXTRA :, :].astype(F32)
        squares = squares + jnp.sum(jnp.sum(side, axis=0), axis=0, keepdims=True)
        product = lax.dot_general(
            w_ref[here].reshape(step * depth, 2 * HD),
            x_ref[here].reshape(step * depth, rows),
            (((0,), (0,)), ((), ())),
            preferred_element_type=F32,
        )
        if k == 0:
            acc_ref[...] = product
        else:
            acc_ref[...] += product
    scale = lax.rsqrt(squares * (1.0 / D) + EPSILON)
    half = HD // 2
    for head in range(2):
        start = head * HD
        if rotated[head]:
            first = acc_ref[start : start + half, :] * scale
            second = acc_ref[start + half : start + HD, :] * scale
            cos, sin = cos_ref[...], sin_ref[...]
            value = jnp.concatenate(
                [first * cos - second * sin, second * cos + first * sin], axis=0
            )
            if factor != 1.0:
                value = value * factor
        else:
            value = acc_ref[start : start + HD, :] * scale
        out_ref[:, start : start + HD] = jnp.transpose(value).astype(BF)


def project(x_all, weights, pieces, index, cos, sin, rotated, factor):
    chunks, depth, rows = x_all.shape
    vmem = pl.BlockSpec(memory_space=pltpu.VMEM)
    outside = pl.BlockSpec(memory_space=pl.ANY)
    return pl.pallas_call(
        functools.partial(project_kernel, pieces, rotated, factor),
        out_shape=jax.ShapeDtypeStruct((rows, 2 * HD), BF),
        in_specs=[pl.BlockSpec(memory_space=pltpu.SMEM), vmem, vmem]
        + [outside] * (1 + len(weights)),
        out_specs=vmem,
        scratch_shapes=[
            pltpu.VMEM((chunks, depth, rows), BF),
            pltpu.VMEM((chunks, depth, 2 * HD), BF),
            pltpu.VMEM((2 * HD, rows), F32),
            pltpu.SemaphoreType.DMA((4,)),
            pltpu.SemaphoreType.DMA((2 * len(pieces),)),
        ],
        compiler_params=pltpu.CompilerParams(vmem_limit_bytes=60 << 20),
        cost_estimate=pl.CostEstimate(
            flops=2 * rows * 2 * HD * D, bytes_accessed=8 << 20, transcendentals=0
        ),
    )(index, cos, sin, x_all, *weights)


def attend_kernel(distances, first, last, low_ref, q_ref, *rest):
    n = len(distances)
    kv_refs = rest[:n]
    rest = rest[n:]
    if not first:
        sum_in, den_in = rest[:2]
        rest = rest[2:]
    rows = q_ref.shape[0]
    tile = 256

    def part(index, carry):
        here = pl.ds(pl.multiple_of((index // 2) * tile, tile), tile)
        columns = pl.ds(pl.multiple_of(lax.rem(index, 2) * HD, HD), HD)
        q = q_ref[here, columns]
        low = low_ref[here, :]
        if first:
            total = jnp.zeros((tile, HD), F32)
            den = jnp.zeros((tile, HD), F32)
        else:
            total = sum_in[here, columns]
            den = den_in[here, columns]
        for kv_ref, distance in zip(kv_refs, distances):
            score = lax.dot_general(
                q, kv_ref[:, :HD], (((1,), (1,)), ((), ())), preferred_element_type=F32
            )
            weight = jnp.exp2(jnp.tanh(score * (1.0 / SOFT_CAP)) * (SOFT_CAP * LOG2E))
            place = lax.broadcasted_iota(jnp.int32, (tile, rows), 1)
            allowed = place >= low + distance * rows
            if distance == 0:
                own = lax.broadcasted_iota(jnp.int32, (tile, rows), 0) + (index // 2) * tile
                allowed = allowed & (place <= own)
            weight = jnp.where(allowed, weight, 0.0)
            for c in range(rows // HD):
                den = den + weight[:, c * HD : (c + 1) * HD]
            total = total + jnp.dot(
                weight.astype(BF), kv_ref[:, HD:], preferred_element_type=F32
            )
        if last:
            whole = jnp.sum(den, axis=1, keepdims=True)
            rest[0][here, columns] = (total / whole).astype(BF)
        else:
            rest[0][here, columns] = total
            rest[1][here, columns] = den
        return carry

    lax.fori_loop(0, 2 * (rows // tile), part, 0)


def attend(low, queries, kvs, distances, state):
    first = state is None
    last = 8 in distances
    rows = queries.shape[0]
    vmem = pl.BlockSpec(memory_space=pltpu.VMEM)
    n_in = 2 + len(kvs) + (0 if first else 2)
    part = jax.ShapeDtypeStruct((rows, 2 * HD), F32)
    elements = 2 * rows * rows * len(kvs)
    return pl.pallas_call(
        functools.partial(attend_kernel, tuple(distances), first, last),
        out_shape=jax.ShapeDtypeStruct((rows, 2 * HD), BF) if last else (part, part),
        in_specs=[vmem] * n_in,
        out_specs=vmem if last else (vmem, vmem),
        input_output_aliases={} if (first or last) else {n_in - 2: 0, n_in - 1: 1},
        compiler_params=pltpu.CompilerParams(vmem_limit_bytes=8 << 20),
        cost_estimate=pl.CostEstimate(
            flops=elements * 512, bytes_accessed=4 << 20, transcendentals=2 * elements
        ),
    )(low, queries, *kvs, *(() if first else state))


def output_kernel(index_ref, *rest):
    n = len(PLACES)
    sources, w_hbm = rest[: 2 * n], rest[2 * n]
    out_ref, square_ref, x_ref, w_ref, x_sem, w_sem = rest[2 * n + 1 :]
    load = pltpu.make_async_copy(w_hbm, w_ref, w_sem)
    load.start()
    copies = []
    for k, places in enumerate(PLACES):
        slot = sum(len(before) for before in PLACES[:k])
        copies.append(
            [
                pltpu.make_async_copy(
                    sources[part * n + k],
                    x_ref.at[part, pl.ds(slot, len(places))],
                    x_sem.at[part * n + k],
                )
                for part in range(2)
            ]
        )
    for both in copies:
        for copy in both:
            copy.start()
    load.wait()
    slot = 0
    for k, places in enumerate(PLACES):
        for copy in copies[k]:
            copy.wait()
        for _ in places:
            total = None
            place = index_ref[2 + slot]
            for part in range(2):
                parity = index_ref[0] if part == 0 else 1 - index_ref[0]
                holder = lax.rem(2 * place + parity + index_ref[2 + ROUNDS], 2 * ROUNDS)
                side = lax.rem(holder, 2)
                swapped = jnp.where(side == index_ref[1], 0, 1)
                product = lax.dot_general(
                    w_ref[holder - side + swapped],
                    x_ref[part, slot],
                    (((1,), (1,)), ((), ())),
                    preferred_element_type=F32,
                )
                total = product if total is None else total + product
            if slot == 0:
                out_ref[...] = total
            elif slot < ROUNDS - 1:
                out_ref[...] += total
            else:
                total = out_ref[...] + total
                out_ref[...] = total
                squares = jnp.sum(total * total, axis=0, keepdims=True)
                square_ref[...] = jnp.broadcast_to(squares[None], square_ref.shape)
            slot += 1


def output(chunks, weights, index):
    _, rows, width = chunks[0].shape
    features = weights.shape[1]
    vmem = pl.BlockSpec(memory_space=pltpu.VMEM)
    outside = pl.BlockSpec(memory_space=pl.ANY)
    return pl.pallas_call(
        output_kernel,
        out_shape=(
            jax.ShapeDtypeStruct((features, rows), F32),
            jax.ShapeDtypeStruct((SEQ, 1, rows), F32),
        ),
        in_specs=[pl.BlockSpec(memory_space=pltpu.SMEM)] + [outside] * (len(chunks) + 1),
        out_specs=(vmem, vmem),
        scratch_shapes=[
            pltpu.VMEM((2, ROUNDS, rows, width), BF),
            pltpu.VMEM(weights.shape, BF),
            pltpu.SemaphoreType.DMA((2 * len(PLACES),)),
            pltpu.SemaphoreType.DMA,
        ],
        compiler_params=pltpu.CompilerParams(vmem_limit_bytes=60 << 20),
        cost_estimate=pl.CostEstimate(
            flops=2 * rows * features * 4096, bytes_accessed=8 << 20, transcendentals=0
        ),
    )(index, *chunks, weights)


def shards(tokens, pre_gain, post_gain, w_query, w_key, w_value, w_out, segment_ids, page_table):
    rows = tokens.shape[0]
    features = tokens.shape[1]
    seq_index = lax.axis_index("seq")
    z = seq_index // 2
    h = lax.rem(seq_index, 2)
    base = seq_index * rows

    x_own = tokens.T.astype(F32)
    gained = (x_own * (1.0 + pre_gain.astype(F32))[:, None]).astype(BF)
    squares = jnp.sum(x_own * x_own, axis=0, keepdims=True)
    upper = lax.reduce_precision(squares, 8, 7)
    lower = squares - upper
    side = jnp.concatenate(
        [upper.astype(BF), lower.astype(BF), jnp.zeros((EXTRA - 2, rows), BF)], axis=0
    )
    x_all = lax.all_gather(jnp.concatenate([gained, side], axis=0), "mp", axis=0)
    depth = features + EXTRA

    lane = jnp.arange(2 * HD, dtype=jnp.int32)
    marked = 2 * (SEGS - 1)
    limit = jnp.where(lane < marked, lax.rem(lane, SEGS - 1) + 1, 0)
    counts = jnp.sum((segment_ids[:, None] < limit[None, :]).astype(F32), axis=0)
    upper_digit = jnp.floor(counts * (1.0 / 16.0))
    digits = jnp.where(lane < SEGS - 1, upper_digit, counts - 16.0 * upper_digit).astype(BF)
    digits = jnp.pad(digits[None, :], ((2, EXTRA - 3), (0, 0)))
    kv_own = jnp.concatenate([jnp.concatenate([w_key, w_value], axis=1), digits], axis=0)
    start = jnp.concatenate([kv_own, move(kv_own, ACROSS)], axis=0)
    ring = {0: start, 1: move(start, AHEAD), -1: move(start, BEHIND)}
    turned = lax.ppermute(w_out.T, ("seq", "mp"), TURNS[0])
    ring[2] = move(ring[1], AHEAD)
    ring[-2] = move(ring[-1], BEHIND)
    ring[2], ring[-2], turned = tie(ring[2], ring[-2], turned)
    q_own, _ = tie(w_query, ring[1])
    q_pair = jnp.concatenate([q_own, move(q_own, ACROSS)], axis=0)
    ring[3] = move(ring[2], AHEAD)
    ring[-3] = move(ring[-2], BEHIND)
    ring[3], ring[-3], q_pair = tie(ring[3], ring[-3], q_pair)
    q_all = lax.all_gather(q_pair, "seq", axis=0, axis_index_groups=COLUMNS)
    turned = lax.ppermute(turned, ("seq", "mp"), TURNS[1])
    last = move(ring[3][:, :HD], AHEAD)
    opposite = move(ring[-3][:, HD:], BEHIND)
    last, opposite, turned = tie(last, opposite, turned)

    mp_index = lax.axis_index("mp")
    y = mp_index // 4
    over = lax.rem(mp_index // 2, 2)
    placed = [
        2 * lax.rem(y + dy + 4, 4) + jnp.where(dx == 0, over, 1 - over)
        for places in PLACES
        for dy, dx in places
    ]

    def index_of(steps, origin):
        places = [lax.rem(jnp.int32(origin - step + ROUNDS), ROUNDS) for step in steps]
        return jnp.stack([lax.rem(mp_index, 2), h, *placed, *places]).astype(jnp.int32)

    steps = [0, 1, -1, 2, -2, 3, -3, 4]
    index = index_of(steps, z)
    kv_weights = [ring[step] for step in steps[:7]] + [last, opposite]
    kv_pieces = tuple((k, None, k, 0) for k in range(ROUNDS)) + ((8, None, 7, HD),)
    q_pieces = tuple((0, k, k, 0) for k in range(ROUNDS))

    n_marks = 2 * (SEGS - 1)
    marks = jnp.zeros((n_marks,), F32)
    for block in kv_weights[:8]:
        for part in range(2):
            marks = marks + block[part * depth + features + 2, :n_marks].astype(F32)
    starts = (marks[: SEGS - 1] * 16.0 + marks[SEGS - 1 :]).astype(jnp.int32)
    global_index = base + jnp.arange(rows, dtype=jnp.int32)
    offsets = jnp.zeros((rows,), jnp.int32)
    for s in range(1, SEGS):
        offsets = jnp.where(segment_ids == s, starts[s - 1], offsets)
    within = (global_index - offsets).astype(F32)
    low = (jnp.maximum(offsets, global_index - (WINDOW - 1)) - base)[:, None]
    half = HD // 2
    freqs = jnp.exp(-math.log(10000.0) * jnp.arange(half, dtype=F32) * (2.0 / HD))
    angles = freqs[:, None] * within[None, :]
    cos = jnp.cos(angles)
    sin = jnp.sin(angles)

    kv = project(x_all, kv_weights, kv_pieces, index, cos, sin, (True, False), 1.0)

    straight, crossed, current, state = [kv], [None], kv, None
    for step in range(4):
        following = move(current, LATER)
        chosen = jnp.where(h == 0, current, following)
        if step == 0:
            following, chosen = tie(following, chosen)
        elif step == 1:
            following, chosen, crossed[1], q_all = tie(following, chosen, crossed[1], q_all)
            queries = project(
                x_all,
                [q_all],
                q_pieces,
                index_of([-k for k in range(ROUNDS)], 0),
                cos,
                sin,
                (True, True),
                float(D // HQ) ** (-0.5),
            )
            state = attend(low, queries, [kv], [0], None)
        else:
            if step == 2:
                facing_out = move(turned, ACROSS)
                following, chosen, crossed[2], facing_out, *state = tie(
                    following, chosen, crossed[2], facing_out, *state
                )
            else:
                following, chosen, crossed[3], *state = tie(
                    following, chosen, crossed[3], *state
                )
            k = step - 1
            state = attend(low, queries, [straight[k], crossed[k]], [2 * k, 2 * k - 1], state)
        straight.append(following)
        crossed.append(move(chosen, ACROSS))
        current = following
    out_pair, straight[4] = tie(jnp.concatenate([turned, facing_out], axis=0), straight[4])
    out_all = lax.all_gather(out_pair, "seq", axis=0, axis_index_groups=COLUMNS)
    for k in range(3, 5):
        state = attend(low, queries, [straight[k], crossed[k]], [2 * k, 2 * k - 1], state)

    a_block = state[None]
    a_pair = jnp.concatenate([a_block, shift(a_block, SIDE)], axis=0)
    a_up, a_down = shift(a_pair, UP), shift(a_pair, DOWN)
    a_swaps = [shift(a_pair, SWAP)]
    a_up, a_down, a_swaps[0] = tie(a_up, a_down, a_swaps[0])
    a_far = [shift(a_up[:1], UP), shift(a_down[1:], DOWN)]
    a_swaps += [shift(a_up, SWAP), shift(a_down, SWAP)]
    a_far[0], a_far[1], a_swaps[1], a_swaps[2] = tie(*a_far, *a_swaps[1:])
    a_swaps += [shift(block, SWAP) for block in a_far]
    share, partial = output(
        [a_pair, a_up, a_down, *a_far, *a_swaps],
        out_all.reshape(2 * ROUNDS, features, 2 * HD),
        jnp.concatenate([index[: 2 + ROUNDS], mp_index[None].astype(jnp.int32)]),
    )
    square_total = jnp.sum(lax.all_to_all(partial, "mp", 0, 0, tiled=True), axis=(0, 1))
    post_scale = lax.rsqrt(square_total / D + EPSILON)
    post = share * post_scale[None, :] * (1.0 + post_gain.astype(F32))[:, None]
    layer_output = (tokens.T.astype(F32) + post).astype(BF).T

    pages = page_table.shape[0]
    local_slot = page_table - seq_index * pages
    kv_pages = kv.reshape(pages, PAGE, 2 * HD)
    caches = []
    for slot in range(pages):
        chosen = kv_pages[0]
        for page in range(1, pages):
            chosen = jnp.where(local_slot[page] == slot, kv_pages[page], chosen)
        caches.append(chosen)
    caches = jnp.stack(caches)
    return (layer_output, caches[:, :, :HD], caches[:, :, HD:])


def solution(mesh):
    return jax.shard_map(
        shards,
        mesh=mesh,
        in_specs=(
            P("seq", "mp"),
            P("mp"),
            P("mp"),
            P("seq", "mp"),
            P("seq", "mp"),
            P("seq", "mp"),
            P("mp", "seq"),
            P("seq"),
            P("seq"),
        ),
        out_specs=(P("seq", "mp"), P("seq", None, "mp"), P("seq", None, "mp")),
        check_vma=False,
    )
```

```python
import functools
import math

import jax
import jax.numpy as jnp
from jax import lax
from jax.experimental import pallas as pl
from jax.experimental.pallas import tpu as pltpu
from jax.sharding import PartitionSpec as P

D = 4608
HQ = 32
HD = 128
WINDOW = 4096
PAGE = 128
SEGS = 4

EPSILON = 1e-06
SOFT_CAP = 50.0
LOG2E = 1.4426950408889634
EXTRA = 16
SEQ = 16
ROUNDS = 8

BF = jnp.bfloat16
F32 = jnp.float32

AHEAD = [(i, (i + 2) % SEQ) for i in range(SEQ)]
BEHIND = [((i + 2) % SEQ, i) for i in range(SEQ)]
LATER = [(i, i + 2) for i in range(SEQ - 2)]
ACROSS = [(i, i ^ 1) for i in range(SEQ)]
TURNS = (
    [(s * SEQ + m, (s + m) % SEQ * SEQ + m) for s in range(SEQ) for m in range(SEQ)],
    [(a * SEQ + m, a * SEQ + (a - m) % SEQ) for a in range(SEQ) for m in range(SEQ)],
)
SIDE = [(i, i ^ 2) for i in range(SEQ)]
UP = [(i, (i + 4) % SEQ) for i in range(SEQ)]
DOWN = [((i + 4) % SEQ, i) for i in range(SEQ)]
SWAP = [(i, i ^ 1) for i in range(SEQ)]
COLUMNS = [[2 * i + c for i in range(ROUNDS)] for c in range(2)]
PLACES = (((0, 0), (0, 1)), ((-1, 0), (-1, 1)), ((1, 0), (1, 1)), ((2, 0),), ((2, 1),))


def move(block, perm):
    return lax.ppermute(block, "seq", perm)


def shift(block, perm):
    return lax.ppermute(block, "mp", perm)


def tie(*values):
    return lax.optimization_barrier(values)


def project_kernel(pieces, rotated, factor, index_ref, cos_ref, sin_ref, x_hbm, *rest):
    w_refs = rest[:-6]
    out_ref, x_ref, w_ref, acc_ref, x_sem, w_sem = rest[-6:]
    chunks, depth, rows = x_ref.shape
    copies = []
    for k, (which, lead, slot, offset) in enumerate(pieces):
        place = index_ref[2 + ROUNDS + slot]
        source = w_refs[which] if lead is None else w_refs[which].at[lead]
        length, width = source.shape[0] // 2, source.shape[1]
        for part in range(2):
            parity = index_ref[1] if part == 0 else 1 - index_ref[1]
            copies.append(
                pltpu.make_async_copy(
                    source.at[pl.ds(part * length, length)],
                    w_ref.at[2 * place + parity, pl.ds(0, length), pl.ds(offset, width)],
                    w_sem.at[2 * k + part],
                )
            )
    step = chunks // 4
    for k in range(4):
        copies.append(
            pltpu.make_async_copy(
                x_hbm.at[pl.ds(k * step, step)], x_ref.at[pl.ds(k * step, step)], x_sem.at[k]
            )
        )
    for copy in copies:
        copy.start()
    if length < depth:
        w_ref[:, length:, :] = jnp.zeros((chunks, depth - length, 2 * HD), BF)
    for copy in copies[:-4]:
        copy.wait()
    squares = jnp.zeros((1, rows), F32)
    for k in range(4):
        copies[k - 4].wait()
        here = slice(k * step, (k + 1) * step)
        side = x_ref[here, depth - EXTRA :, :].astype(F32)
        squares = squares + jnp.sum(jnp.sum(side, axis=0), axis=0, keepdims=True)
        product = lax.dot_general(
            w_ref[here].reshape(step * depth, 2 * HD),
            x_ref[here].reshape(step * depth, rows),
            (((0,), (0,)), ((), ())),
            preferred_element_type=F32,
        )
        if k == 0:
            acc_ref[...] = product
        else:
            acc_ref[...] += product
    scale = lax.rsqrt(squares * (1.0 / D) + EPSILON)
    half = HD // 2
    for head in range(2):
        start = head * HD
        if rotated[head]:
            first = acc_ref[start : start + half, :] * scale
            second = acc_ref[start + half : start + HD, :] * scale
            cos, sin = cos_ref[...], sin_ref[...]
            value = jnp.concatenate(
                [first * cos - second * sin, second * cos + first * sin], axis=0
            )
            if factor != 1.0:
                value = value * factor
        else:
            value = acc_ref[start : start + HD, :] * scale
        out_ref[:, start : start + HD] = jnp.transpose(value).astype(BF)


def project(x_all, weights, pieces, index, cos, sin, rotated, factor):
    chunks, depth, rows = x_all.shape
    vmem = pl.BlockSpec(memory_space=pltpu.VMEM)
    outside = pl.BlockSpec(memory_space=pl.ANY)
    return pl.pallas_call(
        functools.partial(project_kernel, pieces, rotated, factor),
        out_shape=jax.ShapeDtypeStruct((rows, 2 * HD), BF),
        in_specs=[pl.BlockSpec(memory_space=pltpu.SMEM), vmem, vmem]
        + [outside] * (1 + len(weights)),
        out_specs=vmem,
        scratch_shapes=[
            pltpu.VMEM((chunks, depth, rows), BF),
            pltpu.VMEM((chunks, depth, 2 * HD), BF),
            pltpu.VMEM((2 * HD, rows), F32),
            pltpu.SemaphoreType.DMA((4,)),
            pltpu.SemaphoreType.DMA((2 * len(pieces),)),
        ],
        compiler_params=pltpu.CompilerParams(vmem_limit_bytes=60 << 20),
        cost_estimate=pl.CostEstimate(
            flops=2 * rows * 2 * HD * D, bytes_accessed=8 << 20, transcendentals=0
        ),
    )(index, cos, sin, x_all, *weights)


def attend_kernel(distances, first, last, low_ref, q_ref, *rest):
    n = len(distances)
    kv_refs = rest[:n]
    rest = rest[n:]
    if not first:
        sum_in, den_in = rest[:2]
        rest = rest[2:]
    rows = q_ref.shape[0]
    tile = 256

    def part(index, carry):
        here = pl.ds(pl.multiple_of((index // 2) * tile, tile), tile)
        columns = pl.ds(pl.multiple_of(lax.rem(index, 2) * HD, HD), HD)
        q = q_ref[here, columns]
        low = low_ref[here, :]
        if first:
            total = jnp.zeros((tile, HD), F32)
            den = jnp.zeros((tile, HD), F32)
        else:
            total = sum_in[here, columns]
            den = den_in[here, columns]
        for kv_ref, distance in zip(kv_refs, distances):
            score = lax.dot_general(
                q, kv_ref[:, :HD], (((1,), (1,)), ((), ())), preferred_element_type=F32
            )
            weight = jnp.exp2(jnp.tanh(score * (1.0 / SOFT_CAP)) * (SOFT_CAP * LOG2E))
            place = lax.broadcasted_iota(jnp.int32, (tile, rows), 1)
            allowed = place >= low + distance * rows
            if distance == 0:
                own = lax.broadcasted_iota(jnp.int32, (tile, rows), 0) + (index // 2) * tile
                allowed = allowed & (place <= own)
            weight = jnp.where(allowed, weight, 0.0)
            for c in range(rows // HD):
                den = den + weight[:, c * HD : (c + 1) * HD]
            total = total + jnp.dot(
                weight.astype(BF), kv_ref[:, HD:], preferred_element_type=F32
            )
        if last:
            whole = jnp.sum(den, axis=1, keepdims=True)
            rest[0][here, columns] = (total / whole).astype(BF)
        else:
            rest[0][here, columns] = total
            rest[1][here, columns] = den
        return carry

    lax.fori_loop(0, 2 * (rows // tile), part, 0)


def attend(low, queries, kvs, distances, state):
    first = state is None
    last = 8 in distances
    rows = queries.shape[0]
    vmem = pl.BlockSpec(memory_space=pltpu.VMEM)
    n_in = 2 + len(kvs) + (0 if first else 2)
    part = jax.ShapeDtypeStruct((rows, 2 * HD), F32)
    elements = 2 * rows * rows * len(kvs)
    return pl.pallas_call(
        functools.partial(attend_kernel, tuple(distances), first, last),
        out_shape=jax.ShapeDtypeStruct((rows, 2 * HD), BF) if last else (part, part),
        in_specs=[vmem] * n_in,
        out_specs=vmem if last else (vmem, vmem),
        input_output_aliases={} if (first or last) else {n_in - 2: 0, n_in - 1: 1},
        compiler_params=pltpu.CompilerParams(vmem_limit_bytes=8 << 20),
        cost_estimate=pl.CostEstimate(
            flops=elements * 512, bytes_accessed=4 << 20, transcendentals=2 * elements
        ),
    )(low, queries, *kvs, *(() if first else state))


def output_kernel(index_ref, *rest):
    n = len(PLACES)
    sources, w_hbm = rest[: 2 * n], rest[2 * n]
    out_ref, square_ref, x_ref, w_ref, x_sem, w_sem = rest[2 * n + 1 :]
    load = pltpu.make_async_copy(w_hbm, w_ref, w_sem)
    load.start()
    copies = []
    for k, places in enumerate(PLACES):
        slot = sum(len(before) for before in PLACES[:k])
        copies.append(
            [
                pltpu.make_async_copy(
                    sources[part * n + k],
                    x_ref.at[part, pl.ds(slot, len(places))],
                    x_sem.at[part * n + k],
                )
                for part in range(2)
            ]
        )
    for both in copies:
        for copy in both:
            copy.start()
    load.wait()
    slot = 0
    for k, places in enumerate(PLACES):
        for copy in copies[k]:
            copy.wait()
        for _ in places:
            total = None
            place = index_ref[2 + slot]
            for part in range(2):
                parity = index_ref[0] if part == 0 else 1 - index_ref[0]
                holder = lax.rem(2 * place + parity + index_ref[2 + ROUNDS], 2 * ROUNDS)
                side = lax.rem(holder, 2)
                swapped = jnp.where(side == index_ref[1], 0, 1)
                product = lax.dot_general(
                    w_ref[holder - side + swapped],
                    x_ref[part, slot],
                    (((1,), (1,)), ((), ())),
                    preferred_element_type=F32,
                )
                total = product if total is None else total + product
            if slot == 0:
                out_ref[...] = total
            elif slot < ROUNDS - 1:
                out_ref[...] += total
            else:
                total = out_ref[...] + total
                out_ref[...] = total
                squares = jnp.sum(total * total, axis=0, keepdims=True)
                square_ref[...] = jnp.broadcast_to(squares[None], square_ref.shape)
            slot += 1


def output(chunks, weights, index):
    _, rows, width = chunks[0].shape
    features = weights.shape[1]
    vmem = pl.BlockSpec(memory_space=pltpu.VMEM)
    outside = pl.BlockSpec(memory_space=pl.ANY)
    return pl.pallas_call(
        output_kernel,
        out_shape=(
            jax.ShapeDtypeStruct((features, rows), F32),
            jax.ShapeDtypeStruct((SEQ, 1, rows), F32),
        ),
        in_specs=[pl.BlockSpec(memory_space=pltpu.SMEM)] + [outside] * (len(chunks) + 1),
        out_specs=(vmem, vmem),
        scratch_shapes=[
            pltpu.VMEM((2, ROUNDS, rows, width), BF),
            pltpu.VMEM(weights.shape, BF),
            pltpu.SemaphoreType.DMA((2 * len(PLACES),)),
            pltpu.SemaphoreType.DMA,
        ],
        compiler_params=pltpu.CompilerParams(vmem_limit_bytes=60 << 20),
        cost_estimate=pl.CostEstimate(
            flops=2 * rows * features * 4096, bytes_accessed=8 << 20, transcendentals=0
        ),
    )(index, *chunks, weights)


def shards(tokens, pre_gain, post_gain, w_query, w_key, w_value, w_out, segment_ids, page_table):
    rows = tokens.shape[0]
    features = tokens.shape[1]
    seq_index = lax.axis_index("seq")
    z = seq_index // 2
    h = lax.rem(seq_index, 2)
    base = seq_index * rows

    x_own = tokens.T.astype(F32)
    gained = (x_own * (1.0 + pre_gain.astype(F32))[:, None]).astype(BF)
    squares = jnp.sum(x_own * x_own, axis=0, keepdims=True)
    upper = lax.reduce_precision(squares, 8, 7)
    lower = squares - upper
    side = jnp.concatenate(
        [upper.astype(BF), lower.astype(BF), jnp.zeros((EXTRA - 2, rows), BF)], axis=0
    )
    x_all = lax.all_gather(jnp.concatenate([gained, side], axis=0), "mp", axis=0)
    depth = features + EXTRA

    lane = jnp.arange(2 * HD, dtype=jnp.int32)
    marked = 2 * (SEGS - 1)
    limit = jnp.where(lane < marked, lax.rem(lane, SEGS - 1) + 1, 0)
    counts = jnp.sum((segment_ids[:, None] < limit[None, :]).astype(F32), axis=0)
    upper_digit = jnp.floor(counts * (1.0 / 16.0))
    digits = jnp.where(lane < SEGS - 1, upper_digit, counts - 16.0 * upper_digit).astype(BF)
    digits = jnp.pad(digits[None, :], ((2, EXTRA - 3), (0, 0)))
    kv_own = jnp.concatenate([jnp.concatenate([w_key, w_value], axis=1), digits], axis=0)
    start = jnp.concatenate([kv_own, move(kv_own, ACROSS)], axis=0)
    ring = {0: start, 1: move(start, AHEAD), -1: move(start, BEHIND)}
    turned = lax.ppermute(w_out.T, ("seq", "mp"), TURNS[0])
    ring[2] = move(ring[1], AHEAD)
    ring[-2] = move(ring[-1], BEHIND)
    ring[2], ring[-2], turned = tie(ring[2], ring[-2], turned)
    q_own, _ = tie(w_query, ring[1])
    q_pair = jnp.concatenate([q_own, move(q_own, ACROSS)], axis=0)
    ring[3] = move(ring[2], AHEAD)
    ring[-3] = move(ring[-2], BEHIND)
    ring[3], ring[-3], q_pair = tie(ring[3], ring[-3], q_pair)
    q_all = lax.all_gather(q_pair, "seq", axis=0, axis_index_groups=COLUMNS)
    turned = lax.ppermute(turned, ("seq", "mp"), TURNS[1])
    last = move(ring[3][:, :HD], AHEAD)
    opposite = move(ring[-3][:, HD:], BEHIND)
    last, opposite, turned = tie(last, opposite, turned)

    mp_index = lax.axis_index("mp")
    y = mp_index // 4
    over = lax.rem(mp_index // 2, 2)
    placed = [
        2 * lax.rem(y + dy + 4, 4) + jnp.where(dx == 0, over, 1 - over)
        for places in PLACES
        for dy, dx in places
    ]

    def index_of(steps, origin):
        places = [lax.rem(jnp.int32(origin - step + ROUNDS), ROUNDS) for step in steps]
        return jnp.stack([lax.rem(mp_index, 2), h, *placed, *places]).astype(jnp.int32)

    steps = [0, 1, -1, 2, -2, 3, -3, 4]
    index = index_of(steps, z)
    kv_weights = [ring[step] for step in steps[:7]] + [last, opposite]
    kv_pieces = tuple((k, None, k, 0) for k in range(ROUNDS)) + ((8, None, 7, HD),)
    q_pieces = tuple((0, k, k, 0) for k in range(ROUNDS))

    n_marks = 2 * (SEGS - 1)
    marks = jnp.zeros((n_marks,), F32)
    for block in kv_weights[:8]:
        for part in range(2):
            marks = marks + block[part * depth + features + 2, :n_marks].astype(F32)
    starts = (marks[: SEGS - 1] * 16.0 + marks[SEGS - 1 :]).astype(jnp.int32)
    global_index = base + jnp.arange(rows, dtype=jnp.int32)
    offsets = jnp.zeros((rows,), jnp.int32)
    for s in range(1, SEGS):
        offsets = jnp.where(segment_ids == s, starts[s - 1], offsets)
    low = (jnp.maximum(offsets, global_index - (WINDOW - 1)) - base)[:, None]
    half = HD // 2
    freqs = jnp.exp(-math.log(10000.0) * jnp.arange(half, dtype=F32) * (2.0 / HD))
    angles = freqs[:, None] * global_index.astype(F32)[None, :]
    cos_index, sin_index = tie(jnp.cos(angles), jnp.sin(angles), ring[2])[:2]
    turns = freqs[:, None] * starts.astype(F32)[None, :]
    cos_starts, sin_starts = jnp.cos(turns), jnp.sin(turns)
    cos_start, sin_start = jnp.ones_like(angles), jnp.zeros_like(angles)
    for s in range(1, SEGS):
        here = (segment_ids == s)[None, :]
        cos_start = jnp.where(here, cos_starts[:, s - 1 : s], cos_start)
        sin_start = jnp.where(here, sin_starts[:, s - 1 : s], sin_start)
    cos = cos_index * cos_start + sin_index * sin_start
    sin = sin_index * cos_start - cos_index * sin_start

    kv = project(x_all, kv_weights, kv_pieces, index, cos, sin, (True, False), 1.0)

    straight, crossed, current, state = [kv], [None], kv, None
    for step in range(4):
        following = move(current, LATER)
        chosen = jnp.where(h == 0, current, following)
        if step == 0:
            following, chosen = tie(following, chosen)
        elif step == 1:
            following, chosen, crossed[1], q_all = tie(following, chosen, crossed[1], q_all)
            queries = project(
                x_all,
                [q_all],
                q_pieces,
                index_of([-k for k in range(ROUNDS)], 0),
                cos,
                sin,
                (True, True),
                float(D // HQ) ** (-0.5),
            )
            state = attend(low, queries, [kv], [0], None)
        else:
            if step == 2:
                facing_out = move(turned, ACROSS)
                following, chosen, crossed[2], facing_out, *state = tie(
                    following, chosen, crossed[2], facing_out, *state
                )
            else:
                following, chosen, crossed[3], *state = tie(
                    following, chosen, crossed[3], *state
                )
            k = step - 1
            state = attend(low, queries, [straight[k], crossed[k]], [2 * k, 2 * k - 1], state)
        straight.append(following)
        crossed.append(move(chosen, ACROSS))
        current = following
    out_pair, straight[4] = tie(jnp.concatenate([turned, facing_out], axis=0), straight[4])
    out_all = lax.all_gather(out_pair, "seq", axis=0, axis_index_groups=COLUMNS)
    for k in range(3, 5):
        state = attend(low, queries, [straight[k], crossed[k]], [2 * k, 2 * k - 1], state)

    a_block = state[None]
    a_pair = jnp.concatenate([a_block, shift(a_block, SIDE)], axis=0)
    a_up, a_down = shift(a_pair, UP), shift(a_pair, DOWN)
    a_swaps = [shift(a_pair, SWAP)]
    a_up, a_down, a_swaps[0] = tie(a_up, a_down, a_swaps[0])
    a_far = [shift(a_up[:1], UP), shift(a_down[1:], DOWN)]
    a_swaps += [shift(a_up, SWAP), shift(a_down, SWAP)]
    a_far[0], a_far[1], a_swaps[1], a_swaps[2] = tie(*a_far, *a_swaps[1:])
    a_swaps += [shift(block, SWAP) for block in a_far]
    share, partial = output(
        [a_pair, a_up, a_down, *a_far, *a_swaps],
        out_all.reshape(2 * ROUNDS, features, 2 * HD),
        jnp.concatenate([index[: 2 + ROUNDS], mp_index[None].astype(jnp.int32)]),
    )
    square_total = jnp.sum(lax.all_to_all(partial, "mp", 0, 0, tiled=True), axis=(0, 1))
    post_scale = lax.rsqrt(square_total / D + EPSILON)
    post = share * post_scale[None, :] * (1.0 + post_gain.astype(F32))[:, None]
    layer_output = (tokens.T.astype(F32) + post).astype(BF).T

    pages = page_table.shape[0]
    local_slot = page_table - seq_index * pages
    kv_pages = kv.reshape(pages, PAGE, 2 * HD)
    caches = []
    for slot in range(pages):
        chosen = kv_pages[0]
        for page in range(1, pages):
            chosen = jnp.where(local_slot[page] == slot, kv_pages[page], chosen)
        caches.append(chosen)
    caches = jnp.stack(caches)
    return (layer_output, caches[:, :, :HD], caches[:, :, HD:])


def solution(mesh):
    return jax.shard_map(
        shards,
        mesh=mesh,
        in_specs=(
            P("seq", "mp"),
            P("mp"),
            P("mp"),
            P("seq", "mp"),
            P("seq", "mp"),
            P("seq", "mp"),
            P("mp", "seq"),
            P("seq"),
            P("seq"),
        ),
        out_specs=(P("seq", "mp"), P("seq", None, "mp"), P("seq", None, "mp")),
        check_vma=False,
    )
```
